32 devices in a mesh: groups: 2 (over x), seq: 16 (over z, y, core).
Axes of the slice: x: 2, y: 2, z: 4, core: 2. Of those that a mesh axis runs over, the one named last changes fastest.
Arguments:
- values: bfloat16 [16384, 2048], P(('groups', 'seq')), parts along dimension 0, may hold values from -6 to 6
- b_proj: bfloat16 [16384, 64], P(('groups', 'seq')), parts along dimension 0, may hold values from -0.03125 to 0.03125
- c_proj: bfloat16 [16384, 64], P(('groups', 'seq')), parts along dimension 0, may hold values from -6 to 6
- step_sizes: float32 [16384, 32], P(('groups', 'seq')), parts along dimension 0, may hold values from 0.5 to 2
- decay_rates: float32 [32], replicated, may hold values from 3.0517578e-05 to 0.05
- skip_gain: float32 [32], replicated, may hold values from 0.5 to 1.5
- teacher: bfloat16 [16384, 2048], P(('groups', 'seq')), parts along dimension 0, may hold values from -6 to 6
- doc_lengths: int32 [32], P('groups'), parts along dimension 0, may hold values from 1 to 2048, 8192 in all
Outputs:
- loss: float32 [2], P('groups'), parts along dimension 0
- grad_values: float32 [16384, 2048], P(('groups', 'seq')), parts along dimension 0
- grad_b: float32 [16384, 64], P(('groups', 'seq')), parts along dimension 0
- grad_c: float32 [16384, 64], P(('groups', 'seq')), parts along dimension 0
The draws below stay inside these ranges and needn't reach their ends.
There are 2 independent parts, one for each index of `groups`. The reference program is written for one: setup_inputs(seed, part) draws one part's arguments, and reference() takes and returns one part's arrays. A program takes and returns all parts, laid end to end along the dimension named above; an argument that names none is the same for every part. Nothing has to cross between parts.
Inputs may be any that keep to these rules, and one draw needn't show every extreme that they name: `doc_lengths`: the documents' lengths sum to 8192, the longest is exactly 2048.
All inputs are finite; a program needn't handle non-finite values.
Results may differ from the reference program's by a relative error of at most 0.004.
Values sent between devices are 32-bit elements; how exact they have to be, the bound alone decides.
No kernel may reach another device: no remote copies, remote signals or barrier semaphores. Data moves between devices by JAX's collectives and lax.ppermute only.
A program may use at most 128 MiB of HBM per device.

```python
import math
import jax
import jax.numpy as jnp
import numpy as np
from jax import lax

HEADS = 32
HEAD_DIM = 64
STATE = 64
TOK_DEV = 512
DOCS = 16
SEQLEN = 8192
MOST = 2048


def levels(own_key, extent, cuts, smallest, top_value):
    def one(axis_at, parts):
        steps = jax.random.uniform(jax.random.fold_in(jax.random.fold_in(own_key, 6), axis_at), (parts,), jnp.float32, smallest / len(cuts), top_value / len(cuts))
        return jnp.repeat(jnp.exp(steps), extent[axis_at] // parts).reshape((-1,) + (1,) * (len(extent) - axis_at - 1))

    level = one(*cuts[0])
    for cut in cuts[1:]:
        level = level * one(*cut)
    return level


def profile(amount, total, limit, slope):
    loads = [(1 << 20) // math.isqrt(rank ** slope) + 1 for rank in range(2, amount + 1)]
    rest, holding = total - limit - (amount - 1), [1] * (amount - 1)
    while rest > 0:
        movable = [i for i in range(amount - 1) if holding[i] < limit]
        whole, remaining = sum([loads[i] for i in movable]), rest
        for i in movable:
            addition = min(limit - holding[i], max(1, remaining * loads[i] // whole), rest)
            holding[i] = holding[i] + addition
            rest = rest - addition
    return np.array([limit] + holding)


def uneven(own_key, amount, total, most, slope):
    if amount == 2:
        one = jax.random.randint(own_key, (), max(1, total - most), min(most, total - 1) + 1)
        return jnp.stack([one, total - one])
    sizes = jnp.asarray(profile(amount, total, most, slope), jnp.int32)
    pairs = (amount - 1) // 2
    donor, sink = sizes[1:1 + 2 * pairs:2], sizes[2:2 + 2 * pairs:2]
    slack = jnp.minimum(donor - 1, most - sink)
    moved = jax.random.randint(jax.random.fold_in(own_key, 1), (pairs,), 0, 1 << 20) % (slack + 1)
    sizes = sizes.at[1:1 + 2 * pairs:2].set(donor - moved).at[2:2 + 2 * pairs:2].set(sink + moved)
    return sizes[jax.random.permutation(jax.random.fold_in(own_key, 2), amount)]


def centred(rng, extent, spread, bound, cuts=(), kind=jnp.bfloat16):
    result = jax.random.normal(rng, extent, jnp.float32) * spread
    if len(cuts) > 0:
        result = levels(rng, extent, cuts, -0.22, 0.18) * result
    return jnp.clip(result, min=-bound, max=bound).astype(kind)


def setup_inputs(seed: int = 0, part: int = 0) -> dict:
    splits = jax.random.split(jax.random.key(seed), 9)
    part_keys = jax.random.split(jax.random.fold_in(splits[8], part), 9)
    values = centred(part_keys[0], (SEQLEN, HEADS * HEAD_DIM), 1.0, 6.0, ((0, 16),))
    b_proj = centred(part_keys[1], (SEQLEN, STATE), (STATE * 512) ** -0.5, 0.03125, ((0, 16),))
    c_proj = centred(part_keys[2], (SEQLEN, STATE), 1.0, 6.0, ((0, 16),))
    step_sizes = jnp.clip(jnp.exp(math.log(2.0) - 1.3862944 * jax.random.uniform(part_keys[3], (SEQLEN, HEADS), jnp.float32) ** levels(part_keys[3], (SEQLEN, HEADS), ((0, 16),), -0.2, 0.2)), 0.5, 2.0)
    decay_rates = jnp.clip(jnp.exp(jax.random.uniform(splits[4], (HEADS,), jnp.float32, math.log(3.0517578125e-05), math.log(0.05))), 3.0517578125e-05, 0.05)
    skip_gain = jnp.clip(jax.random.uniform(splits[5], (HEADS,), jnp.float32, 0.5, 1.5), 0.5, 1.5)
    teacher = centred(part_keys[6], (SEQLEN, HEADS * HEAD_DIM), 1.0, 6.0, ((0, 16),))
    doc_lengths = uneven(part_keys[7], DOCS, SEQLEN, MOST, 2).astype(jnp.int32)
    return dict(values=values, b_proj=b_proj, c_proj=c_proj, step_sizes=step_sizes, decay_rates=decay_rates, skip_gain=skip_gain, teacher=teacher, doc_lengths=doc_lengths)


highest = lax.Precision.HIGHEST


def product(form, left, right):
    return jnp.einsum(form, left.astype(jnp.float32), right.astype(jnp.float32), precision=highest)


def decay_terms(step_sizes, decay_rates, doc_count):
    length = step_sizes.shape[0]
    log_level = jnp.cumsum(-(step_sizes * decay_rates[None, :]), axis=0)
    last_level = log_level[-1]
    positions = jnp.arange(length, dtype=jnp.int32)
    same_doc = (doc_count[:, None] == doc_count[None, :]) & (positions[:, None] >= positions[None, :])
    log_gap = log_level.T[:, :, None] - log_level.T[:, None, :]
    banded = jnp.where(same_doc[None], jnp.exp(jnp.minimum(log_gap, 0.0)), 0.0)
    enter_weight = jnp.where((doc_count == 0)[:, None], jnp.exp(log_level), 0.0)
    leave_weight = jnp.where((doc_count == doc_count[-1])[:, None], jnp.exp(last_level[None, :] - log_level), 0.0)
    through_decay = jnp.where(doc_count[-1] == 0, jnp.exp(last_level), 0.0)
    return banded, enter_weight, leave_weight, through_decay


def forward_local(inputs, b_proj, c_proj, step_sizes, banded, leave_weight):
    scaled = (step_sizes[:, :, None] * inputs.astype(jnp.float32)).astype(jnp.bfloat16)
    scores = jnp.dot(c_proj, b_proj.T, preferred_element_type=jnp.float32)
    mixing = (banded * scores[None]).astype(jnp.bfloat16)
    inner = product("hts,shp->thp", mixing, scaled)
    local_state = product("shp,sn->hpn", leave_weight[:, :, None] * scaled.astype(jnp.float32), b_proj)
    return scaled, mixing, inner, local_state


def backward_local(b_proj, c_proj, step_sizes, skip_gain, banded, mixing, scaled, enter_weight, leave_weight, mismatch, state_in, adjoint_in):
    low = mismatch.astype(jnp.bfloat16)
    wide_b = b_proj.astype(jnp.float32)
    wide_c = c_proj.astype(jnp.float32)
    back_inner = product("hts,thp->shp", mixing, low)
    from_later = jnp.einsum("hpn,sn->shp", adjoint_in, wide_b, precision=highest)
    grad_values = skip_gain[None, :, None] * mismatch + step_sizes[:, :, None] * (back_inner + leave_weight[:, :, None] * from_later)
    pair_terms = product("thp,shp->hts", low, scaled)
    pair_sum = jnp.sum(banded * pair_terms, axis=0)
    grad_c = jnp.dot(pair_sum, wide_b, precision=highest, preferred_element_type=jnp.float32)
    grad_c = grad_c + jnp.einsum("thp,hpn->tn", enter_weight[:, :, None] * mismatch, state_in, precision=highest)
    grad_b = jnp.dot(pair_sum.T, wide_c, precision=highest, preferred_element_type=jnp.float32)
    grad_b = grad_b + jnp.einsum("shp,hpn->sn", leave_weight[:, :, None] * scaled.astype(jnp.float32), adjoint_in, precision=highest)
    return grad_values, grad_b, grad_c


def reference(values, b_proj, c_proj, step_sizes, decay_rates, skip_gain, teacher, doc_lengths):
    length = TOK_DEV
    blocks = SEQLEN // length
    doc_starts = jnp.cumsum(doc_lengths) - doc_lengths
    positions = jnp.arange(SEQLEN, dtype=jnp.int32)
    flags = jnp.any(positions[:, None] == doc_starts[None, :].astype(jnp.int32), axis=1).astype(jnp.int32)
    counts = jnp.cumsum(flags.reshape(blocks, length), axis=1).astype(jnp.int32)
    inputs = values.reshape(blocks, length, HEADS, HEAD_DIM)
    b_blocks = b_proj.reshape(blocks, length, STATE)
    c_blocks = c_proj.reshape(blocks, length, STATE)
    step_blocks = step_sizes.reshape(blocks, length, HEADS)
    teacher_blocks = teacher.astype(jnp.float32).reshape(blocks, length, HEADS, HEAD_DIM)

    def forward(state_in, block):
        inputs_b, b_blk, c_blk, step_blk, teacher_blk, count_blk = block
        banded, enter_weight, leave_weight, through_decay = decay_terms(step_blk, decay_rates, count_blk)
        scaled, mixing, inner, local_state = forward_local(inputs_b, b_blk, c_blk, step_blk, banded, leave_weight)
        output = inner + enter_weight[:, :, None] * jnp.einsum("hpn,tn->thp", state_in, c_blk.astype(jnp.float32), precision=highest)
        output = output + skip_gain[None, :, None] * inputs_b.astype(jnp.float32)
        mismatch = output - teacher_blk
        new_state = through_decay[:, None, None] * state_in + local_state
        return new_state, (mismatch, state_in, jnp.sum(mismatch * mismatch))

    zero_state = jnp.zeros((HEADS, HEAD_DIM, STATE), jnp.float32)
    _, (mismatch, states, squares) = lax.scan(forward, zero_state, (inputs, b_blocks, c_blocks, step_blocks, teacher_blocks, counts))

    def backward(adjoint_in, block):
        inputs_b, b_blk, c_blk, step_blk, count_blk, mismatch_blk, state_blk = block
        banded, enter_weight, leave_weight, through_decay = decay_terms(step_blk, decay_rates, count_blk)
        scaled, mixing, inner, local_state = forward_local(inputs_b, b_blk, c_blk, step_blk, banded, leave_weight)
        grads = backward_local(b_blk, c_blk, step_blk, skip_gain, banded, mixing, scaled, enter_weight, leave_weight, mismatch_blk, state_blk, adjoint_in)
        back_local = jnp.einsum("thp,tn->hpn", enter_weight[:, :, None] * mismatch_blk, c_blk.astype(jnp.float32), precision=highest)
        return through_decay[:, None, None] * adjoint_in + back_local, grads

    _, (grad_values, grad_b, grad_c) = lax.scan(backward, zero_state, (inputs, b_blocks, c_blocks, step_blocks, counts, mismatch, states), reverse=True)
    loss = (jnp.sum(squares) / (SEQLEN * HEADS * HEAD_DIM)).reshape(1)
    return loss, grad_values.reshape(SEQLEN, HEADS * HEAD_DIM), grad_b.reshape(SEQLEN, STATE), grad_c.reshape(SEQLEN, STATE)
```

```python
import functools
import jax
import jax.numpy as jnp
from jax import lax
from jax.experimental import pallas as pl
from jax.experimental.pallas import tpu as pltpu
from jax.sharding import PartitionSpec as P

F32 = jnp.float32
BF16 = jnp.bfloat16
PAD = 8
CHUNK = 512
LIMIT = 40 << 20


def dot(a, b):
    return jnp.dot(a, b, preferred_element_type=F32)


def dot_nt(a, b):
    return lax.dot_general(a, b, (((1,), (1,)), ((), ())), preferred_element_type=F32)


def iota(shape, axis):
    return lax.broadcasted_iota(jnp.int32, shape, axis)


def split3(x):
    hi = x.astype(BF16)
    rest = x - hi.astype(F32)
    mid = rest.astype(BF16)
    lo = (rest - mid.astype(F32)).astype(BF16)
    return jnp.concatenate([hi, mid, lo], axis=1)


def split2_rows(x):
    hi = x.astype(BF16)
    lo = (x - hi.astype(F32)).astype(BF16)
    return jnp.concatenate([hi, lo], axis=0)


def expander(heads, head_dim, width, chunk):
    rows = lax.rem(iota((3 * heads, width), 0), heads)
    cols = iota((3 * heads, width), 1) // head_dim + chunk * (width // head_dim)
    return (rows == cols).astype(F32).astype(BF16)


def doc_ids(info, docs, length, axis):
    shape = (length, 1) if axis == 0 else (1, length)
    place = iota(shape, axis)
    ids = jnp.zeros(shape, jnp.int32)
    before = jnp.int32(0)
    final = jnp.int32(0)
    start = -info[0]
    for d in range(docs):
        ids = ids + (place >= start).astype(jnp.int32)
        before = before + (start <= -1).astype(jnp.int32)
        final = final + (start <= length - 1).astype(jnp.int32)
        start = start + info[2 + d]
    return ids, before, final


def same_doc(info, docs, length):
    col = doc_ids(info, docs, length, 0)[0]
    row = doc_ids(info, docs, length, 1)[0]
    return (col == row) & (iota((length, length), 0) >= iota((length, length), 1))


def put_half(info, j, per_half, keep_ref, send_ref, state, decay):
    width = state.shape[1]
    rows = state.shape[0]
    place = pl.ds(pl.multiple_of(lax.rem(j, per_half) * width, width), width)
    mine = j // per_half == info[1]

    def put(ref):
        ref[0:rows, place] = state
        ref[rows : rows + PAD, place] = jnp.broadcast_to(decay, (PAD, width))

    pl.when(mine)(lambda: put(keep_ref))
    pl.when(jnp.logical_not(mine))(lambda: put(send_ref))


def get_half(info, j, per_half, mine_ref, other_ref, width):
    place = pl.ds(pl.multiple_of(lax.rem(j, per_half) * width, width), width)
    own = (j // per_half == info[1]).astype(F32)
    return jnp.where(own > 0.5, mine_ref[:, place], other_ref[:, place])


def prepare_kernel(
    docs,
    info,
    v_ref,
    b_ref,
    c_ref,
    step_ref,
    rate_ref,
    gain_ref,
    x_ref,
    keep_ref,
    send_ref,
    enter3_ref,
    sf3_ref,
    rows_ref,
    bm_ref,
    cm_ref,
    f3,
    s3,
    r3,
    bt,
):
    j = pl.program_id(0)
    length, heads = step_ref.shape
    width = v_ref.shape[1]
    head_dim = width * pl.num_programs(0) // heads

    @pl.when(j == 0)
    def _():
        step = step_ref[...]
        lower = (iota((length, length), 0) >= iota((length, length), 1)).astype(F32).astype(BF16)
        sums = dot(lower, split3(-(step * rate_ref[...])))
        level = sums[:, :heads] + sums[:, heads : 2 * heads] + sums[:, 2 * heads :]
        middle = level[length // 2 - 1 : length // 2, :]
        last = level[length - 1 : length, :]
        ids, before, final = doc_ids(info, docs, length, 0)
        leave = jnp.exp(middle - level)
        enter3_ref[...] = split3(jnp.exp(level - middle))
        f3[...] = split3(leave)
        s3[...] = split3(step)
        sf3_ref[...] = split3(step * leave)
        through = jnp.where(before == final, jnp.exp(last), 0.0)
        pick = iota((PAD, heads), 0)
        table = jnp.where(pick == 0, jnp.exp(middle), 0.0)
        table = jnp.where(pick == 1, jnp.exp(last - middle), table)
        table = jnp.where(pick == 2, through, table)
        table = jnp.where(pick == 3, gain_ref[...], table)
        r3[...] = split3(table)
        bm = jnp.where(ids == final, b_ref[...].astype(F32), 0.0)
        bm_ref[...] = bm.astype(BF16)
        bt[...] = bm.T.astype(BF16)
        cm_ref[...] = jnp.where(ids == before, c_ref[...].astype(F32), 0.0).astype(BF16)

    spread = expander(heads, head_dim, width, j)
    rows = dot(r3[...], spread)
    rows_ref[...] = rows
    scaled = (dot(s3[...], spread) * v_ref[...].astype(F32)).astype(BF16).astype(F32)
    x = dot(f3[...], spread) * scaled
    hi = x.astype(BF16)
    lo = (x - hi.astype(F32)).astype(BF16)
    x_ref[...] = hi
    state = (dot(bt[...], hi) + dot(bt[...], lo)) * rows[1:2, :]
    put_half(info, j, pl.num_programs(0) // 2, keep_ref, send_ref, state, rows[2:3, :])


def inner_kernel(docs, info, x_ref, v_ref, teach_ref, b_ref, c_ref, enter3_ref, rows_ref, base_ref, st_ref, s):
    j = pl.program_id(0)
    length = x_ref.shape[0]
    width = x_ref.shape[1]
    heads = enter3_ref.shape[1] // 3
    head_dim = width * pl.num_programs(0) // heads

    @pl.when(j == 0)
    def _():
        scores = jnp.where(same_doc(info, docs, length), dot_nt(c_ref[...], b_ref[...]), 0.0)
        s[...] = scores.astype(BF16)
        st_ref[...] = scores.T.astype(BF16)

    enter = dot(enter3_ref[...], expander(heads, head_dim, width, j))
    base_ref[...] = (
        enter * dot(s[...], x_ref[...])
        + rows_ref[3:4, :] * v_ref[...].astype(F32)
        - teach_ref[...].astype(F32)
    )


def mismatch_kernel(
    info, base_ref, enter3_ref, rows_ref, cm_ref, mine_ref, other_ref, mm_ref, y_ref, keep_ref, send_ref, loss_ref, ct
):
    j = pl.program_id(0)
    length, width = base_ref.shape
    heads = enter3_ref.shape[1] // 3
    head_dim = width * pl.num_programs(0) // heads
    per_half = pl.num_programs(0) // 2

    @pl.when(j == 0)
    def _():
        ct[...] = cm_ref[...].astype(F32).T.astype(BF16)
        loss_ref[...] = jnp.zeros_like(loss_ref)

    enter = dot(enter3_ref[...], expander(heads, head_dim, width, j))
    state = split2_rows(get_half(info, j, per_half, mine_ref, other_ref, width) * rows_ref[0:1, :])
    cm = cm_ref[...]
    mm = base_ref[...] + enter * dot(jnp.concatenate([cm, cm], axis=1), state)
    mm_ref[...] = mm
    y = (enter * mm).astype(BF16)
    y_ref[...] = y
    loss_ref[...] += jnp.sum((mm * mm).reshape(length // 8, 8, width), axis=0)
    put_half(info, j, per_half, keep_ref, send_ref, dot(ct[...], y) * rows_ref[0:1, :], rows_ref[2:3, :])


def pair_kernel(
    docs,
    info,
    mm_ref,
    y_ref,
    x_ref,
    st_ref,
    sf3_ref,
    rows_ref,
    b_ref,
    c_ref,
    mine_ref,
    other_ref,
    g_ref,
    gb_ref,
    gc_ref,
    pair,
    acc,
):
    j = pl.program_id(0)
    length, width = mm_ref.shape
    heads = sf3_ref.shape[1] // 3
    head_dim = width * pl.num_programs(0) // heads
    width_n = b_ref.shape[1]

    @pl.when(j == 0)
    def _():
        pair[...] = jnp.zeros_like(pair)
        acc[...] = jnp.zeros_like(acc)

    y = y_ref[...]
    pair[...] += dot_nt(y, x_ref[...])
    sf = dot(sf3_ref[...], expander(heads, head_dim, width, j))
    g_ref[...] = rows_ref[3:4, :] * mm_ref[...] + sf * dot(st_ref[...], y)
    state = get_half(info, j, pl.num_programs(0) // 2, mine_ref, other_ref, width) * rows_ref[0:1, :]
    acc[...] += dot_nt(y, split2_rows(state))

    @pl.when(j == pl.num_programs(0) - 1)
    def _():
        masked = jnp.where(same_doc(info, docs, length), pair[...], 0.0)
        hi = masked.astype(BF16)
        lo = (masked - hi.astype(F32)).astype(BF16)
        turned = masked.T
        hi_t = turned.astype(BF16)
        lo_t = (turned - hi_t.astype(F32)).astype(BF16)
        ids, before, _final = doc_ids(info, docs, length, 0)
        through = acc[:, :width_n] + acc[:, width_n:]
        gc_ref[...] = dot(hi, b_ref[...]) + dot(lo, b_ref[...]) + jnp.where(ids == before, through, 0.0)
        gb_ref[...] = dot(hi_t, c_ref[...]) + dot(lo_t, c_ref[...])


def finish_kernel(
    docs, info, g_ref, x_ref, sf3_ref, rows_ref, bm_ref, gb_part_ref, mine_ref, other_ref, gv_ref, gb_ref, acc
):
    j = pl.program_id(0)
    length, width = g_ref.shape
    heads = sf3_ref.shape[1] // 3
    head_dim = width * pl.num_programs(0) // heads
    width_n = bm_ref.shape[1]

    @pl.when(j == 0)
    def _():
        acc[...] = jnp.zeros_like(acc)

    sf = dot(sf3_ref[...], expander(heads, head_dim, width, j))
    adjoint = split2_rows(
        get_half(info, j, pl.num_programs(0) // 2, mine_ref, other_ref, width) * rows_ref[1:2, :]
    )
    bm = bm_ref[...]
    gv_ref[...] = g_ref[...] + sf * dot(jnp.concatenate([bm, bm], axis=1), adjoint)
    acc[...] += dot_nt(x_ref[...], adjoint)

    @pl.when(j == pl.num_programs(0) - 1)
    def _():
        ids, _before, final = doc_ids(info, docs, length, 0)
        through = acc[:, :width_n] + acc[:, width_n:]
        gb_ref[...] = gb_part_ref[...] + jnp.where(ids == final, through, 0.0)


def call(kernel, info, ins, in_kinds, outs, out_kinds, scratch, steps, flops):
    def spec(shape, kind):
        if kind == "cols":
            return pl.BlockSpec((shape[0], shape[1] // steps), lambda j, info: (0, j))
        return pl.BlockSpec(shape, lambda j, info: (0, 0))

    size = sum(a.size * a.dtype.itemsize for a in ins) + sum(o.size * o.dtype.itemsize for o in outs)
    return pl.pallas_call(
        kernel,
        out_shape=outs,
        grid_spec=pltpu.PrefetchScalarGridSpec(
            num_scalar_prefetch=1,
            grid=(steps,),
            in_specs=[spec(a.shape, k) for a, k in zip(ins, in_kinds)],
            out_specs=[spec(o.shape, k) for o, k in zip(outs, out_kinds)],
            scratch_shapes=scratch,
        ),
        compiler_params=pltpu.CompilerParams(
            dimension_semantics=("arbitrary",), vmem_limit_bytes=LIMIT
        ),
        cost_estimate=pl.CostEstimate(flops=flops, bytes_accessed=size, transcendentals=0),
    )(info, *ins)


def swap(x, devices):
    return lax.ppermute(x, "seq", [(i, i ^ 1) for i in range(devices)])


def shift(x, by, devices):
    return lax.ppermute(
        x, "seq", [(i, i + by) for i in range(devices) if 0 <= i + by < devices]
    )


def carry(keep, send, odd, devices, way):
    rows = keep.shape[0] - PAD
    got = swap(send, devices)
    near = (odd == 0) if way == 1 else (odd == 1)
    first = jnp.where(near, keep, got)
    second = jnp.where(near, got, keep)
    first_decay = first[rows : rows + 1]
    second_decay = second[rows : rows + 1]
    both = second[:rows] + second_decay * first[:rows]
    decay = jnp.broadcast_to(first_decay * second_decay, (PAD, both.shape[1]))
    packed = jnp.concatenate([both, decay], axis=0)
    reach = max(1, devices // 8)
    one = shift(packed, 2 * way, devices)
    two = shift(packed if reach > 2 else both, 4 * way, devices)
    state = one[:rows] + one[rows : rows + 1] * two[:rows]
    if reach > 2:
        run = one[rows:] * two[rows:]
        span = 2
        while span < reach:
            more = shift(jnp.concatenate([state, run], axis=0), 2 * span * way, devices)
            state = state + run[0:1] * more[:rows]
            run = run * more[rows:]
            span *= 2
    inside = first[:rows] + first_decay * state
    mine = jnp.where(near, state, inside)
    other = swap(jnp.where(near, inside, state), devices)
    return mine, other


def local(values, b_proj, c_proj, step_sizes, decay_rates, skip_gain, teacher, doc_lengths):
    length, total = values.shape
    heads = step_sizes.shape[1]
    state = b_proj.shape[1]
    docs = doc_lengths.shape[0]
    devices = lax.axis_size("seq")
    index = lax.axis_index("seq")
    odd = lax.rem(index, 2)
    info = jnp.concatenate([jnp.stack([index * length, odd]).astype(jnp.int32), doc_lengths])
    steps = total // CHUNK
    rates = decay_rates.reshape(1, heads)
    gains = skip_gain.reshape(1, heads)

    def out(*shape, dtype=F32):
        return jax.ShapeDtypeStruct(shape, dtype)

    half = out(state + PAD, total // 2)
    thirds = out(length, 3 * heads, dtype=BF16)
    square = 2 * length * length * total
    thin = 2 * length * state * total
    x, keep, send, enter3, sf3, rows, bm, cm = call(
        functools.partial(prepare_kernel, docs),
        info,
        [values, b_proj, c_proj, step_sizes, rates, gains],
        ["cols", "all", "all", "all", "all", "all"],
        [
            out(length, total, dtype=BF16),
            half,
            half,
            thirds,
            thirds,
            out(PAD, total),
            out(length, state, dtype=BF16),
            out(length, state, dtype=BF16),
        ],
        ["cols", "all", "all", "all", "all", "cols", "all", "all"],
        [
            pltpu.VMEM((length, 3 * heads), BF16),
            pltpu.VMEM((length, 3 * heads), BF16),
            pltpu.VMEM((PAD, 3 * heads), BF16),
            pltpu.VMEM((state, length), BF16),
        ],
        steps,
        4 * thin,
    )
    base, score_t = call(
        functools.partial(inner_kernel, docs),
        info,
        [x, values, teacher, b_proj, c_proj, enter3, rows],
        ["cols", "cols", "cols", "all", "all", "all", "cols"],
        [out(length, total), out(length, length, dtype=BF16)],
        ["cols", "all"],
        [pltpu.VMEM((length, length), BF16)],
        steps,
        square,
    )
    state_mine, state_other = carry(keep, send, odd, devices, 1)
    mm, y, back_keep, back_send, squares = call(
        mismatch_kernel,
        info,
        [base, enter3, rows, cm, state_mine, state_other],
        ["cols", "all", "cols", "all", "all", "all"],
        [out(length, total), out(length, total, dtype=BF16), half, half, out(8, CHUNK)],
        ["cols", "cols", "all", "all", "all"],
        [pltpu.VMEM((state, length), BF16)],
        steps,
        4 * thin,
    )
    parts = jnp.broadcast_to(jnp.sum(squares), (devices, 128))
    parts = lax.all_to_all(parts, "seq", split_axis=0, concat_axis=0, tiled=True)
    loss = (jnp.sum(parts[:, 0]) / (devices * length * total)).reshape(1)
    g, gb_part, grad_c = call(
        functools.partial(pair_kernel, docs),
        info,
        [mm, y, x, score_t, sf3, rows, b_proj, c_proj, state_mine, state_other],
        ["cols", "cols", "cols", "all", "all", "cols", "all", "all", "all", "all"],
        [out(length, total), out(length, state), out(length, state)],
        ["cols", "all", "all"],
        [pltpu.VMEM((length, length), F32), pltpu.VMEM((length, 2 * state), F32)],
        steps,
        2 * square,
    )
    adj_mine, adj_other = carry(back_keep, back_send, odd, devices, -1)
    grad_values, grad_b = call(
        functools.partial(finish_kernel, docs),
        info,
        [g, x, sf3, rows, bm, gb_part, adj_mine, adj_other],
        ["cols", "cols", "all", "cols", "all", "all", "all", "all"],
        [out(length, total), out(length, state)],
        ["cols", "all"],
        [pltpu.VMEM((length, 2 * state), F32)],
        steps,
        4 * thin,
    )
    return loss, grad_values, grad_b, grad_c


def solution(mesh):
    rows = P(("groups", "seq"), None)
    in_specs = (rows, rows, rows, rows, P(), P(), rows, P("groups"))
    out_specs = (P("groups"), rows, rows, rows)
    return jax.shard_map(local, mesh=mesh, in_specs=in_specs, out_specs=out_specs, check_vma=False)
```

```python
import functools
import jax
import jax.numpy as jnp
from jax import lax
from jax.experimental import pallas as pl
from jax.experimental.pallas import tpu as pltpu
from jax.sharding import PartitionSpec as P

F32 = jnp.float32
BF16 = jnp.bfloat16
PAD = 8
CHUNK = 512
LIMIT = 60 << 20


def dot(a, b):
    return jnp.dot(a, b, preferred_element_type=F32)


def dot_nt(a, b):
    return lax.dot_general(a, b, (((1,), (1,)), ((), ())), preferred_element_type=F32)


def iota(shape, axis):
    return lax.broadcasted_iota(jnp.int32, shape, axis)


def dot_tn(a, b):
    return lax.dot_general(a, b, (((0,), (0,)), ((), ())), preferred_element_type=F32)


def split3(x):
    hi = x.astype(BF16)
    rest = x - hi.astype(F32)
    mid = rest.astype(BF16)
    lo = (rest - mid.astype(F32)).astype(BF16)
    return jnp.concatenate([hi, mid, lo], axis=0)


def split2(x):
    hi = x.astype(BF16)
    lo = (x - hi.astype(F32)).astype(BF16)
    return jnp.concatenate([hi, lo], axis=0)


def twice(x):
    return jnp.concatenate([x, x], axis=0)


def expander(heads, head_dim, width, chunk):
    rows = lax.rem(iota((3 * heads, width), 0), heads)
    cols = iota((3 * heads, width), 1) // head_dim + chunk * (width // head_dim)
    return (rows == cols).astype(F32).astype(BF16)


def doc_ids(lengths, docs, length, axis):
    shape = (length, 1) if axis == 0 else (1, length)
    place = iota(shape, axis)
    ids = jnp.zeros(shape, jnp.int32)
    before = jnp.int32(0)
    final = jnp.int32(0)
    start = -lax.axis_index("seq") * length
    for d in range(docs):
        ids = ids + (place >= start).astype(jnp.int32)
        before = before + (start <= -1).astype(jnp.int32)
        final = final + (start <= length - 1).astype(jnp.int32)
        start = start + lengths[d]
    return ids, before, final


def own_half(j, per_half):
    return j // per_half == lax.rem(lax.axis_index("seq"), 2)


def put_half(j, per_half, keep_ref, send_ref, state, decay):
    width = state.shape[1]
    rows = state.shape[0]
    place = pl.ds(pl.multiple_of(lax.rem(j, per_half) * width, width), width)
    mine = own_half(j, per_half)

    def put(ref):
        ref[0:rows, place] = state
        ref[rows : rows + 1, place] = decay

    pl.when(mine)(lambda: put(keep_ref))
    pl.when(jnp.logical_not(mine))(lambda: put(send_ref))


def get_half(j, per_half, mine_ref, other_ref, width):
    place = pl.ds(pl.multiple_of(lax.rem(j, per_half) * width, width), width)
    own = own_half(j, per_half).astype(F32)
    return jnp.where(own > 0.5, mine_ref[:, place], other_ref[:, place])


def column(row):
    n = row.shape[1]
    return jnp.sum(jnp.where(iota((n, n), 0) == iota((n, n), 1), row, 0.0), axis=1, keepdims=True)


def prepare_kernel(
    docs,
    lengths,
    v_ref,
    b_ref,
    c_ref,
    step_ref,
    rate_ref,
    gain_ref,
    x_ref,
    keep_ref,
    send_ref,
    enter3_ref,
    sf3_ref,
    rows_ref,
    bm_ref,
    cm_ref,
    f3,
    s3,
    r3,
):
    j = pl.program_id(0)
    heads, length = step_ref.shape
    width = v_ref.shape[1]
    head_dim = width * pl.num_programs(0) // heads

    @pl.when(j == 0)
    def _():
        blank = jnp.zeros((PAD, keep_ref.shape[1]), F32)
        keep_ref[b_ref.shape[0] :, :] = blank
        send_ref[b_ref.shape[0] :, :] = blank
        step = step_ref[...]
        upper = (iota((length, length), 0) <= iota((length, length), 1)).astype(F32).astype(BF16)
        sums = dot(split3(-(step * column(rate_ref[...]))), upper)
        level = sums[:heads] + sums[heads : 2 * heads] + sums[2 * heads :]
        middle = level[:, length // 2 - 1 : length // 2]
        last = level[:, length - 1 : length]
        ids, before, final = doc_ids(lengths, docs, length, 1)
        leave = jnp.exp(middle - level)
        enter3_ref[...] = split3(jnp.exp(level - middle))
        f3[...] = split3(leave)
        s3[...] = split3(step)
        sf3_ref[...] = split3(step * leave)
        through = jnp.where(before == final, jnp.exp(last), 0.0)
        pick = iota((heads, 128), 1)
        table = jnp.where(pick == 0, jnp.exp(middle), 0.0)
        table = jnp.where(pick == 1, jnp.exp(last - middle), table)
        table = jnp.where(pick == 2, through, table)
        table = jnp.where(pick == 3, column(gain_ref[...]), table)
        r3[...] = split3(table)
        bm_ref[...] = jnp.where(ids == final, b_ref[...].astype(F32), 0.0).astype(BF16)
        cm_ref[...] = jnp.where(ids == before, c_ref[...].astype(F32), 0.0).astype(BF16)

    spread = expander(heads, head_dim, width, j)
    rows = dot_tn(r3[...], spread)[:PAD]
    rows_ref[...] = rows
    scaled = (dot_tn(s3[...], spread) * v_ref[...].astype(F32)).astype(BF16).astype(F32)
    x = dot_tn(f3[...], spread) * scaled
    hi = x.astype(BF16)
    lo = (x - hi.astype(F32)).astype(BF16)
    x_ref[...] = hi
    state = (dot(bm_ref[...], hi) + dot(bm_ref[...], lo)) * rows[1:2, :]
    put_half(j, pl.num_programs(0) // 2, keep_ref, send_ref, state, rows[2:3, :])


def inner_kernel(
    docs, lengths, x_ref, v_ref, teach_ref, b_ref, c_ref, enter3_ref, rows_ref, base_ref, st_ref, s
):
    j = pl.program_id(0)
    length = x_ref.shape[0]
    width = x_ref.shape[1]
    heads = enter3_ref.shape[0] // 3
    head_dim = width * pl.num_programs(0) // heads

    @pl.when(j == 0)
    def _():
        col = doc_ids(lengths, docs, length, 0)[0]
        row = doc_ids(lengths, docs, length, 1)[0]
        down = iota((length, length), 0)
        along = iota((length, length), 1)
        scores = dot_tn(c_ref[...], b_ref[...])
        s[...] = jnp.where((col == row) & (down >= along), scores, 0.0).astype(BF16)
        turned = dot_tn(b_ref[...], c_ref[...])
        st_ref[...] = jnp.where((col == row) & (down <= along), turned, 0.0).astype(BF16)

    enter = dot_tn(enter3_ref[...], expander(heads, head_dim, width, j))
    base_ref[...] = (
        enter * dot(s[...], x_ref[...])
        + rows_ref[3:4, :] * v_ref[...].astype(F32)
        - teach_ref[...].astype(F32)
    )


def mismatch_kernel(
    base_ref, enter3_ref, rows_ref, cm_ref, mine_ref, other_ref, mm_ref, y_ref, keep_ref, send_ref
):
    j = pl.program_id(0)
    length, width = base_ref.shape
    heads = enter3_ref.shape[0] // 3
    head_dim = width * pl.num_programs(0) // heads
    per_half = pl.num_programs(0) // 2

    @pl.when(j == 0)
    def _():
        blank = jnp.zeros((PAD, keep_ref.shape[1]), F32)
        keep_ref[cm_ref.shape[0] :, :] = blank
        send_ref[cm_ref.shape[0] :, :] = blank

    enter = dot_tn(enter3_ref[...], expander(heads, head_dim, width, j))
    state = split2(get_half(j, per_half, mine_ref, other_ref, width) * rows_ref[0:1, :])
    cm = cm_ref[...]
    mm = base_ref[...] + enter * dot_tn(twice(cm), state)
    mm_ref[...] = mm
    y = (enter * mm).astype(BF16)
    y_ref[...] = y
    squares = jnp.sum(mm * mm, axis=0, keepdims=True)
    line = slice(cm_ref.shape[0] + 1, cm_ref.shape[0] + 2)
    keep_ref[line, :width] += squares
    send_ref[line, :width] += squares
    put_half(j, per_half, keep_ref, send_ref, dot(cm, y) * rows_ref[0:1, :], rows_ref[2:3, :])


def pair_kernel(
    docs,
    lengths,
    mm_ref,
    y_ref,
    x_ref,
    st_ref,
    sf3_ref,
    rows_ref,
    b_ref,
    c_ref,
    mine_ref,
    other_ref,
    g_ref,
    gb_ref,
    gc_ref,
    pair,
    acc,
):
    j = pl.program_id(0)
    length, width = mm_ref.shape
    heads = sf3_ref.shape[0] // 3
    head_dim = width * pl.num_programs(0) // heads
    width_n = b_ref.shape[0]

    @pl.when(j == 0)
    def _():
        pair[...] = jnp.zeros_like(pair)
        acc[...] = jnp.zeros_like(acc)

    y = y_ref[...]
    pair[...] += dot_nt(y, x_ref[...])
    sf = dot_tn(sf3_ref[...], expander(heads, head_dim, width, j))
    g_ref[...] = rows_ref[3:4, :] * mm_ref[...] + sf * dot(st_ref[...], y)
    state = get_half(j, pl.num_programs(0) // 2, mine_ref, other_ref, width) * rows_ref[0:1, :]
    acc[...] += dot_nt(split2(state), y)

    @pl.when(j == pl.num_programs(0) - 1)
    def _():
        col = doc_ids(lengths, docs, length, 0)[0]
        row, before, _final = doc_ids(lengths, docs, length, 1)
        keep = (col == row) & (iota((length, length), 0) >= iota((length, length), 1))
        masked = jnp.where(keep, pair[...], 0.0)
        hi = masked.astype(BF16)
        lo = (masked - hi.astype(F32)).astype(BF16)
        through = acc[:width_n] + acc[width_n:]
        gc_ref[...] = dot_nt(b_ref[...], hi) + dot_nt(b_ref[...], lo) + jnp.where(row == before, through, 0.0)
        gb_ref[...] = dot(c_ref[...], hi) + dot(c_ref[...], lo)


def finish_kernel(
    docs, lengths, g_ref, x_ref, sf3_ref, rows_ref, bm_ref, gb_part_ref, mine_ref, other_ref, gv_ref, gb_ref, acc
):
    j = pl.program_id(0)
    length, width = g_ref.shape
    heads = sf3_ref.shape[0] // 3
    head_dim = width * pl.num_programs(0) // heads
    width_n = bm_ref.shape[0]

    @pl.when(j == 0)
    def _():
        acc[...] = jnp.zeros_like(acc)

    sf = dot_tn(sf3_ref[...], expander(heads, head_dim, width, j))
    adjoint = split2(
        get_half(j, pl.num_programs(0) // 2, mine_ref, other_ref, width) * rows_ref[1:2, :]
    )
    gv_ref[...] = g_ref[...] + sf * dot_tn(twice(bm_ref[...]), adjoint)
    acc[...] += dot_nt(x_ref[...], adjoint)

    @pl.when(j == pl.num_programs(0) - 1)
    def _():
        ids, _before, final = doc_ids(lengths, docs, length, 1)
        through = (acc[:, :width_n] + acc[:, width_n:]).T
        gb_ref[...] = gb_part_ref[...] + jnp.where(ids == final, through, 0.0)


def call(kernel, scalars, ins, in_kinds, outs, out_kinds, scratch, steps, flops):
    def spec(shape, kind):
        if kind == "cols":
            return pl.BlockSpec((shape[0], shape[1] // steps), lambda j, *_: (0, j))
        return pl.BlockSpec(shape, lambda j, *_: (0, 0))

    size = sum(a.size * a.dtype.itemsize for a in ins) + sum(o.size * o.dtype.itemsize for o in outs)
    return pl.pallas_call(
        kernel,
        out_shape=outs,
        grid_spec=pltpu.PrefetchScalarGridSpec(
            num_scalar_prefetch=len(scalars),
            grid=(steps,),
            in_specs=[spec(a.shape, k) for a, k in zip(ins, in_kinds)],
            out_specs=[spec(o.shape, k) for o, k in zip(outs, out_kinds)],
            scratch_shapes=scratch,
        ),
        compiler_params=pltpu.CompilerParams(
            dimension_semantics=("arbitrary",), vmem_limit_bytes=LIMIT
        ),
        cost_estimate=pl.CostEstimate(flops=flops, bytes_accessed=size, transcendentals=0),
    )(*scalars, *ins)


def swap(x, devices):
    return lax.ppermute(x, "seq", [(i, i ^ 1) for i in range(devices)])


def shift(x, by, devices):
    return lax.ppermute(
        x, "seq", [(i, i + by) for i in range(devices) if 0 <= i + by < devices]
    )


def turn(x, by, devices):
    return lax.ppermute(x, "seq", [(i, (i + by) % devices) for i in range(devices)])


def chip_order(way, mine_ref, got_ref):
    near = lax.rem(lax.axis_index("seq"), 2) == (0 if way == 1 else 1)
    near = near.astype(F32) > 0.5
    mine, got = mine_ref[...], got_ref[...]
    return near, jnp.where(near, mine, got), jnp.where(near, got, mine)


def compose_kernel(way, keep_ref, got_ref, packed_ref, both_ref):
    rows = both_ref.shape[0]
    _near, first, second = chip_order(way, keep_ref, got_ref)
    both = second[:rows] + second[rows : rows + 1] * first[:rows]
    both_ref[...] = both
    packed_ref[:rows] = both
    a, b = first[rows:], second[rows:]
    packed_ref[rows:] = jnp.where(iota(a.shape, 0) == 0, a * b, a + b)


def arrive_kernel(way, keep_ref, got_ref, packed_ref, one_ref, two_ref, mine_ref, theirs_ref, line_ref):
    rows = mine_ref.shape[0]
    near, first, _second = chip_order(way, keep_ref, got_ref)
    state = one_ref[:rows] + one_ref[rows : rows + 1] * two_ref[:rows]
    inside = first[:rows] + first[rows : rows + 1] * state
    mine_ref[...] = jnp.where(near, state, inside)
    theirs_ref[...] = jnp.where(near, inside, state)
    line_ref[...] = packed_ref[rows + 1 : rows + 2] + one_ref[rows + 1 : rows + 2]


def small(kernel, ins, outs):
    size = sum(a.size * a.dtype.itemsize for a in ins) + sum(o.size * o.dtype.itemsize for o in outs)
    return pl.pallas_call(
        kernel,
        out_shape=outs,
        in_specs=[pl.BlockSpec(memory_space=pltpu.VMEM)] * len(ins),
        out_specs=[pl.BlockSpec(memory_space=pltpu.VMEM)] * len(outs),
        compiler_params=pltpu.CompilerParams(vmem_limit_bytes=8 << 20),
        cost_estimate=pl.CostEstimate(flops=0, bytes_accessed=size, transcendentals=0),
    )(*ins)


def carry(keep, send, devices, way, beside):
    rows, width = keep.shape[0] - PAD, keep.shape[1]
    part = jax.ShapeDtypeStruct((rows, width), F32)
    got = swap(send, devices)
    packed, both = small(
        functools.partial(compose_kernel, way), [keep, got], [jax.ShapeDtypeStruct(keep.shape, F32), part]
    )
    reach = max(1, devices // 8)
    one = shift(packed, 2, devices) if way == 1 else turn(packed, -2, devices)
    two = shift(packed if reach > 2 else both, 4 * way, devices)
    if reach > 2:
        state = one[:rows] + one[rows : rows + 1] * two[:rows]
        run = one[rows : rows + 1] * two[rows : rows + 1]
        span = 2
        while span < reach:
            more = shift(jnp.concatenate([state, jnp.broadcast_to(run, (PAD, width))], axis=0), 2 * span * way, devices)
            state = state + run * more[:rows]
            run = run * more[rows : rows + 1]
            span *= 2
        one = jnp.concatenate([state, one[rows:]], axis=0)
        two = jnp.zeros_like(state)
    mine, theirs, line = small(
        functools.partial(arrive_kernel, way),
        [keep, got, packed, one, two],
        [part, part, jax.ShapeDtypeStruct((1, width), F32)],
    )
    theirs, beside = lax.optimization_barrier((theirs, beside))
    return mine, swap(theirs, devices), line, beside


def local(values, b_proj, c_proj, step_sizes, decay_rates, skip_gain, teacher, doc_lengths):
    length, total = values.shape
    heads = step_sizes.shape[1]
    state = b_proj.shape[1]
    docs = doc_lengths.shape[0]
    devices = lax.axis_size("seq")
    steps = total // CHUNK
    rates = decay_rates.reshape(1, heads)
    gains = skip_gain.reshape(1, heads)
    b = b_proj.T
    c = c_proj.T

    def out(*shape, dtype=F32):
        return jax.ShapeDtypeStruct(shape, dtype)

    half = out(state + PAD, total // 2)
    thirds = out(3 * heads, length, dtype=BF16)
    narrow = out(state, length, dtype=BF16)
    square = 2 * length * length * total
    thin = 2 * length * state * total
    x, keep, send, enter3, sf3, rows, bm, cm = call(
        functools.partial(prepare_kernel, docs),
        [doc_lengths],
        [values, b, c, step_sizes.T, rates, gains],
        ["cols", "all", "all", "all", "all", "all"],
        [out(length, total, dtype=BF16), half, half, thirds, thirds, out(PAD, total), narrow, narrow],
        ["cols", "all", "all", "all", "all", "cols", "all", "all"],
        [
            pltpu.VMEM((3 * heads, length), BF16),
            pltpu.VMEM((3 * heads, length), BF16),
            pltpu.VMEM((3 * heads, 128), BF16),
        ],
        steps,
        4 * thin,
    )
    inner = call(
        functools.partial(inner_kernel, docs),
        [doc_lengths],
        [x, values, teacher, b, c, enter3, rows],
        ["cols", "cols", "cols", "all", "all", "all", "cols"],
        [out(length, total), out(length, length, dtype=BF16)],
        ["cols", "all"],
        [pltpu.VMEM((length, length), BF16)],
        steps,
        square,
    )
    state_mine, state_other, _, (base, score_t) = carry(keep, send, devices, 1, inner)
    mm, y, back_keep, back_send = call(
        mismatch_kernel,
        [],
        [base, enter3, rows, cm, state_mine, state_other],
        ["cols", "all", "cols", "all", "all", "all"],
        [out(length, total), out(length, total, dtype=BF16), half, half],
        ["cols", "cols", "all", "all"],
        [],
        steps,
        4 * thin,
    )
    pairs = call(
        functools.partial(pair_kernel, docs),
        [doc_lengths],
        [mm, y, x, score_t, sf3, rows, b, c, state_mine, state_other],
        ["cols", "cols", "cols", "all", "all", "cols", "all", "all", "all", "all"],
        [out(length, total), out(state, length), out(state, length)],
        ["cols", "all", "all"],
        [pltpu.VMEM((length, length), F32), pltpu.VMEM((2 * state, length), F32)],
        steps,
        2 * square,
    )
    adj_mine, adj_other, squares, (g, gb_part, grad_c) = carry(back_keep, back_send, devices, -1, pairs)
    span = 2
    while span < devices // 2:
        squares = squares + turn(squares, -2 * span, devices)
        span *= 2
    grad_values, grad_b = call(
        functools.partial(finish_kernel, docs),
        [doc_lengths],
        [g, x, sf3, rows, bm, gb_part, adj_mine, adj_other],
        ["cols", "cols", "all", "cols", "all", "all", "all", "all"],
        [out(length, total), out(state, length)],
        ["cols", "all"],
        [pltpu.VMEM((length, 2 * state), F32)],
        steps,
        4 * thin,
    )
    loss = (jnp.sum(squares) / (devices * length * total)).reshape(1)
    return loss, grad_values, grad_b.T, grad_c.T


def solution(mesh):
    rows = P(("groups", "seq"), None)
    in_specs = (rows, rows, rows, rows, P(), P(), rows, P("groups"))
    out_specs = (P("groups"), rows, rows, rows)
    return jax.shard_map(local, mesh=mesh, in_specs=in_specs, out_specs=out_specs, check_vma=False)
```

```python
import functools
import jax
import jax.numpy as jnp
from jax import lax
from jax.experimental import pallas as pl
from jax.experimental.pallas import tpu as pltpu
from jax.sharding import PartitionSpec as P

F32 = jnp.float32
BF16 = jnp.bfloat16
PAD = 8
STEPS = 4
LIMIT = 24 << 20
HBM = pl.BlockSpec(memory_space=pltpu.MemorySpace.HBM)
VMEM = pl.BlockSpec(memory_space=pltpu.MemorySpace.VMEM)


def dot(a, b):
    return jnp.dot(a, b, preferred_element_type=F32)


def dot_nt(a, b):
    return lax.dot_general(a, b, (((1,), (1,)), ((), ())), preferred_element_type=F32)


def dot_tn(a, b):
    return lax.dot_general(a, b, (((0,), (0,)), ((), ())), preferred_element_type=F32)


def iota(shape, axis):
    return lax.broadcasted_iota(jnp.int32, shape, axis)


def split3(x):
    hi = x.astype(BF16)
    rest = x - hi.astype(F32)
    mid = rest.astype(BF16)
    lo = (rest - mid.astype(F32)).astype(BF16)
    return jnp.concatenate([hi, mid, lo], axis=0)


def split2(x):
    hi = x.astype(BF16)
    lo = (x - hi.astype(F32)).astype(BF16)
    return jnp.concatenate([hi, lo], axis=0)


def twice(x):
    return jnp.concatenate([x, x], axis=0)


def expander(heads, head_dim, width, chunk):
    rows = lax.rem(iota((3 * heads, width), 0), heads)
    cols = iota((3 * heads, width), 1) // head_dim + chunk * (width // head_dim)
    return (rows == cols).astype(F32).astype(BF16)


def column(row):
    n = row.shape[1]
    return jnp.sum(jnp.where(iota((n, n), 0) == iota((n, n), 1), row, 0.0), axis=1, keepdims=True)


def tall(row):
    return jnp.broadcast_to(row, (128, row.shape[1])).T


def same_doc(ids_ref):
    ids = ids_ref[0:1, :]
    return tall(ids)[:, 0:1] == ids


def odd_core():
    return lax.rem(lax.axis_index("seq"), 2)


def put_half(j, keep_ref, send_ref, state, decay):
    width = state.shape[1]
    rows = state.shape[0]
    half = STEPS // 2
    place = slice((j % half) * width, (j % half + 1) * width)
    mine = odd_core() == j // half

    def put(ref):
        ref[0:rows, place] = state
        ref[rows : rows + 1, place] = decay

    pl.when(mine)(lambda: put(keep_ref))
    pl.when(jnp.logical_not(mine))(lambda: put(send_ref))


def get_half(j, mine_ref, other_ref, width):
    half = STEPS // 2
    place = slice((j % half) * width, (j % half + 1) * width)
    own = (odd_core() == j // half).astype(F32)
    return jnp.where(own > 0.5, mine_ref[:, place], other_ref[:, place])


def prepare_kernel(
    lengths_hbm,
    v_hbm,
    b_hbm,
    c_hbm,
    step_hbm,
    rate_hbm,
    gain_hbm,
    x_ref,
    keep_ref,
    send_ref,
    enter3_ref,
    sf3_ref,
    rows_ref,
    bm_ref,
    cm_ref,
    ids_ref,
    lengths,
    v,
    b,
    c,
    step,
    rate,
    gain,
    sems,
    v_sems,
):
    heads, length = step.shape
    total = v.shape[1]
    width = total // STEPS
    head_dim = total // heads
    small = [(step_hbm, step), (rate_hbm, rate), (gain_hbm, gain), (lengths_hbm, lengths), (b_hbm, b), (c_hbm, c)]
    small = [pltpu.make_async_copy(src, dst, sems.at[i]) for i, (src, dst) in enumerate(small)]
    parts = [slice(j * width, (j + 1) * width) for j in range(STEPS)]
    large = [pltpu.make_async_copy(v_hbm.at[:, p], v.at[:, p], v_sems.at[j]) for j, p in enumerate(parts)]
    for copy in small + large:
        copy.start()
    blank = jnp.zeros((PAD, keep_ref.shape[1]), F32)
    keep_ref[b.shape[0] :, :] = blank
    send_ref[b.shape[0] :, :] = blank
    upper = (iota((length, length), 0) <= iota((length, length), 1)).astype(F32).astype(BF16)
    for copy in small:
        copy.wait()
    sums = dot(split3(-(step[...] * column(rate[...]))), upper)
    level = sums[:heads] + sums[heads : 2 * heads] + sums[2 * heads :]
    middle = level[:, length // 2 - 1 : length // 2]
    last = level[:, length - 1 : length]
    place = iota((1, length), 1)
    ids = jnp.zeros((1, length), jnp.int32)
    before = jnp.int32(0)
    final = jnp.int32(0)
    start = -lax.axis_index("seq") * length
    for d in range(lengths.shape[0]):
        ids = ids + (place >= start).astype(jnp.int32)
        before = before + (start <= -1).astype(jnp.int32)
        final = final + (start <= length - 1).astype(jnp.int32)
        start = start + lengths[d]
    first_doc = (ids == before).astype(F32)
    last_doc = (ids == final).astype(F32)
    ids_ref[0:1, :] = ids.astype(F32)
    ids_ref[1:2, :] = first_doc
    ids_ref[2:3, :] = last_doc
    leave = jnp.exp(middle - level)
    enter3_ref[...] = split3(jnp.exp(level - middle))
    f3 = split3(leave)
    s3 = split3(step[...])
    sf3_ref[...] = split3(step[...] * leave)
    through = jnp.where(before == final, jnp.exp(last), 0.0)
    pick = iota((heads, 128), 1)
    table = jnp.where(pick == 0, jnp.exp(middle), 0.0)
    table = jnp.where(pick == 1, jnp.exp(last - middle), table)
    table = jnp.where(pick == 2, through, table)
    table = jnp.where(pick == 3, column(gain[...]), table)
    r3 = split3(table)
    bm = (b[...].astype(F32) * last_doc).astype(BF16)
    bm_ref[...] = bm
    cm_ref[...] = (c[...].astype(F32) * first_doc).astype(BF16)
    for j, part in enumerate(parts):
        spread = expander(heads, head_dim, width, j)
        rows = dot_tn(r3, spread)[:PAD]
        rows_ref[:, part] = rows
        steps = dot_tn(s3, spread)
        leaves = dot_tn(f3, spread)
        large[j].wait()
        scaled = (steps * v[:, part].astype(F32)).astype(BF16).astype(F32)
        x = leaves * scaled
        hi = x.astype(BF16)
        lo = (x - hi.astype(F32)).astype(BF16)
        x_ref[:, part] = hi
        state = (dot(bm, hi) + dot(bm, lo)) * rows[1:2, :]
        put_half(j, keep_ref, send_ref, state, rows[2:3, :])


def inner_kernel(x_ref, v_ref, teach_ref, b_ref, c_ref, enter3_ref, rows_ref, ids_ref, base_ref, st_ref):
    length, total = x_ref.shape
    width = total // STEPS
    heads = enter3_ref.shape[0] // 3
    same = same_doc(ids_ref)
    down = iota((length, length), 0)
    along = iota((length, length), 1)
    s = jnp.where(same & (down >= along), dot_tn(c_ref[...], b_ref[...]), 0.0).astype(BF16)
    st_ref[...] = jnp.where(same & (down <= along), dot_tn(b_ref[...], c_ref[...]), 0.0).astype(BF16)
    for j in range(STEPS):
        part = slice(j * width, (j + 1) * width)
        enter = dot_tn(enter3_ref[...], expander(heads, total // heads, width, j))
        base_ref[:, part] = (
            enter * dot(s, x_ref[:, part])
            + rows_ref[3:4, part] * v_ref[:, part].astype(F32)
            - teach_ref[:, part].astype(F32)
        )


def mismatch_kernel(
    base_ref, enter3_ref, rows_ref, cm_ref, mine_ref, other_ref, mm_ref, y_ref, keep_ref, send_ref
):
    length, total = base_ref.shape
    width = total // STEPS
    heads = enter3_ref.shape[0] // 3
    n = cm_ref.shape[0]
    blank = jnp.zeros((PAD, keep_ref.shape[1]), F32)
    keep_ref[n:, :] = blank
    send_ref[n:, :] = blank
    cm = cm_ref[...]
    sums = jnp.zeros((1, width), F32)
    for j in range(STEPS):
        part = slice(j * width, (j + 1) * width)
        enter = dot_tn(enter3_ref[...], expander(heads, total // heads, width, j))
        state = split2(get_half(j, mine_ref, other_ref, width) * rows_ref[0:1, part])
        mm = base_ref[:, part] + enter * dot_tn(twice(cm), state)
        mm_ref[:, part] = mm
        y = (enter * mm).astype(BF16)
        y_ref[:, part] = y
        sums = sums + jnp.sum(mm * mm, axis=0, keepdims=True)
        put_half(j, keep_ref, send_ref, dot(cm, y) * rows_ref[0:1, part], rows_ref[2:3, part])
    keep_ref[n + 1 : n + 2, :width] = sums
    send_ref[n + 1 : n + 2, :width] = sums


def pair_kernel(
    mm_ref,
    y_ref,
    x_ref,
    st_ref,
    sf3_ref,
    rows_ref,
    b_ref,
    c_ref,
    ids_ref,
    mine_ref,
    other_ref,
    g_ref,
    gb_ref,
    gc_hbm,
    pair,
    gc,
    sem,
):
    length, total = mm_ref.shape
    width = total // STEPS
    heads = sf3_ref.shape[0] // 3
    n = b_ref.shape[0]
    acc = jnp.zeros((2 * n, length), F32)
    for j in range(STEPS):
        part = slice(j * width, (j + 1) * width)
        y = y_ref[:, part]
        sf = dot_tn(sf3_ref[...], expander(heads, total // heads, width, j))
        g_ref[:, part] = rows_ref[3:4, part] * mm_ref[:, part] + sf * dot(st_ref[...], y)
        state = get_half(j, mine_ref, other_ref, width) * rows_ref[0:1, part]
        acc = acc + dot_nt(split2(state), y)
    pair[...] = dot_nt(y_ref[...], x_ref[...])
    keep = same_doc(ids_ref) & (iota((length, length), 0) >= iota((length, length), 1))
    masked = jnp.where(keep, pair[...], 0.0)
    hi = masked.astype(BF16)
    lo = (masked - hi.astype(F32)).astype(BF16)
    through = (acc[:n] + acc[n:]) * ids_ref[1:2, :]
    gc[...] = dot_nt(b_ref[...], hi) + dot_nt(b_ref[...], lo) + through
    copy = pltpu.make_async_copy(gc, gc_hbm, sem)
    copy.start()
    gb_ref[...] = dot(c_ref[...], hi) + dot(c_ref[...], lo)
    copy.wait()


def finish_kernel(
    g_ref, x_ref, sf3_ref, rows_ref, bm_ref, ids_ref, gb_part_ref, mine_ref, other_ref, gv_hbm, gb_hbm, gv, gb, sems
):
    length, total = g_ref.shape
    width = total // STEPS
    heads = sf3_ref.shape[0] // 3
    n = bm_ref.shape[0]
    acc = jnp.zeros((length, 2 * n), F32)
    copies = []
    for j in range(STEPS):
        part = slice(j * width, (j + 1) * width)
        sf = dot_tn(sf3_ref[...], expander(heads, total // heads, width, j))
        adjoint = split2(get_half(j, mine_ref, other_ref, width) * rows_ref[1:2, part])
        gv[:, part] = g_ref[:, part] + sf * dot_tn(twice(bm_ref[...]), adjoint)
        copies.append(pltpu.make_async_copy(gv.at[:, part], gv_hbm.at[:, part], sems.at[j]))
        copies[j].start()
        acc = acc + dot_nt(x_ref[:, part], adjoint)
    through = (acc[:, :n] + acc[:, n:]).T
    gb[...] = gb_part_ref[...] + through * ids_ref[2:3, :]
    copies.append(pltpu.make_async_copy(gb, gb_hbm, sems.at[STEPS]))
    copies[STEPS].start()
    for copy in copies:
        copy.wait()


def call(kernel, ins, outs, flops=0, in_specs=None, out_specs=None, scratch=()):
    size = sum(a.size * a.dtype.itemsize for a in ins) + sum(o.size * o.dtype.itemsize for o in outs)
    return pl.pallas_call(
        kernel,
        out_shape=outs,
        in_specs=in_specs or [VMEM] * len(ins),
        out_specs=out_specs or [VMEM] * len(outs),
        scratch_shapes=scratch,
        compiler_params=pltpu.CompilerParams(vmem_limit_bytes=LIMIT),
        cost_estimate=pl.CostEstimate(flops=flops, bytes_accessed=size, transcendentals=0),
    )(*ins)


def out(*shape, dtype=F32):
    return jax.ShapeDtypeStruct(shape, dtype)


def swap(x, devices):
    return lax.ppermute(x, "seq", [(i, i ^ 1) for i in range(devices)])


def shift(x, by, devices):
    return lax.ppermute(
        x, "seq", [(i, i + by) for i in range(devices) if 0 <= i + by < devices]
    )


def turn(x, by, devices):
    return lax.ppermute(x, "seq", [(i, (i + by) % devices) for i in range(devices)])


def chip_order(way, mine_ref, got_ref):
    near = odd_core() == (0 if way == 1 else 1)
    near = near.astype(F32) > 0.5
    mine, got = mine_ref[...], got_ref[...]
    return near, jnp.where(near, mine, got), jnp.where(near, got, mine)


def compose_kernel(way, keep_ref, got_ref, packed_ref):
    rows = keep_ref.shape[0] - PAD
    _near, first, second = chip_order(way, keep_ref, got_ref)
    packed_ref[:rows] = second[:rows] + second[rows : rows + 1] * first[:rows]
    a, b = first[rows:], second[rows:]
    packed_ref[rows:] = jnp.where(iota(a.shape, 0) == 0, a * b, a + b)


def arrive_kernel(way, keep_ref, got_ref, packed_ref, one_ref, two_ref, mine_ref, theirs_ref, line2_ref, line3_ref):
    rows = mine_ref.shape[0]
    near, first, _second = chip_order(way, keep_ref, got_ref)
    state = one_ref[:rows] + one_ref[rows : rows + 1] * two_ref[:rows]
    inside = first[:rows] + first[rows : rows + 1] * state
    mine_ref[...] = jnp.where(near, state, inside)
    theirs_ref[...] = jnp.where(near, inside, state)
    line = slice(rows + 1, rows + 2)
    line2_ref[...] = packed_ref[line] + one_ref[line]
    line3_ref[...] = packed_ref[line] + one_ref[line] + two_ref[line]


def loss_kernel(scale, *refs):
    total = refs[0][...]
    for ref in refs[1:-1]:
        total = total + ref[...]
    refs[-1][...] = jnp.broadcast_to(jnp.sum(total) * scale, (1, 1))


def carry(keep, send, devices, way, beside):
    rows, width = keep.shape[0] - PAD, keep.shape[1]
    got = swap(send, devices)
    [packed] = call(functools.partial(compose_kernel, way), [keep, got], [out(rows + PAD, width)])
    reach = max(1, devices // 8)
    move = shift if way == 1 else turn
    one = move(packed, 2 * way, devices)
    two = move(packed, 4 * way, devices)
    if reach > 2:
        state = one[:rows] + one[rows : rows + 1] * two[:rows]
        run = one[rows : rows + 1] * two[rows : rows + 1]
        span = 2
        while span < reach:
            more = shift(jnp.concatenate([state, jnp.broadcast_to(run, (PAD, width))], axis=0), 2 * span * way, devices)
            state = state + run * more[:rows]
            run = run * more[rows : rows + 1]
            span *= 2
        one = jnp.concatenate([state, one[rows:]], axis=0)
        two = jnp.concatenate([jnp.zeros_like(state), two[rows:]], axis=0)
    mine, theirs, line2, line3 = call(
        functools.partial(arrive_kernel, way),
        [keep, got, packed, one, two],
        [out(rows, width), out(rows, width), out(1, width), out(1, width)],
    )
    theirs, beside = lax.optimization_barrier((theirs, beside))
    return mine, swap(theirs, devices), line2, line3, beside


def loss_lines(line2, line3, devices):
    chips = devices // 2
    if chips == 8:
        return [line3, turn(line3, -6, devices), turn(line2, -12, devices)]
    span = 2
    while span < chips:
        line2 = line2 + turn(line2, -2 * span, devices)
        span *= 2
    return [line2]


def local(values, b_proj, c_proj, step_sizes, decay_rates, skip_gain, teacher, doc_lengths):
    length, total = values.shape
    heads = step_sizes.shape[1]
    state = b_proj.shape[1]
    devices = lax.axis_size("seq")
    b = b_proj.T
    c = c_proj.T
    half = out(state + PAD, total // 2)
    thirds = out(3 * heads, length, dtype=BF16)
    narrow = out(state, length, dtype=BF16)
    square = 2 * length * length * total
    dma = pltpu.SemaphoreType.DMA
    x, keep, send, enter3, sf3, rows, bm, cm, ids = call(
        prepare_kernel,
        [
            pltpu.with_memory_space_constraint(a, pltpu.MemorySpace.HBM)
            for a in (
                doc_lengths,
                values,
                b,
                c,
                step_sizes.T,
                decay_rates.reshape(1, heads),
                skip_gain.reshape(1, heads),
            )
        ],
        [
            out(length, total, dtype=BF16),
            half,
            half,
            thirds,
            thirds,
            out(PAD, total),
            narrow,
            narrow,
            out(PAD, length),
        ],
        in_specs=[HBM] * 7,
        scratch=[
            pltpu.SMEM(doc_lengths.shape, jnp.int32),
            pltpu.VMEM((length, total), BF16),
            pltpu.VMEM((state, length), BF16),
            pltpu.VMEM((state, length), BF16),
            pltpu.VMEM((heads, length), F32),
            pltpu.VMEM((1, heads), F32),
            pltpu.VMEM((1, heads), F32),
            dma((6,)),
            dma((STEPS,)),
        ],
    )
    inner = call(
        inner_kernel,
        [x, values, teacher, b, c, enter3, rows, ids],
        [out(length, total), out(length, length, dtype=BF16)],
        square,
    )
    state_mine, state_other, _, _, (base, score_t) = carry(keep, send, devices, 1, inner)
    mm, y, back_keep, back_send = call(
        mismatch_kernel,
        [base, enter3, rows, cm, state_mine, state_other],
        [out(length, total), out(length, total, dtype=BF16), half, half],
    )
    pairs = call(
        pair_kernel,
        [mm, y, x, score_t, sf3, rows, b, c, ids, state_mine, state_other],
        [out(length, total), out(state, length), out(state, length)],
        2 * square,
        out_specs=[VMEM, VMEM, HBM],
        scratch=[pltpu.VMEM((length, length), F32), pltpu.VMEM((state, length), F32), dma],
    )
    adj_mine, adj_other, line2, line3, (g, gb_part, grad_c) = carry(back_keep, back_send, devices, -1, pairs)
    lines = loss_lines(line2, line3, devices)
    grad_values, grad_b = call(
        finish_kernel,
        [g, x, sf3, rows, bm, ids, gb_part, adj_mine, adj_other],
        [out(length, total), out(state, length)],
        out_specs=[HBM, HBM],
        scratch=[pltpu.VMEM((length, total), F32), pltpu.VMEM((state, length), F32), dma((STEPS + 1,))],
    )
    lines, grad_values = lax.optimization_barrier((lines, grad_values))
    scale = 1.0 / (devices * length * total)
    [loss] = call(functools.partial(loss_kernel, scale), lines, [out(1, 1)])
    return loss.reshape(1), grad_values, grad_b.T, grad_c.T


def solution(mesh):
    rows = P(("groups", "seq"), None)
    in_specs = (rows, rows, rows, rows, P(), P(), rows, P("groups"))
    out_specs = (P("groups"), rows, rows, rows)
    return jax.shard_map(local, mesh=mesh, in_specs=in_specs, out_specs=out_specs, check_vma=False)
```

```python
import functools
import jax
import jax.numpy as jnp
from jax import lax
from jax.experimental import pallas as pl
from jax.experimental.pallas import tpu as pltpu
from jax.sharding import PartitionSpec as P

F32 = jnp.float32
BF16 = jnp.bfloat16
PAD = 8
STEPS = 4
LIMIT = 24 << 20
HBM = pl.BlockSpec(memory_space=pltpu.MemorySpace.HBM)
VMEM = pl.BlockSpec(memory_space=pltpu.MemorySpace.VMEM)


def dot(a, b):
    return jnp.dot(a, b, preferred_element_type=F32)


def dot_nt(a, b):
    return lax.dot_general(a, b, (((1,), (1,)), ((), ())), preferred_element_type=F32)


def dot_tn(a, b):
    return lax.dot_general(a, b, (((0,), (0,)), ((), ())), preferred_element_type=F32)


def iota(shape, axis):
    return lax.broadcasted_iota(jnp.int32, shape, axis)


def split3(x):
    hi = x.astype(BF16)
    rest = x - hi.astype(F32)
    mid = rest.astype(BF16)
    lo = (rest - mid.astype(F32)).astype(BF16)
    return jnp.concatenate([hi, mid, lo], axis=0)


def split2(x):
    hi = x.astype(BF16)
    lo = (x - hi.astype(F32)).astype(BF16)
    return jnp.concatenate([hi, lo], axis=0)


def twice(x):
    return jnp.concatenate([x, x], axis=0)


def expander(heads, head_dim, width, chunk):
    rows = lax.rem(iota((3 * heads, width), 0), heads)
    cols = iota((3 * heads, width), 1) // head_dim + chunk * (width // head_dim)
    return (rows == cols).astype(F32).astype(BF16)


def column(row):
    n = row.shape[1]
    return jnp.sum(jnp.where(iota((n, n), 0) == iota((n, n), 1), row, 0.0), axis=1, keepdims=True)


def tall(row):
    return jnp.broadcast_to(row, (128, row.shape[1])).T


def same_doc(ids_ref):
    ids = ids_ref[0:1, :]
    return tall(ids)[:, 0:1] == ids


def odd_core():
    return lax.rem(lax.axis_index("seq"), 2)


def tiles(j, rows, width, ref):
    groups = ref.shape[0] // (rows // 8)
    inside = width // 128
    return [
        (r * groups + (j % (STEPS // 2)) * inside + q, r, q) for r in range(rows // 8) for q in range(inside)
    ]


def put_half(j, keep_ref, send_ref, state, decay):
    rows, width = state.shape
    groups = keep_ref.shape[0] // (rows // 8)
    last = groups * (rows // 8)
    mine = odd_core() == j // (STEPS // 2)

    def put(ref):
        for t, r, q in tiles(j, rows, width, ref):
            ref[t] = state[r * 8 : (r + 1) * 8, q * 128 : (q + 1) * 128]
            if r == 0:
                ref[last, t % groups : t % groups + 1, :] = decay[:, q * 128 : (q + 1) * 128]

    pl.when(mine)(lambda: put(keep_ref))
    pl.when(jnp.logical_not(mine))(lambda: put(send_ref))


def get_half(j, rows, mine_ref, other_ref, width):
    own = (odd_core() == j // (STEPS // 2)).astype(F32) > 0.5
    lines = [[] for _ in range(rows // 8)]
    for t, r, _q in tiles(j, rows, width, mine_ref):
        lines[r].append(jnp.where(own, mine_ref[t], other_ref[t]))
    return jnp.concatenate([jnp.concatenate(line, axis=1) for line in lines], axis=0)


def prepare_kernel(
    lengths_hbm,
    v_hbm,
    b_hbm,
    c_hbm,
    step_hbm,
    rate_hbm,
    gain_hbm,
    x_ref,
    keep_ref,
    send_ref,
    enter3_ref,
    sf3_ref,
    rows_ref,
    bm_ref,
    cm_ref,
    ids_ref,
    lengths,
    v,
    b,
    c,
    step,
    rate,
    gain,
    sems,
    v_sems,
):
    heads, length = step.shape
    total = v.shape[1]
    width = total // STEPS
    head_dim = total // heads
    small = [(step_hbm, step), (rate_hbm, rate), (gain_hbm, gain), (lengths_hbm, lengths), (b_hbm, b), (c_hbm, c)]
    small = [pltpu.make_async_copy(src, dst, sems.at[i]) for i, (src, dst) in enumerate(small)]
    parts = [slice(j * width, (j + 1) * width) for j in range(STEPS)]
    large = [pltpu.make_async_copy(v_hbm.at[:, p], v.at[:, p], v_sems.at[j]) for j, p in enumerate(parts)]
    for copy in small + large:
        copy.start()
    last_tile = keep_ref.shape[0] - 1
    keep_ref[last_tile] = jnp.zeros((8, 128), F32)
    send_ref[last_tile] = jnp.zeros((8, 128), F32)
    upper = (iota((length, length), 0) <= iota((length, length), 1)).astype(F32).astype(BF16)
    for copy in small:
        copy.wait()
    sums = dot(split3(-(step[...] * column(rate[...]))), upper)
    level = sums[:heads] + sums[heads : 2 * heads] + sums[2 * heads :]
    middle = level[:, length // 2 - 1 : length // 2]
    last = level[:, length - 1 : length]
    place = iota((1, length), 1)
    ids = jnp.zeros((1, length), jnp.int32)
    before = jnp.int32(0)
    final = jnp.int32(0)
    start = -lax.axis_index("seq") * length
    for d in range(lengths.shape[0]):
        ids = ids + (place >= start).astype(jnp.int32)
        before = before + (start <= -1).astype(jnp.int32)
        final = final + (start <= length - 1).astype(jnp.int32)
        start = start + lengths[d]
    first_doc = (ids == before).astype(F32)
    last_doc = (ids == final).astype(F32)
    ids_ref[0:1, :] = ids.astype(F32)
    ids_ref[1:2, :] = first_doc
    ids_ref[2:3, :] = last_doc
    leave = jnp.exp(middle - level)
    enter3_ref[...] = split3(jnp.exp(level - middle))
    f3 = split3(leave)
    s3 = split3(step[...])
    sf3_ref[...] = split3(step[...] * leave)
    through = jnp.where(before == final, jnp.exp(last), 0.0)
    pick = iota((heads, 128), 1)
    table = jnp.where(pick == 0, jnp.exp(middle), 0.0)
    table = jnp.where(pick == 1, jnp.exp(last - middle), table)
    table = jnp.where(pick == 2, through, table)
    table = jnp.where(pick == 3, column(gain[...]), table)
    r3 = split3(table)
    bm = (b[...].astype(F32) * last_doc).astype(BF16)
    bm_ref[...] = bm
    cm_ref[...] = (c[...].astype(F32) * first_doc).astype(BF16)
    for j, part in enumerate(parts):
        spread = expander(heads, head_dim, width, j)
        rows = dot_tn(r3, spread)[:PAD]
        rows_ref[:, part] = rows
        steps = dot_tn(s3, spread)
        leaves = dot_tn(f3, spread)
        large[j].wait()
        scaled = (steps * v[:, part].astype(F32)).astype(BF16).astype(F32)
        x = leaves * scaled
        hi = x.astype(BF16)
        lo = (x - hi.astype(F32)).astype(BF16)
        x_ref[:, part] = hi
        state = (dot(bm, hi) + dot(bm, lo)) * rows[1:2, :]
        put_half(j, keep_ref, send_ref, state, rows[2:3, :])


def inner_kernel(x_ref, v_ref, teach_ref, b_ref, c_ref, enter3_ref, rows_ref, ids_ref, base_ref, st_ref):
    length, total = x_ref.shape
    width = total // STEPS
    heads = enter3_ref.shape[0] // 3
    same = same_doc(ids_ref)
    down = iota((length, length), 0)
    along = iota((length, length), 1)
    s = jnp.where(same & (down >= along), dot_tn(c_ref[...], b_ref[...]), 0.0).astype(BF16)
    st_ref[...] = jnp.where(same & (down <= along), dot_tn(b_ref[...], c_ref[...]), 0.0).astype(BF16)
    for j in range(STEPS):
        part = slice(j * width, (j + 1) * width)
        enter = dot_tn(enter3_ref[...], expander(heads, total // heads, width, j))
        base_ref[:, part] = (
            enter * dot(s, x_ref[:, part])
            + rows_ref[3:4, part] * v_ref[:, part].astype(F32)
            - teach_ref[:, part].astype(F32)
        )


def mismatch_kernel(base_ref, enter3_ref, rows_ref, cm_ref, mine_ref, other_ref, mm_ref, y_ref, keep_ref, send_ref):
    length, total = base_ref.shape
    width = total // STEPS
    heads = enter3_ref.shape[0] // 3
    cm = cm_ref[...]
    sums = jnp.zeros((8, width), F32)
    for j in range(STEPS):
        part = slice(j * width, (j + 1) * width)
        enter = dot_tn(enter3_ref[...], expander(heads, total // heads, width, j))
        state = split2(get_half(j, cm.shape[0], mine_ref, other_ref, width) * rows_ref[0:1, part])
        mm = base_ref[:, part] + enter * dot_tn(twice(cm), state)
        mm_ref[:, part] = mm
        y = (enter * mm).astype(BF16)
        y_ref[:, part] = y
        sums = sums + jnp.sum((mm * mm).reshape(length // 8, 8, width), axis=0)
        put_half(j, keep_ref, send_ref, dot(cm, y) * rows_ref[0:1, part], rows_ref[2:3, part])
    line = sums[:, :128]
    for q in range(1, width // 128):
        line = line + sums[:, q * 128 : (q + 1) * 128]
    last_tile = keep_ref.shape[0] - 1
    keep_ref[last_tile] = line
    send_ref[last_tile] = line


def pair_kernel(
    mm_ref,
    y_ref,
    x_ref,
    st_ref,
    sf3_ref,
    rows_ref,
    b_ref,
    c_ref,
    ids_ref,
    mine_ref,
    other_ref,
    g_ref,
    gb_ref,
    gc_hbm,
    pair,
    gc,
    sem,
):
    length, total = mm_ref.shape
    width = total // STEPS
    heads = sf3_ref.shape[0] // 3
    n = b_ref.shape[0]
    acc = jnp.zeros((2 * n, length), F32)
    for j in range(STEPS):
        part = slice(j * width, (j + 1) * width)
        y = y_ref[:, part]
        sf = dot_tn(sf3_ref[...], expander(heads, total // heads, width, j))
        g_ref[:, part] = rows_ref[3:4, part] * mm_ref[:, part] + sf * dot(st_ref[...], y)
        state = get_half(j, n, mine_ref, other_ref, width) * rows_ref[0:1, part]
        acc = acc + dot_nt(split2(state), y)
    pair[...] = dot_nt(y_ref[...], x_ref[...])
    keep = same_doc(ids_ref) & (iota((length, length), 0) >= iota((length, length), 1))
    masked = jnp.where(keep, pair[...], 0.0)
    hi = masked.astype(BF16)
    lo = (masked - hi.astype(F32)).astype(BF16)
    through = (acc[:n] + acc[n:]) * ids_ref[1:2, :]
    gc[...] = dot_nt(b_ref[...], hi) + dot_nt(b_ref[...], lo) + through
    copy = pltpu.make_async_copy(gc, gc_hbm, sem)
    copy.start()
    gb_ref[...] = dot(c_ref[...], hi) + dot(c_ref[...], lo)
    copy.wait()


def finish_kernel(
    scale,
    g_ref,
    x_ref,
    sf3_ref,
    rows_ref,
    bm_ref,
    ids_ref,
    gb_part_ref,
    mine_ref,
    other_ref,
    gv_hbm,
    gb_hbm,
    loss_ref,
    gv,
    gb,
    sems,
):
    length, total = g_ref.shape
    width = total // STEPS
    heads = sf3_ref.shape[0] // 3
    n = bm_ref.shape[0]
    acc = jnp.zeros((length, 2 * n), F32)
    copies = []
    for j in range(STEPS):
        part = slice(j * width, (j + 1) * width)
        sf = dot_tn(sf3_ref[...], expander(heads, total // heads, width, j))
        adjoint = split2(get_half(j, n, mine_ref, other_ref, width) * rows_ref[1:2, part])
        gv[:, part] = g_ref[:, part] + sf * dot_tn(twice(bm_ref[...]), adjoint)
        copies.append(pltpu.make_async_copy(gv.at[:, part], gv_hbm.at[:, part], sems.at[j]))
        copies[j].start()
        acc = acc + dot_nt(x_ref[:, part], adjoint)
    last_tile = mine_ref.shape[0] - 1
    loss_ref[...] = jnp.broadcast_to(jnp.sum(mine_ref[last_tile] + other_ref[last_tile]) * scale, (1, 1))
    through = (acc[:, :n] + acc[:, n:]).T
    gb[...] = gb_part_ref[...] + through * ids_ref[2:3, :]
    copies.append(pltpu.make_async_copy(gb, gb_hbm, sems.at[STEPS]))
    copies[STEPS].start()
    for copy in copies:
        copy.wait()


def call(kernel, ins, outs, flops=0, in_specs=None, out_specs=None, scratch=()):
    size = sum(a.size * a.dtype.itemsize for a in ins) + sum(o.size * o.dtype.itemsize for o in outs)
    return pl.pallas_call(
        kernel,
        out_shape=outs,
        in_specs=in_specs or [VMEM] * len(ins),
        out_specs=out_specs or [VMEM] * len(outs),
        scratch_shapes=scratch,
        compiler_params=pltpu.CompilerParams(vmem_limit_bytes=LIMIT),
        cost_estimate=pl.CostEstimate(flops=flops, bytes_accessed=size, transcendentals=0),
    )(*ins)


def out(*shape, dtype=F32):
    return jax.ShapeDtypeStruct(shape, dtype)


def swap(x, devices):
    return lax.ppermute(x, "seq", [(i, i ^ 1) for i in range(devices)])


def shift(x, by, devices):
    return lax.ppermute(
        x, "seq", [(i, i + by) for i in range(devices) if 0 <= i + by < devices]
    )


def turn(x, by, devices):
    return lax.ppermute(x, "seq", [(i, (i + by) % devices) for i in range(devices)])


def in_order(way, keep_ref, got_ref, body):
    near = odd_core() == (0 if way == 1 else 1)
    pl.when(near)(lambda: body(keep_ref, got_ref, True))
    pl.when(jnp.logical_not(near))(lambda: body(got_ref, keep_ref, False))


def columns(groups, count):
    return [(q, range(q, count, groups)) for q in range(groups)]


def compose_kernel(way, groups, keep_ref, got_ref, packed_ref, both_ref, line_ref):
    count = both_ref.shape[0] - 1

    def body(first_ref, second_ref, _near):
        packed_ref[count] = first_ref[count] * second_ref[count]
        for q, places in columns(groups, count):
            decay = second_ref[count, q : q + 1, :]
            for t in places:
                both = second_ref[t] + decay * first_ref[t]
                packed_ref[t] = both
                both_ref[t] = both

    in_order(way, keep_ref, got_ref, body)
    line = keep_ref[count + 1] + got_ref[count + 1]
    packed_ref[count + 1] = line
    both_ref[count] = line
    line_ref[...] = line


def arrive_kernel(way, groups, near_chips, keep_ref, got_ref, line_ref, one_ref, two_ref, *refs):
    more_refs, mine_ref, theirs_ref = refs[:-2], refs[-2], refs[-1]
    count = mine_ref.shape[0] - 1

    def body(first_ref, _second_ref, near):
        outer_ref, inner_ref = (mine_ref, theirs_ref) if near else (theirs_ref, mine_ref)
        for q, places in columns(groups, count):
            far_decay = one_ref[count, q : q + 1, :]
            decay = first_ref[count, q : q + 1, :]
            for t in places:
                state = one_ref[t] + far_decay * two_ref[t]
                outer_ref[t] = state
                inner_ref[t] = first_ref[t] + decay * state

    in_order(way, keep_ref, got_ref, body)
    line = jnp.zeros((8, 128), F32)
    if near_chips:
        line = line_ref[...] + one_ref[count + 1] + two_ref[count]
        line = jnp.where((odd_core() == 0).astype(F32) > 0.5, line, 0.0)
    for ref in more_refs:
        line = line + ref[...]
    mine_ref[count] = line
    theirs_ref[count] = line


def far_squares(line, devices):
    chips = devices // 2
    if chips != 8:
        return [lax.psum(line, "seq") * 0.25], False
    lines = []
    for far in range(3, chips, 2):
        pairs = [(i, (i - 2 * (far + i % 2)) % devices) for i in range(devices) if far + i % 2 < chips]
        lines.append(lax.ppermute(line, "seq", pairs))
    return lines, True


def carry(keep, send, groups, devices, way, beside):
    count = keep.shape[0] - 2
    got = swap(send, devices)
    packed, both, line = call(
        functools.partial(compose_kernel, way, groups),
        [keep, got],
        [out(*keep.shape), out(count + 1, 8, 128), out(8, 128)],
    )
    reach = max(1, devices // 8)
    move = shift if way == 1 else turn
    one = move(packed, 2 * way, devices)
    two = move(packed if reach > 2 else both, 4 * way, devices)
    lines, near_chips = far_squares(line, devices) if way == -1 else ([], False)
    if reach > 2:

        def join(near, far):
            decay = near[count, :groups]
            state = near[:count].reshape(-1, groups, 8, 128) + decay[:, None, :] * far[:count].reshape(-1, groups, 8, 128)
            return jnp.concatenate([state.reshape(count, 8, 128), (near[count:] * far[count:])], axis=0)

        one = join(one, two)
        span = 2
        while span < reach:
            one = join(one, shift(one, 2 * span * way, devices))
            span *= 2
        two = jnp.zeros_like(both)
    mine, theirs = call(
        functools.partial(arrive_kernel, way, groups, near_chips),
        [keep, got, line, one, two, *lines],
        [out(count + 1, 8, 128), out(count + 1, 8, 128)],
    )
    theirs, beside = lax.optimization_barrier((theirs, beside))
    return mine, swap(theirs, devices), beside


def local(values, b_proj, c_proj, step_sizes, decay_rates, skip_gain, teacher, doc_lengths):
    length, total = values.shape
    heads = step_sizes.shape[1]
    state = b_proj.shape[1]
    devices = lax.axis_size("seq")
    b = b_proj.T
    c = c_proj.T
    groups = total // 2 // 128
    half = out(state // 8 * groups + 2, 8, 128)
    thirds = out(3 * heads, length, dtype=BF16)
    narrow = out(state, length, dtype=BF16)
    square = 2 * length * length * total
    dma = pltpu.SemaphoreType.DMA
    x, keep, send, enter3, sf3, rows, bm, cm, ids = call(
        prepare_kernel,
        [
            pltpu.with_memory_space_constraint(a, pltpu.MemorySpace.HBM)
            for a in (
                doc_lengths,
                values,
                b,
                c,
                step_sizes.T,
                decay_rates.reshape(1, heads),
                skip_gain.reshape(1, heads),
            )
        ],
        [
            out(length, total, dtype=BF16),
            half,
            half,
            thirds,
            thirds,
            out(PAD, total),
            narrow,
            narrow,
            out(PAD, length),
        ],
        in_specs=[HBM] * 7,
        scratch=[
            pltpu.SMEM(doc_lengths.shape, jnp.int32),
            pltpu.VMEM((length, total), BF16),
            pltpu.VMEM((state, length), BF16),
            pltpu.VMEM((state, length), BF16),
            pltpu.VMEM((heads, length), F32),
            pltpu.VMEM((1, heads), F32),
            pltpu.VMEM((1, heads), F32),
            dma((6,)),
            dma((STEPS,)),
        ],
    )
    inner = call(
        inner_kernel,
        [x, values, teacher, b, c, enter3, rows, ids],
        [out(length, total), out(length, length, dtype=BF16)],
        square,
    )
    state_mine, state_other, (base, score_t) = carry(keep, send, groups, devices, 1, inner)
    mm, y, back_keep, back_send = call(
        mismatch_kernel,
        [base, enter3, rows, cm, state_mine, state_other],
        [out(length, total), out(length, total, dtype=BF16), half, half],
    )
    pairs = call(
        pair_kernel,
        [mm, y, x, score_t, sf3, rows, b, c, ids, state_mine, state_other],
        [out(length, total), out(state, length), out(state, length)],
        2 * square,
        out_specs=[VMEM, VMEM, HBM],
        scratch=[pltpu.VMEM((length, length), F32), pltpu.VMEM((state, length), F32), dma],
    )
    adj_mine, adj_other, (g, gb_part, grad_c) = carry(back_keep, back_send, groups, devices, -1, pairs)
    scale = 1.0 / (devices * length * total)
    grad_values, grad_b, loss = call(
        functools.partial(finish_kernel, scale),
        [g, x, sf3, rows, bm, ids, gb_part, adj_mine, adj_other],
        [out(length, total), out(state, length), out(1, 1)],
        out_specs=[HBM, HBM, VMEM],
        scratch=[pltpu.VMEM((length, total), F32), pltpu.VMEM((state, length), F32), dma((STEPS + 1,))],
    )
    return loss.reshape(1), grad_values, grad_b.T, grad_c.T


def solution(mesh):
    rows = P(("groups", "seq"), None)
    in_specs = (rows, rows, rows, rows, P(), P(), rows, P("groups"))
    out_specs = (P("groups"), rows, rows, rows)
    return jax.shard_map(local, mesh=mesh, in_specs=in_specs, out_specs=out_specs, check_vma=False)
```

```python
import functools
import jax
import jax.numpy as jnp
from jax import lax
from jax.experimental import pallas as pl
from jax.experimental.pallas import tpu as pltpu
from jax.sharding import PartitionSpec as P

F32 = jnp.float32
BF16 = jnp.bfloat16
PAD = 8
STEPS = 4
LIMIT = 24 << 20
HBM = pl.BlockSpec(memory_space=pltpu.MemorySpace.HBM)
VMEM = pl.BlockSpec(memory_space=pltpu.MemorySpace.VMEM)


def dot(a, b):
    return jnp.dot(a, b, preferred_element_type=F32)


def dot_nt(a, b):
    return lax.dot_general(a, b, (((1,), (1,)), ((), ())), preferred_element_type=F32)


def dot_tn(a, b):
    return lax.dot_general(a, b, (((0,), (0,)), ((), ())), preferred_element_type=F32)


def iota(shape, axis):
    return lax.broadcasted_iota(jnp.int32, shape, axis)


def split3(x):
    hi = x.astype(BF16)
    rest = x - hi.astype(F32)
    mid = rest.astype(BF16)
    lo = (rest - mid.astype(F32)).astype(BF16)
    return jnp.concatenate([hi, mid, lo], axis=0)


def split2(x):
    hi = x.astype(BF16)
    lo = (x - hi.astype(F32)).astype(BF16)
    return jnp.concatenate([hi, lo], axis=0)


def twice(x):
    return jnp.concatenate([x, x], axis=0)


def chunk_of(j):
    half = STEPS // 2
    return jnp.where(odd_core() == 0, (j + half) % STEPS, j)


def span_of(j, width):
    return pl.ds(pl.multiple_of(chunk_of(j) * width, width), width)


def expander(heads, head_dim, width, j):
    rows = lax.rem(iota((3 * heads, width), 0), heads)
    cols = iota((3 * heads, width), 1) // head_dim + chunk_of(j) * (width // head_dim)
    return (rows == cols).astype(F32).astype(BF16)


def column(row):
    n = row.shape[1]
    return jnp.sum(jnp.where(iota((n, n), 0) == iota((n, n), 1), row, 0.0), axis=1, keepdims=True)


def tall(row):
    return jnp.broadcast_to(row, (128, row.shape[1])).T


def same_doc(ids_ref):
    ids = ids_ref[0:1, :]
    return tall(ids)[:, 0:1] == ids


def odd_core():
    return lax.rem(lax.axis_index("seq"), 2)


def put_half(a, ref, state, decay):
    rows, width = state.shape
    groups = ref.shape[0] // (rows // 8)
    for q in range(width // 128):
        g = a * (width // 128) + q
        cols = slice(q * 128, (q + 1) * 128)
        for r in range(rows // 8):
            ref[r * groups + g] = state[r * 8 : (r + 1) * 8, cols]
        ref[groups * (rows // 8), g : g + 1, :] = decay[:, cols]


def get_half(a, rows, ref, width):
    groups = ref.shape[0] // (rows // 8)
    inside = range(a * (width // 128), (a + 1) * (width // 128))
    return jnp.concatenate(
        [jnp.concatenate([ref[r * groups + g] for g in inside], axis=1) for r in range(rows // 8)], axis=0
    )


def state_half(first, f3, s3, bm, rows_ref, v_ref, x_ref, message_ref, heads):
    total = v_ref.shape[1]
    width = total // STEPS
    for a in range(STEPS // 2):
        j = first + a
        rel = slice(j * width, (j + 1) * width)
        spread = expander(heads, total // heads, width, j)
        scaled = (dot_tn(s3, spread) * v_ref[:, rel].astype(F32)).astype(BF16).astype(F32)
        x = dot_tn(f3, spread) * scaled
        hi = x.astype(BF16)
        lo = (x - hi.astype(F32)).astype(BF16)
        x_ref[:, a * width : (a + 1) * width] = hi
        state = (dot(bm, hi) + dot(bm, lo)) * rows_ref[1:2, rel]
        put_half(a, message_ref, state, rows_ref[2:3, rel])
    message_ref[message_ref.shape[0] - 1] = jnp.zeros((8, 128), F32)


def prepare_kernel(
    lengths_hbm,
    v_hbm,
    teach_hbm,
    b_hbm,
    c_hbm,
    step_hbm,
    rate_hbm,
    gain_hbm,
    x_ref,
    send_ref,
    enter3_ref,
    sf3_ref,
    f3_ref,
    s3_ref,
    rows_ref,
    bm_ref,
    cm_ref,
    ids_ref,
    v,
    teach,
    b,
    c,
    lengths,
    step,
    rate,
    gain,
    sems,
    v_sems,
    t_sems,
):
    heads, length = step.shape
    total = v.shape[1]
    width = total // STEPS
    small = [(step_hbm, step), (rate_hbm, rate), (gain_hbm, gain), (lengths_hbm, lengths), (b_hbm, b), (c_hbm, c)]
    small = [pltpu.make_async_copy(src, dst, sems.at[i]) for i, (src, dst) in enumerate(small)]
    large = []
    for src, dst, sem in ((v_hbm, v, v_sems), (teach_hbm, teach, t_sems)):
        for j in range(STEPS):
            rel = slice(j * width, (j + 1) * width)
            large.append(pltpu.make_async_copy(src.at[:, span_of(j, width)], dst.at[:, rel], sem.at[j]))
    for copy in small + large:
        copy.start()
    upper = (iota((length, length), 0) <= iota((length, length), 1)).astype(F32).astype(BF16)
    for copy in small:
        copy.wait()
    sums = dot(split3(-(step[...] * column(rate[...]))), upper)
    level = sums[:heads] + sums[heads : 2 * heads] + sums[2 * heads :]
    middle = level[:, length // 2 - 1 : length // 2]
    last = level[:, length - 1 : length]
    place = iota((1, length), 1)
    ids = jnp.zeros((1, length), jnp.int32)
    before = jnp.int32(0)
    final = jnp.int32(0)
    start = -lax.axis_index("seq") * length
    for d in range(lengths.shape[0]):
        ids = ids + (place >= start).astype(jnp.int32)
        before = before + (start <= -1).astype(jnp.int32)
        final = final + (start <= length - 1).astype(jnp.int32)
        start = start + lengths[d]
    first_doc = (ids == before).astype(F32)
    last_doc = (ids == final).astype(F32)
    ids_ref[0:1, :] = ids.astype(F32)
    ids_ref[1:2, :] = first_doc
    ids_ref[2:3, :] = last_doc
    leave = jnp.exp(middle - level)
    enter3_ref[...] = split3(jnp.exp(level - middle))
    f3 = split3(leave)
    s3 = split3(step[...])
    f3_ref[...] = f3
    s3_ref[...] = s3
    sf3_ref[...] = split3(step[...] * leave)
    through = jnp.where(before == final, jnp.exp(last), 0.0)
    pick = iota((heads, 128), 1)
    table = jnp.where(pick == 0, jnp.exp(middle), 0.0)
    table = jnp.where(pick == 1, jnp.exp(last - middle), table)
    table = jnp.where(pick == 2, through, table)
    table = jnp.where(pick == 3, column(gain[...]), table)
    r3 = split3(table)
    for j in range(STEPS):
        spread = expander(heads, total // heads, width, j)
        rows_ref[:, j * width : (j + 1) * width] = dot_tn(r3, spread)[:PAD]
    bm = (b[...].astype(F32) * last_doc).astype(BF16)
    bm_ref[...] = bm
    cm_ref[...] = (c[...].astype(F32) * first_doc).astype(BF16)
    for copy in large[: STEPS // 2]:
        copy.wait()
    state_half(0, f3, s3, bm, rows_ref, v, x_ref, send_ref, heads)
    for copy in large[STEPS // 2 :]:
        copy.wait()


def prepare_own_kernel(f3_ref, s3_ref, bm_ref, rows_ref, v_ref, x_ref, keep_ref):
    state_half(
        STEPS // 2, f3_ref[...], s3_ref[...], bm_ref[...], rows_ref, v_ref, x_ref, keep_ref, f3_ref.shape[0] // 3
    )


def inner_kernel(xf_ref, xo_ref, v_ref, teach_ref, b_ref, c_ref, enter3_ref, rows_ref, ids_ref, base_ref, st_ref):
    length, total = base_ref.shape
    width = total // STEPS
    heads = enter3_ref.shape[0] // 3
    same = same_doc(ids_ref)
    down = iota((length, length), 0)
    along = iota((length, length), 1)
    s = jnp.where(same & (down >= along), dot_tn(c_ref[...], b_ref[...]), 0.0).astype(BF16)
    st_ref[...] = jnp.where(same & (down <= along), dot_tn(b_ref[...], c_ref[...]), 0.0).astype(BF16)
    for j in range(STEPS):
        rel = slice(j * width, (j + 1) * width)
        a = j % (STEPS // 2)
        x_ref = xf_ref if j < STEPS // 2 else xo_ref
        enter = dot_tn(enter3_ref[...], expander(heads, total // heads, width, j))
        base_ref[:, rel] = (
            enter * dot(s, x_ref[:, a * width : (a + 1) * width])
            + rows_ref[3:4, rel] * v_ref[:, rel].astype(F32)
            - teach_ref[:, rel].astype(F32)
        )


def mismatch_kernel(first, base_ref, enter3_ref, rows_ref, cm_ref, state_ref, *refs):
    more, (mm_ref, y_ref, message_ref) = refs[:-3], refs[-3:]
    length, total = base_ref.shape
    width = total // STEPS
    heads = enter3_ref.shape[0] // 3
    cm = cm_ref[...]
    sums = jnp.zeros((8, width), F32)
    for a in range(STEPS // 2):
        j = first + a
        rel = slice(j * width, (j + 1) * width)
        part = slice(a * width, (a + 1) * width)
        enter = dot_tn(enter3_ref[...], expander(heads, total // heads, width, j))
        state = split2(get_half(a, cm.shape[0], state_ref, width) * rows_ref[0:1, rel])
        mm = base_ref[:, rel] + enter * dot_tn(twice(cm), state)
        mm_ref[:, part] = mm
        y = (enter * mm).astype(BF16)
        y_ref[:, part] = y
        sums = sums + jnp.sum((mm * mm).reshape(length // 8, 8, width), axis=0)
        put_half(a, message_ref, dot(cm, y) * rows_ref[0:1, rel], rows_ref[2:3, rel])
    line = sums[:, :128]
    for q in range(1, width // 128):
        line = line + sums[:, q * 128 : (q + 1) * 128]
    for ref in more:
        line = line + ref[ref.shape[0] - 1]
    message_ref[message_ref.shape[0] - 1] = line


def pair_kernel(
    mmf_ref,
    mmo_ref,
    yf_ref,
    yo_ref,
    xf_ref,
    xo_ref,
    st_ref,
    sf3_ref,
    rows_ref,
    b_ref,
    c_ref,
    ids_ref,
    other_ref,
    mine_ref,
    gf_ref,
    go_ref,
    gb_ref,
    gc_hbm,
    pair,
    gc,
    sem,
):
    length, half = mmf_ref.shape
    width = 2 * half // STEPS
    heads = sf3_ref.shape[0] // 3
    n = b_ref.shape[0]
    acc = jnp.zeros((2 * n, length), F32)
    for j in range(STEPS):
        a = j % (STEPS // 2)
        rel = slice(j * width, (j + 1) * width)
        part = slice(a * width, (a + 1) * width)
        far = j < STEPS // 2
        mm_ref, y_ref, state_ref, g_ref = (
            (mmf_ref, yf_ref, other_ref, gf_ref) if far else (mmo_ref, yo_ref, mine_ref, go_ref)
        )
        y = y_ref[:, part]
        sf = dot_tn(sf3_ref[...], expander(heads, 2 * half // heads, width, j))
        g_ref[:, part] = rows_ref[3:4, rel] * mm_ref[:, part] + sf * dot(st_ref[...], y)
        acc = acc + dot_nt(split2(get_half(a, n, state_ref, width) * rows_ref[0:1, rel]), y)
    pair[...] = dot_nt(yf_ref[...], xf_ref[...])
    pair[...] += dot_nt(yo_ref[...], xo_ref[...])
    keep = same_doc(ids_ref) & (iota((length, length), 0) >= iota((length, length), 1))
    masked = jnp.where(keep, pair[...], 0.0)
    hi = masked.astype(BF16)
    lo = (masked - hi.astype(F32)).astype(BF16)
    through = (acc[:n] + acc[n:]) * ids_ref[1:2, :]
    gc[...] = dot_nt(b_ref[...], hi) + dot_nt(b_ref[...], lo) + through
    copy = pltpu.make_async_copy(gc, gc_hbm, sem)
    copy.start()
    gb_ref[...] = dot(c_ref[...], hi) + dot(c_ref[...], lo)
    copy.wait()


def finish_half(first, g_ref, x_ref, sf3_ref, rows_ref, bm_ref, state_ref, gv_hbm, gv, sems):
    half = g_ref.shape[1]
    width = 2 * half // STEPS
    heads = sf3_ref.shape[0] // 3
    bm2 = twice(bm_ref[...])
    copies = []
    acc = jnp.zeros((g_ref.shape[0], bm2.shape[0]), F32)
    for a in range(STEPS // 2):
        j = first + a
        rel = slice(j * width, (j + 1) * width)
        part = slice(a * width, (a + 1) * width)
        sf = dot_tn(sf3_ref[...], expander(heads, 2 * half // heads, width, j))
        adjoint = split2(get_half(a, bm_ref.shape[0], state_ref, width) * rows_ref[1:2, rel])
        gv[:, part] = g_ref[:, part] + sf * dot_tn(bm2, adjoint)
        copies.append(pltpu.make_async_copy(gv.at[:, part], gv_hbm.at[:, span_of(j, width)], sems.at[a]))
        copies[a].start()
        acc = acc + dot_nt(x_ref[:, part], adjoint)
    return acc, copies


def finish_own_kernel(g_ref, x_ref, sf3_ref, rows_ref, bm_ref, mine_ref, gv_hbm, acc_ref, gv, sems):
    acc, copies = finish_half(STEPS // 2, g_ref, x_ref, sf3_ref, rows_ref, bm_ref, mine_ref, gv_hbm, gv, sems)
    acc_ref[...] = acc
    for copy in copies:
        copy.wait()


def finish_kernel(
    scale,
    _gv_in,
    g_ref,
    x_ref,
    sf3_ref,
    rows_ref,
    bm_ref,
    ids_ref,
    gb_part_ref,
    acc_ref,
    mine_ref,
    other_ref,
    gv_hbm,
    gb_hbm,
    loss_hbm,
    gv,
    gb,
    loss,
    sems,
):
    n = bm_ref.shape[0]
    last = mine_ref.shape[0] - 1
    loss[...] = jnp.broadcast_to(jnp.sum(mine_ref[last] + other_ref[last]) * scale, (1, 128))
    half = STEPS // 2
    out_loss = pltpu.make_async_copy(loss, loss_hbm, sems.at[half])
    out_loss.start()
    acc, copies = finish_half(0, g_ref, x_ref, sf3_ref, rows_ref, bm_ref, other_ref, gv_hbm, gv, sems)
    acc = acc + acc_ref[...]
    gb[...] = gb_part_ref[...] + (acc[:, :n] + acc[:, n:]).T * ids_ref[2:3, :]
    out_gb = pltpu.make_async_copy(gb, gb_hbm, sems.at[half + 1])
    out_gb.start()
    for copy in (*copies, out_loss, out_gb):
        copy.wait()


def call(kernel, ins, outs, flops=0, in_specs=None, out_specs=None, scratch=(), aliases=None):
    size = sum(a.size * a.dtype.itemsize for a in ins) + sum(o.size * o.dtype.itemsize for o in outs)
    return pl.pallas_call(
        kernel,
        out_shape=outs,
        in_specs=in_specs or [VMEM] * len(ins),
        out_specs=out_specs or [VMEM] * len(outs),
        scratch_shapes=scratch,
        input_output_aliases=aliases or {},
        compiler_params=pltpu.CompilerParams(vmem_limit_bytes=LIMIT),
        cost_estimate=pl.CostEstimate(flops=flops, bytes_accessed=size, transcendentals=0),
    )(*ins)


def out(*shape, dtype=F32):
    return jax.ShapeDtypeStruct(shape, dtype)


def swap(x, devices):
    return lax.ppermute(x, "seq", [(i, i ^ 1) for i in range(devices)])


def shift(x, by, devices):
    return lax.ppermute(
        x, "seq", [(i, i + by) for i in range(devices) if 0 <= i + by < devices]
    )


def turn(x, by, devices):
    return lax.ppermute(x, "seq", [(i, (i + by) % devices) for i in range(devices)])


def in_order(way, keep_ref, got_ref, body):
    near = odd_core() == (0 if way == 1 else 1)
    pl.when(near)(lambda: body(keep_ref, got_ref, True))
    pl.when(jnp.logical_not(near))(lambda: body(got_ref, keep_ref, False))


def columns(groups, count):
    return [(q, range(q, count, groups)) for q in range(groups)]


def compose_kernel(way, groups, keep_ref, send_ref, got_ref, packed_ref, both_ref, line_ref):
    count = both_ref.shape[0] - 1

    def body(first_ref, second_ref, _near):
        packed_ref[count] = first_ref[count] * second_ref[count]
        for q, places in columns(groups, count):
            decay = second_ref[count, q : q + 1, :]
            for t in places:
                both = second_ref[t] + decay * first_ref[t]
                packed_ref[t] = both
                both_ref[t] = both

    in_order(way, keep_ref, got_ref, body)
    line = send_ref[count + 1] + got_ref[count + 1]
    packed_ref[count + 1] = line
    both_ref[count] = line
    line_ref[...] = line


def arrive_kernel(way, groups, near_chips, keep_ref, got_ref, line_ref, one_ref, two_ref, *refs):
    more_refs, mine_ref, theirs_ref = refs[:-2], refs[-2], refs[-1]
    count = mine_ref.shape[0] - 1

    def body(first_ref, _second_ref, near):
        outer_ref, inner_ref = (mine_ref, theirs_ref) if near else (theirs_ref, mine_ref)
        for q, places in columns(groups, count):
            far_decay = one_ref[count, q : q + 1, :]
            decay = first_ref[count, q : q + 1, :]
            for t in places:
                state = one_ref[t] + far_decay * two_ref[t]
                outer_ref[t] = state
                inner_ref[t] = first_ref[t] + decay * state

    in_order(way, keep_ref, got_ref, body)
    line = jnp.zeros((8, 128), F32)
    if near_chips:
        line = line_ref[...] + one_ref[count + 1] + two_ref[count]
        line = jnp.where((odd_core() == 0).astype(F32) > 0.5, line, 0.0)
    for ref in more_refs:
        line = line + ref[...]
    mine_ref[count] = line
    theirs_ref[count] = line


def far_squares(line, devices):
    chips = devices // 2
    if chips != 8:
        return [lax.psum(line, "seq") * 0.25], False
    lines = []
    for far in range(3, chips, 2):
        pairs = [(i, (i - 2 * (far + i % 2)) % devices) for i in range(devices) if far + i % 2 < chips]
        lines.append(lax.ppermute(line, "seq", pairs))
    return lines, True


def carry(keep, send, groups, devices, way, beside):
    count = keep.shape[0] - 2
    got = swap(send, devices)
    packed, both, line = call(
        functools.partial(compose_kernel, way, groups),
        [keep, send, got],
        [out(*keep.shape), out(count + 1, 8, 128), out(8, 128)],
    )
    reach = max(1, devices // 8)
    move = shift if way == 1 else turn
    one = move(packed, 2 * way, devices)
    two = move(packed if reach > 2 else both, 4 * way, devices)
    lines, near_chips = [], False
    if way == -1:
        lines, near_chips = far_squares(line, devices)
    if reach > 2:

        def join(near, far):
            decay = near[count, :groups]
            state = near[:count].reshape(-1, groups, 8, 128) + decay[:, None, :] * far[:count].reshape(-1, groups, 8, 128)
            return jnp.concatenate([state.reshape(count, 8, 128), (near[count:] * far[count:])], axis=0)

        one = join(one, two)
        span = 2
        while span < reach:
            one = join(one, shift(one, 2 * span * way, devices))
            span *= 2
        two = jnp.zeros_like(both)
    mine, theirs = call(
        functools.partial(arrive_kernel, way, groups, near_chips),
        [keep, got, line, one, two, *lines],
        [out(count + 1, 8, 128), out(count + 1, 8, 128)],
    )
    theirs, beside = lax.optimization_barrier((theirs, beside))
    return mine, swap(theirs, devices), beside


def local(values, b_proj, c_proj, step_sizes, decay_rates, skip_gain, teacher, doc_lengths):
    length, total = values.shape
    heads = step_sizes.shape[1]
    state = b_proj.shape[1]
    devices = lax.axis_size("seq")
    b = b_proj.T
    c = c_proj.T
    groups = total // 2 // 128
    half = out(state // 8 * groups + 2, 8, 128)
    thirds = out(3 * heads, length, dtype=BF16)
    narrow = out(state, length, dtype=BF16)
    square = 2 * length * length * total
    dma = pltpu.SemaphoreType.DMA
    wide = out(length, total, dtype=BF16)
    part = out(length, total // 2)
    part16 = out(length, total // 2, dtype=BF16)
    x_far, send, enter3, sf3, f3, s3, rows, bm, cm, ids, v, teach, b, c = call(
        prepare_kernel,
        [
            pltpu.with_memory_space_constraint(a, pltpu.MemorySpace.HBM)
            for a in (
                doc_lengths,
                values,
                teacher,
                b,
                c,
                step_sizes.T,
                decay_rates.reshape(1, heads),
                skip_gain.reshape(1, heads),
            )
        ],
        [
            part16,
            half,
            thirds,
            thirds,
            thirds,
            thirds,
            out(PAD, total),
            narrow,
            narrow,
            out(PAD, length),
            wide,
            wide,
            narrow,
            narrow,
        ],
        in_specs=[HBM] * 8,
        scratch=[
            pltpu.SMEM(doc_lengths.shape, jnp.int32),
            pltpu.VMEM((heads, length), F32),
            pltpu.VMEM((1, heads), F32),
            pltpu.VMEM((1, heads), F32),
            dma((6,)),
            dma((STEPS,)),
            dma((STEPS,)),
        ],
    )
    x_own, keep = call(prepare_own_kernel, [f3, s3, bm, rows, v], [part16, half])
    inner = call(
        inner_kernel,
        [x_far, x_own, v, teach, b, c, enter3, rows, ids],
        [out(length, total), out(length, length, dtype=BF16)],
        square,
    )
    mine, other, (base, score_t) = carry(keep, send, groups, devices, 1, inner)
    mm_own, y_own, keep = call(
        functools.partial(mismatch_kernel, STEPS // 2), [base, enter3, rows, cm, mine], [part, part16, half]
    )
    mm_far, y_far, send = call(
        functools.partial(mismatch_kernel, 0), [base, enter3, rows, cm, other, keep], [part, part16, half]
    )
    pairs = call(
        pair_kernel,
        [mm_far, mm_own, y_far, y_own, x_far, x_own, score_t, sf3, rows, b, c, ids, other, mine],
        [part, part, out(state, length), out(state, length)],
        2 * square,
        out_specs=[VMEM, VMEM, VMEM, HBM],
        scratch=[pltpu.VMEM((length, length), F32), pltpu.VMEM((state, length), F32), dma],
    )
    mine, other, (g_far, g_own, gb_part, grad_c) = carry(keep, send, groups, devices, -1, pairs)
    grad_values, acc = call(
        finish_own_kernel,
        [g_own, x_own, sf3, rows, bm, mine],
        [out(length, total), out(length, 2 * state)],
        out_specs=[HBM, VMEM],
        scratch=[pltpu.VMEM((length, total // 2), F32), dma((STEPS // 2,))],
    )
    scale = 1.0 / (devices * length * total)
    grad_values, grad_b, loss = call(
        functools.partial(finish_kernel, scale),
        [grad_values, g_far, x_far, sf3, rows, bm, ids, gb_part, acc, mine, other],
        [out(length, total), out(state, length), out(1, 128)],
        in_specs=[HBM] + [VMEM] * 10,
        out_specs=[HBM, HBM, HBM],
        scratch=[
            pltpu.VMEM((length, total // 2), F32),
            pltpu.VMEM((state, length), F32),
            pltpu.VMEM((1, 128), F32),
            dma((STEPS // 2 + 2,)),
        ],
        aliases={0: 0},
    )
    return loss[0, :1], grad_values, grad_b.T, grad_c.T


def solution(mesh):
    rows = P(("groups", "seq"), None)
    in_specs = (rows, rows, rows, rows, P(), P(), rows, P("groups"))
    out_specs = (P("groups"), rows, rows, rows)
    return jax.shard_map(local, mesh=mesh, in_specs=in_specs, out_specs=out_specs, check_vma=False)
```

```python
import functools
import jax
import jax.numpy as jnp
from jax import lax
from jax.experimental import pallas as pl
from jax.experimental.pallas import tpu as pltpu
from jax.sharding import PartitionSpec as P

F32 = jnp.float32
BF16 = jnp.bfloat16
PAD = 8
STEPS = 4
LIMIT = 24 << 20
HBM = pl.BlockSpec(memory_space=pltpu.MemorySpace.HBM)
VMEM = pl.BlockSpec(memory_space=pltpu.MemorySpace.VMEM)


def dot(a, b):
    return jnp.dot(a, b, preferred_element_type=F32)


def dot_nt(a, b):
    return lax.dot_general(a, b, (((1,), (1,)), ((), ())), preferred_element_type=F32)


def dot_tn(a, b):
    return lax.dot_general(a, b, (((0,), (0,)), ((), ())), preferred_element_type=F32)


def iota(shape, axis):
    return lax.broadcasted_iota(jnp.int32, shape, axis)


def split3(x):
    hi = x.astype(BF16)
    rest = x - hi.astype(F32)
    mid = rest.astype(BF16)
    lo = (rest - mid.astype(F32)).astype(BF16)
    return jnp.concatenate([hi, mid, lo], axis=0)


def split2(x):
    hi = x.astype(BF16)
    lo = (x - hi.astype(F32)).astype(BF16)
    return jnp.concatenate([hi, lo], axis=0)


def twice(x):
    return jnp.concatenate([x, x], axis=0)


def chunk_of(j):
    half = STEPS // 2
    return jnp.where(odd_core() == 0, (j + half) % STEPS, j)


def span_of(j, width):
    return pl.ds(pl.multiple_of(chunk_of(j) * width, width), width)


def expander(heads, head_dim, width, j):
    rows = lax.rem(iota((3 * heads, width), 0), heads)
    cols = iota((3 * heads, width), 1) // head_dim + chunk_of(j) * (width // head_dim)
    return (rows == cols).astype(F32).astype(BF16)


def column(row):
    n = row.shape[1]
    return jnp.sum(jnp.where(iota((n, n), 0) == iota((n, n), 1), row, 0.0), axis=1, keepdims=True)


def tall(row):
    return jnp.broadcast_to(row, (128, row.shape[1])).T


def same_doc(ids_ref):
    ids = ids_ref[0:1, :]
    return tall(ids)[:, 0:1] == ids


def odd_core():
    return lax.rem(lax.axis_index("seq"), 2)


def put_half(a, ref, state, decay):
    rows, width = state.shape
    groups = ref.shape[0] // (rows // 8)
    for q in range(width // 128):
        g = a * (width // 128) + q
        cols = slice(q * 128, (q + 1) * 128)
        for r in range(rows // 8):
            ref[r * groups + g] = state[r * 8 : (r + 1) * 8, cols]
        ref[groups * (rows // 8), g : g + 1, :] = decay[:, cols]


def get_half(a, rows, ref, width):
    groups = ref.shape[0] // (rows // 8)
    inside = range(a * (width // 128), (a + 1) * (width // 128))
    return jnp.concatenate(
        [jnp.concatenate([ref[r * groups + g] for g in inside], axis=1) for r in range(rows // 8)], axis=0
    )


def state_half(first, f3, s3, bm, rows_ref, v_ref, x_ref, message_ref, heads):
    total = v_ref.shape[1]
    width = total // STEPS
    for a in range(STEPS // 2):
        j = first + a
        rel = slice(j * width, (j + 1) * width)
        spread = expander(heads, total // heads, width, j)
        scaled = (dot_tn(s3, spread) * v_ref[:, rel].astype(F32)).astype(BF16).astype(F32)
        x = dot_tn(f3, spread) * scaled
        hi = x.astype(BF16)
        lo = (x - hi.astype(F32)).astype(BF16)
        x_ref[:, a * width : (a + 1) * width] = hi
        state = (dot(bm, hi) + dot(bm, lo)) * rows_ref[1:2, rel]
        put_half(a, message_ref, state, rows_ref[2:3, rel])
    message_ref[message_ref.shape[0] - 1] = jnp.zeros((8, 128), F32)


def prepare_kernel(
    lengths_hbm,
    v_hbm,
    teach_hbm,
    b_hbm,
    c_hbm,
    step_hbm,
    rate_hbm,
    gain_hbm,
    x_ref,
    send_ref,
    enter3_ref,
    sf3_ref,
    f3_ref,
    s3_ref,
    rows_ref,
    bm_ref,
    cm_ref,
    ids_ref,
    v,
    teach,
    b,
    c,
    lengths,
    step,
    rate,
    gain,
    sems,
    v_sems,
    t_sems,
):
    heads, length = step.shape
    total = v.shape[1]
    width = total // STEPS
    small = [(step_hbm, step), (rate_hbm, rate), (gain_hbm, gain), (lengths_hbm, lengths), (b_hbm, b), (c_hbm, c)]
    small = [pltpu.make_async_copy(src, dst, sems.at[i]) for i, (src, dst) in enumerate(small)]
    large = []
    for src, dst, sem in ((v_hbm, v, v_sems), (teach_hbm, teach, t_sems)):
        for j in range(STEPS):
            rel = slice(j * width, (j + 1) * width)
            large.append(pltpu.make_async_copy(src.at[:, span_of(j, width)], dst.at[:, rel], sem.at[j]))
    for copy in small + large:
        copy.start()
    upper = (iota((length, length), 0) <= iota((length, length), 1)).astype(F32).astype(BF16)
    for copy in small:
        copy.wait()
    sums = dot(split3(-(step[...] * column(rate[...]))), upper)
    level = sums[:heads] + sums[heads : 2 * heads] + sums[2 * heads :]
    middle = level[:, length // 2 - 1 : length // 2]
    last = level[:, length - 1 : length]
    place = iota((1, length), 1)
    ids = jnp.zeros((1, length), jnp.int32)
    before = jnp.int32(0)
    final = jnp.int32(0)
    start = -lax.axis_index("seq") * length
    for d in range(lengths.shape[0]):
        ids = ids + (place >= start).astype(jnp.int32)
        before = before + (start <= -1).astype(jnp.int32)
        final = final + (start <= length - 1).astype(jnp.int32)
        start = start + lengths[d]
    first_doc = (ids == before).astype(F32)
    last_doc = (ids == final).astype(F32)
    ids_ref[0:1, :] = ids.astype(F32)
    ids_ref[1:2, :] = first_doc
    ids_ref[2:3, :] = last_doc
    leave = jnp.exp(middle - level)
    enter3_ref[...] = split3(jnp.exp(level - middle))
    f3 = split3(leave)
    s3 = split3(step[...])
    f3_ref[...] = f3
    s3_ref[...] = s3
    sf3_ref[...] = split3(step[...] * leave)
    through = jnp.where(before == final, jnp.exp(last), 0.0)
    pick = iota((heads, 128), 1)
    table = jnp.where(pick == 0, jnp.exp(middle), 0.0)
    table = jnp.where(pick == 1, jnp.exp(last - middle), table)
    table = jnp.where(pick == 2, through, table)
    table = jnp.where(pick == 3, column(gain[...]), table)
    r3 = split3(table)
    for j in range(STEPS):
        spread = expander(heads, total // heads, width, j)
        rows_ref[:, j * width : (j + 1) * width] = dot_tn(r3, spread)[:PAD]
    bm = (b[...].astype(F32) * last_doc).astype(BF16)
    bm_ref[...] = bm
    cm_ref[...] = (c[...].astype(F32) * first_doc).astype(BF16)
    for copy in large[: STEPS // 2]:
        copy.wait()
    state_half(0, f3, s3, bm, rows_ref, v, x_ref, send_ref, heads)
    for copy in large[STEPS // 2 :]:
        copy.wait()


def prepare_own_kernel(f3_ref, s3_ref, bm_ref, rows_ref, v_ref, x_ref, keep_ref):
    state_half(
        STEPS // 2, f3_ref[...], s3_ref[...], bm_ref[...], rows_ref, v_ref, x_ref, keep_ref, f3_ref.shape[0] // 3
    )


def inner_kernel(
    xf_ref,
    xo_ref,
    v_ref,
    teach_ref,
    b_ref,
    c_ref,
    enter3_ref,
    sf3_ref,
    rows_ref,
    ids_ref,
    base_ref,
    st_ref,
    enter_ref,
    sf_ref,
):
    length, total = base_ref.shape
    width = total // STEPS
    heads = enter3_ref.shape[0] // 3
    same = same_doc(ids_ref)
    down = iota((length, length), 0)
    along = iota((length, length), 1)
    s = jnp.where(same & (down >= along), dot_tn(c_ref[...], b_ref[...]), 0.0).astype(BF16)
    st_ref[...] = jnp.where(same & (down <= along), dot_tn(b_ref[...], c_ref[...]), 0.0).astype(BF16)
    for j in range(STEPS):
        rel = slice(j * width, (j + 1) * width)
        a = j % (STEPS // 2)
        x_ref = xf_ref if j < STEPS // 2 else xo_ref
        spread = expander(heads, total // heads, width, j)
        enter = dot_tn(enter3_ref[...], spread)
        enter_ref[:, rel] = enter
        sf_ref[:, rel] = dot_tn(sf3_ref[...], spread)
        base_ref[:, rel] = (
            enter * dot(s, x_ref[:, a * width : (a + 1) * width])
            + rows_ref[3:4, rel] * v_ref[:, rel].astype(F32)
            - teach_ref[:, rel].astype(F32)
        )


def mismatch_kernel(first, base_ref, enter_ref, rows_ref, cm_ref, state_ref, *refs):
    more, (mm_ref, y_ref, message_ref) = refs[:-3], refs[-3:]
    length, total = base_ref.shape
    width = total // STEPS
    cm = cm_ref[...]
    sums = jnp.zeros((8, width), F32)
    for a in range(STEPS // 2):
        j = first + a
        rel = slice(j * width, (j + 1) * width)
        part = slice(a * width, (a + 1) * width)
        enter = enter_ref[:, rel]
        state = split2(get_half(a, cm.shape[0], state_ref, width) * rows_ref[0:1, rel])
        mm = base_ref[:, rel] + enter * dot_tn(twice(cm), state)
        mm_ref[:, part] = mm
        y = (enter * mm).astype(BF16)
        y_ref[:, part] = y
        sums = sums + jnp.sum((mm * mm).reshape(length // 8, 8, width), axis=0)
        put_half(a, message_ref, dot(cm, y) * rows_ref[0:1, rel], rows_ref[2:3, rel])
    line = sums[:, :128]
    for q in range(1, width // 128):
        line = line + sums[:, q * 128 : (q + 1) * 128]
    for ref in more:
        line = line + ref[ref.shape[0] - 1]
    message_ref[message_ref.shape[0] - 1] = line


def pair_kernel(
    mmf_ref,
    mmo_ref,
    yf_ref,
    yo_ref,
    xf_ref,
    xo_ref,
    st_ref,
    sf_ref,
    rows_ref,
    b_ref,
    c_ref,
    ids_ref,
    other_ref,
    mine_ref,
    gf_ref,
    go_ref,
    gb_ref,
    gc_hbm,
    pair,
    gc,
    sem,
):
    length, half = mmf_ref.shape
    width = 2 * half // STEPS
    n = b_ref.shape[0]
    acc = jnp.zeros((2 * n, length), F32)
    for j in range(STEPS):
        a = j % (STEPS // 2)
        rel = slice(j * width, (j + 1) * width)
        part = slice(a * width, (a + 1) * width)
        far = j < STEPS // 2
        mm_ref, y_ref, state_ref, g_ref = (
            (mmf_ref, yf_ref, other_ref, gf_ref) if far else (mmo_ref, yo_ref, mine_ref, go_ref)
        )
        y = y_ref[:, part]
        g_ref[:, part] = rows_ref[3:4, rel] * mm_ref[:, part] + sf_ref[:, rel] * dot(st_ref[...], y)
        acc = acc + dot_nt(split2(get_half(a, n, state_ref, width) * rows_ref[0:1, rel]), y)
    pair[...] = dot_nt(yf_ref[...], xf_ref[...])
    pair[...] += dot_nt(yo_ref[...], xo_ref[...])
    keep = same_doc(ids_ref) & (iota((length, length), 0) >= iota((length, length), 1))
    masked = jnp.where(keep, pair[...], 0.0)
    hi = masked.astype(BF16)
    lo = (masked - hi.astype(F32)).astype(BF16)
    through = (acc[:n] + acc[n:]) * ids_ref[1:2, :]
    gc[...] = dot_nt(b_ref[...], hi) + dot_nt(b_ref[...], lo) + through
    copy = pltpu.make_async_copy(gc, gc_hbm, sem)
    copy.start()
    gb_ref[...] = dot(c_ref[...], hi) + dot(c_ref[...], lo)
    copy.wait()


def finish_half(first, g_ref, x_ref, sf_ref, rows_ref, bm_ref, state_ref, gv_hbm, gv, sems):
    half = g_ref.shape[1]
    width = 2 * half // STEPS
    bm2 = twice(bm_ref[...])
    copies = []
    acc = jnp.zeros((g_ref.shape[0], bm2.shape[0]), F32)
    for a in range(STEPS // 2):
        j = first + a
        rel = slice(j * width, (j + 1) * width)
        part = slice(a * width, (a + 1) * width)
        adjoint = split2(get_half(a, bm_ref.shape[0], state_ref, width) * rows_ref[1:2, rel])
        gv[:, part] = g_ref[:, part] + sf_ref[:, rel] * dot_tn(bm2, adjoint)
        copies.append(pltpu.make_async_copy(gv.at[:, part], gv_hbm.at[:, span_of(j, width)], sems.at[a]))
        copies[a].start()
        acc = acc + dot_nt(x_ref[:, part], adjoint)
    return acc, copies


def finish_own_kernel(g_ref, x_ref, sf_ref, rows_ref, bm_ref, mine_ref, gv_hbm, acc_ref, gv, sems):
    acc, copies = finish_half(STEPS // 2, g_ref, x_ref, sf_ref, rows_ref, bm_ref, mine_ref, gv_hbm, gv, sems)
    acc_ref[...] = acc
    for copy in copies:
        copy.wait()


def finish_kernel(
    scale,
    _gv_in,
    g_ref,
    x_ref,
    sf_ref,
    rows_ref,
    bm_ref,
    ids_ref,
    gb_part_ref,
    acc_ref,
    mine_ref,
    other_ref,
    gv_hbm,
    gb_hbm,
    loss_hbm,
    gv,
    gb,
    loss,
    sems,
):
    n = bm_ref.shape[0]
    last = mine_ref.shape[0] - 1
    loss[...] = jnp.broadcast_to(jnp.sum(mine_ref[last] + other_ref[last]) * scale, (1, 128))
    half = STEPS // 2
    out_loss = pltpu.make_async_copy(loss, loss_hbm, sems.at[half])
    out_loss.start()
    acc, copies = finish_half(0, g_ref, x_ref, sf_ref, rows_ref, bm_ref, other_ref, gv_hbm, gv, sems)
    acc = acc + acc_ref[...]
    gb[...] = gb_part_ref[...] + (acc[:, :n] + acc[:, n:]).T * ids_ref[2:3, :]
    out_gb = pltpu.make_async_copy(gb, gb_hbm, sems.at[half + 1])
    out_gb.start()
    for copy in (*copies, out_loss, out_gb):
        copy.wait()


def call(kernel, ins, outs, flops=0, in_specs=None, out_specs=None, scratch=(), aliases=None):
    size = sum(a.size * a.dtype.itemsize for a in ins) + sum(o.size * o.dtype.itemsize for o in outs)
    return pl.pallas_call(
        kernel,
        out_shape=outs,
        in_specs=in_specs or [VMEM] * len(ins),
        out_specs=out_specs or [VMEM] * len(outs),
        scratch_shapes=scratch,
        input_output_aliases=aliases or {},
        compiler_params=pltpu.CompilerParams(vmem_limit_bytes=LIMIT),
        cost_estimate=pl.CostEstimate(flops=flops, bytes_accessed=size, transcendentals=0),
    )(*ins)


def out(*shape, dtype=F32):
    return jax.ShapeDtypeStruct(shape, dtype)


def swap(x, devices):
    return lax.ppermute(x, "seq", [(i, i ^ 1) for i in range(devices)])


def shift(x, by, devices):
    return lax.ppermute(
        x, "seq", [(i, i + by) for i in range(devices) if 0 <= i + by < devices]
    )


def turn(x, by, devices):
    return lax.ppermute(x, "seq", [(i, (i + by) % devices) for i in range(devices)])


def in_order(way, keep_ref, got_ref, body):
    near = odd_core() == (0 if way == 1 else 1)
    pl.when(near)(lambda: body(keep_ref, got_ref, True))
    pl.when(jnp.logical_not(near))(lambda: body(got_ref, keep_ref, False))


def columns(groups, count):
    return [(q, range(q, count, groups)) for q in range(groups)]


def compose_kernel(way, groups, keep_ref, send_ref, got_ref, packed_ref, both_ref, line_ref):
    count = both_ref.shape[0] - 1

    def body(first_ref, second_ref, _near):
        packed_ref[count] = first_ref[count] * second_ref[count]
        for q, places in columns(groups, count):
            decay = second_ref[count, q : q + 1, :]
            for t in places:
                both = second_ref[t] + decay * first_ref[t]
                packed_ref[t] = both
                both_ref[t] = both

    in_order(way, keep_ref, got_ref, body)
    line = send_ref[count + 1] + got_ref[count + 1]
    packed_ref[count + 1] = line
    both_ref[count] = line
    line_ref[...] = line


def arrive_kernel(way, groups, near_chips, keep_ref, got_ref, line_ref, one_ref, two_ref, *refs):
    more_refs, mine_ref, theirs_ref = refs[:-2], refs[-2], refs[-1]
    count = mine_ref.shape[0] - 1

    def body(first_ref, _second_ref, near):
        outer_ref, inner_ref = (mine_ref, theirs_ref) if near else (theirs_ref, mine_ref)
        for q, places in columns(groups, count):
            far_decay = one_ref[count, q : q + 1, :]
            decay = first_ref[count, q : q + 1, :]
            for t in places:
                state = one_ref[t] + far_decay * two_ref[t]
                outer_ref[t] = state
                inner_ref[t] = first_ref[t] + decay * state

    in_order(way, keep_ref, got_ref, body)
    line = jnp.zeros((8, 128), F32)
    if near_chips:
        line = line_ref[...] + one_ref[count + 1] + two_ref[count]
        line = jnp.where((odd_core() == 0).astype(F32) > 0.5, line, 0.0)
    for ref in more_refs:
        line = line + ref[...]
    mine_ref[count] = line
    theirs_ref[count] = line


def far_squares(line, devices):
    chips = devices // 2
    if chips != 8:
        return [lax.psum(line, "seq") * 0.25], False
    lines = []
    for far in range(3, chips, 2):
        pairs = [(i, (i - 2 * (far + i % 2)) % devices) for i in range(devices) if far + i % 2 < chips]
        lines.append(lax.ppermute(line, "seq", pairs))
    return lines, True


def carry(keep, send, groups, devices, way, beside):
    count = keep.shape[0] - 2
    got = swap(send, devices)
    packed, both, line = call(
        functools.partial(compose_kernel, way, groups),
        [keep, send, got],
        [out(*keep.shape), out(count + 1, 8, 128), out(8, 128)],
    )
    reach = max(1, devices // 8)
    move = shift if way == 1 else turn
    one = move(packed, 2 * way, devices)
    two = move(packed if reach > 2 else both, 4 * way, devices)
    lines, near_chips = [], False
    if way == -1:
        lines, near_chips = far_squares(line, devices)
    if reach > 2:

        def join(near, far):
            decay = near[count, :groups]
            state = near[:count].reshape(-1, groups, 8, 128) + decay[:, None, :] * far[:count].reshape(-1, groups, 8, 128)
            return jnp.concatenate([state.reshape(count, 8, 128), (near[count:] * far[count:])], axis=0)

        one = join(one, two)
        span = 2
        while span < reach:
            one = join(one, shift(one, 2 * span * way, devices))
            span *= 2
        two = jnp.zeros_like(both)
    mine, theirs = call(
        functools.partial(arrive_kernel, way, groups, near_chips),
        [keep, got, line, one, two, *lines],
        [out(count + 1, 8, 128), out(count + 1, 8, 128)],
    )
    theirs, beside = lax.optimization_barrier((theirs, beside))
    return mine, swap(theirs, devices), beside


def local(values, b_proj, c_proj, step_sizes, decay_rates, skip_gain, teacher, doc_lengths):
    length, total = values.shape
    heads = step_sizes.shape[1]
    state = b_proj.shape[1]
    devices = lax.axis_size("seq")
    b = b_proj.T
    c = c_proj.T
    groups = total // 2 // 128
    half = out(state // 8 * groups + 2, 8, 128)
    thirds = out(3 * heads, length, dtype=BF16)
    narrow = out(state, length, dtype=BF16)
    square = 2 * length * length * total
    dma = pltpu.SemaphoreType.DMA
    wide = out(length, total, dtype=BF16)
    part = out(length, total // 2)
    part16 = out(length, total // 2, dtype=BF16)
    x_far, send, enter3, sf3, f3, s3, rows, bm, cm, ids, v, teach, b, c = call(
        prepare_kernel,
        [
            pltpu.with_memory_space_constraint(a, pltpu.MemorySpace.HBM)
            for a in (
                doc_lengths,
                values,
                teacher,
                b,
                c,
                step_sizes.T,
                decay_rates.reshape(1, heads),
                skip_gain.reshape(1, heads),
            )
        ],
        [
            part16,
            half,
            thirds,
            thirds,
            thirds,
            thirds,
            out(PAD, total),
            narrow,
            narrow,
            out(PAD, length),
            wide,
            wide,
            narrow,
            narrow,
        ],
        in_specs=[HBM] * 8,
        scratch=[
            pltpu.SMEM(doc_lengths.shape, jnp.int32),
            pltpu.VMEM((heads, length), F32),
            pltpu.VMEM((1, heads), F32),
            pltpu.VMEM((1, heads), F32),
            dma((6,)),
            dma((STEPS,)),
            dma((STEPS,)),
        ],
    )
    x_own, keep = call(prepare_own_kernel, [f3, s3, bm, rows, v], [part16, half])
    inner = call(
        inner_kernel,
        [x_far, x_own, v, teach, b, c, enter3, sf3, rows, ids],
        [out(length, total), out(length, length, dtype=BF16), out(length, total), out(length, total)],
        square,
    )
    mine, other, (base, score_t, enter, sf) = carry(keep, send, groups, devices, 1, inner)
    mm_own, y_own, keep = call(
        functools.partial(mismatch_kernel, STEPS // 2), [base, enter, rows, cm, mine], [part, part16, half]
    )
    mm_far, y_far, send = call(
        functools.partial(mismatch_kernel, 0), [base, enter, rows, cm, other, keep], [part, part16, half]
    )
    pairs = call(
        pair_kernel,
        [mm_far, mm_own, y_far, y_own, x_far, x_own, score_t, sf, rows, b, c, ids, other, mine],
        [part, part, out(state, length), out(state, length)],
        2 * square,
        out_specs=[VMEM, VMEM, VMEM, HBM],
        scratch=[pltpu.VMEM((length, length), F32), pltpu.VMEM((state, length), F32), dma],
    )
    mine, other, (g_far, g_own, gb_part, grad_c) = carry(keep, send, groups, devices, -1, pairs)
    grad_values, acc = call(
        finish_own_kernel,
        [g_own, x_own, sf, rows, bm, mine],
        [out(length, total), out(length, 2 * state)],
        out_specs=[HBM, VMEM],
        scratch=[pltpu.VMEM((length, total // 2), F32), dma((STEPS // 2,))],
    )
    scale = 1.0 / (devices * length * total)
    grad_values, grad_b, loss = call(
        functools.partial(finish_kernel, scale),
        [grad_values, g_far, x_far, sf, rows, bm, ids, gb_part, acc, mine, other],
        [out(length, total), out(state, length), out(1, 128)],
        in_specs=[HBM] + [VMEM] * 10,
        out_specs=[HBM, HBM, HBM],
        scratch=[
            pltpu.VMEM((length, total // 2), F32),
            pltpu.VMEM((state, length), F32),
            pltpu.VMEM((1, 128), F32),
            dma((STEPS // 2 + 2,)),
        ],
        aliases={0: 0},
    )
    return loss[0, :1], grad_values, grad_b.T, grad_c.T


def solution(mesh):
    rows = P(("groups", "seq"), None)
    in_specs = (rows, rows, rows, rows, P(), P(), rows, P("groups"))
    out_specs = (P("groups"), rows, rows, rows)
    return jax.shard_map(local, mesh=mesh, in_specs=in_specs, out_specs=out_specs, check_vma=False)
```

```python
import functools
import jax
import jax.numpy as jnp
from jax import lax
from jax.experimental import pallas as pl
from jax.experimental.pallas import tpu as pltpu
from jax.sharding import PartitionSpec as P

F32 = jnp.float32
BF16 = jnp.bfloat16
PAD = 8
STEPS = 4
LIMIT = 24 << 20
HBM = pl.BlockSpec(memory_space=pltpu.MemorySpace.HBM)
VMEM = pl.BlockSpec(memory_space=pltpu.MemorySpace.VMEM)


def dot(a, b):
    return jnp.dot(a, b, preferred_element_type=F32)


def dot_nt(a, b):
    return lax.dot_general(a, b, (((1,), (1,)), ((), ())), preferred_element_type=F32)


def dot_tn(a, b):
    return lax.dot_general(a, b, (((0,), (0,)), ((), ())), preferred_element_type=F32)


def iota(shape, axis):
    return lax.broadcasted_iota(jnp.int32, shape, axis)


def split3(x):
    hi = x.astype(BF16)
    rest = x - hi.astype(F32)
    mid = rest.astype(BF16)
    lo = (rest - mid.astype(F32)).astype(BF16)
    return jnp.concatenate([hi, mid, lo], axis=0)


def split2(x):
    hi = x.astype(BF16)
    lo = (x - hi.astype(F32)).astype(BF16)
    return jnp.concatenate([hi, lo], axis=0)


def twice(x):
    return jnp.concatenate([x, x], axis=0)


def chunk_of(j):
    half = STEPS // 2
    return jnp.where(odd_core() == 0, (j + half) % STEPS, j)


def span_of(j, width):
    return pl.ds(pl.multiple_of(chunk_of(j) * width, width), width)


def expander(heads, head_dim, width, j):
    rows = lax.rem(iota((3 * heads, width), 0), heads)
    cols = iota((3 * heads, width), 1) // head_dim + chunk_of(j) * (width // head_dim)
    return (rows == cols).astype(F32).astype(BF16)


def column(row):
    n = row.shape[1]
    return jnp.sum(jnp.where(iota((n, n), 0) == iota((n, n), 1), row, 0.0), axis=1, keepdims=True)


def tall(row):
    return jnp.broadcast_to(row, (128, row.shape[1])).T


def same_doc(ids_ref):
    ids = ids_ref[0:1, :]
    return tall(ids)[:, 0:1] == ids


def odd_core():
    return lax.rem(lax.axis_index("seq"), 2)


def put_half(a, ref, state, decay):
    rows, width = state.shape
    groups = ref.shape[0] // (rows // 8)
    for q in range(width // 128):
        g = a * (width // 128) + q
        cols = slice(q * 128, (q + 1) * 128)
        for r in range(rows // 8):
            ref[r * groups + g] = state[r * 8 : (r + 1) * 8, cols]
        ref[groups * (rows // 8), g : g + 1, :] = decay[:, cols]


def get_half(a, rows, ref, width):
    groups = ref.shape[0] // (rows // 8)
    inside = range(a * (width // 128), (a + 1) * (width // 128))
    return jnp.concatenate(
        [jnp.concatenate([ref[r * groups + g] for g in inside], axis=1) for r in range(rows // 8)], axis=0
    )


def state_half(first, f3, s3, bm, rows_ref, v_ref, x_ref, message_ref, heads):
    total = v_ref.shape[1]
    width = total // STEPS
    for a in range(STEPS // 2):
        j = first + a
        rel = slice(j * width, (j + 1) * width)
        spread = expander(heads, total // heads, width, j)
        scaled = (dot_tn(s3, spread) * v_ref[:, rel].astype(F32)).astype(BF16).astype(F32)
        x = dot_tn(f3, spread) * scaled
        hi = x.astype(BF16)
        x_ref[:, a * width : (a + 1) * width] = hi
        state = dot(bm, hi) * rows_ref[1:2, rel]
        put_half(a, message_ref, state, rows_ref[2:3, rel])
    message_ref[message_ref.shape[0] - 1] = jnp.zeros((8, 128), F32)


def prepare_kernel(
    lengths_hbm,
    v_hbm,
    teach_hbm,
    b_hbm,
    c_hbm,
    step_hbm,
    rate_hbm,
    gain_hbm,
    x_ref,
    send_ref,
    enter3_ref,
    sf3_ref,
    f3_ref,
    s3_ref,
    rows_ref,
    bm_ref,
    cm_ref,
    ids_ref,
    v,
    teach,
    b,
    c,
    lengths,
    step,
    rate,
    gain,
    sems,
    v_sems,
    t_sems,
):
    heads, length = step.shape
    total = v.shape[1]
    width = total // STEPS
    small = [(step_hbm, step), (rate_hbm, rate), (gain_hbm, gain), (lengths_hbm, lengths), (b_hbm, b), (c_hbm, c)]
    small = [pltpu.make_async_copy(src, dst, sems.at[i]) for i, (src, dst) in enumerate(small)]
    large = []
    for src, dst, sem in ((v_hbm, v, v_sems), (teach_hbm, teach, t_sems)):
        for j in range(STEPS):
            rel = slice(j * width, (j + 1) * width)
            large.append(pltpu.make_async_copy(src.at[:, span_of(j, width)], dst.at[:, rel], sem.at[j]))
    for copy in small + large:
        copy.start()
    upper = (iota((length, length), 0) <= iota((length, length), 1)).astype(F32).astype(BF16)
    for copy in small:
        copy.wait()
    sums = dot(split3(-(step[...] * column(rate[...]))), upper)
    level = sums[:heads] + sums[heads : 2 * heads] + sums[2 * heads :]
    middle = level[:, length // 2 - 1 : length // 2]
    last = level[:, length - 1 : length]
    place = iota((1, length), 1)
    ids = jnp.zeros((1, length), jnp.int32)
    before = jnp.int32(0)
    final = jnp.int32(0)
    start = -lax.axis_index("seq") * length
    for d in range(lengths.shape[0]):
        ids = ids + (place >= start).astype(jnp.int32)
        before = before + (start <= -1).astype(jnp.int32)
        final = final + (start <= length - 1).astype(jnp.int32)
        start = start + lengths[d]
    first_doc = (ids == before).astype(F32)
    last_doc = (ids == final).astype(F32)
    ids_ref[0:1, :] = ids.astype(F32)
    ids_ref[1:2, :] = first_doc
    ids_ref[2:3, :] = last_doc
    leave = jnp.exp(middle - level)
    enter3_ref[...] = split3(jnp.exp(level - middle))
    f3 = split3(leave)
    s3 = split3(step[...])
    f3_ref[...] = f3
    s3_ref[...] = s3
    sf3_ref[...] = split3(step[...] * leave)
    through = jnp.where(before == final, jnp.exp(last), 0.0)
    pick = iota((heads, 128), 1)
    table = jnp.where(pick == 0, jnp.exp(middle), 0.0)
    table = jnp.where(pick == 1, jnp.exp(last - middle), table)
    table = jnp.where(pick == 2, through, table)
    table = jnp.where(pick == 3, column(gain[...]), table)
    r3 = split3(table)
    for j in range(STEPS):
        spread = expander(heads, total // heads, width, j)
        rows_ref[:, j * width : (j + 1) * width] = dot_tn(r3, spread)[:PAD]
    bm = (b[...].astype(F32) * last_doc).astype(BF16)
    bm_ref[...] = bm
    cm_ref[...] = (c[...].astype(F32) * first_doc).astype(BF16)
    for copy in large[: STEPS // 2]:
        copy.wait()
    state_half(0, f3, s3, bm, rows_ref, v, x_ref, send_ref, heads)
    for copy in large[STEPS // 2 :]:
        copy.wait()


def prepare_own_kernel(f3_ref, s3_ref, bm_ref, rows_ref, v_ref, x_ref, keep_ref):
    state_half(
        STEPS // 2, f3_ref[...], s3_ref[...], bm_ref[...], rows_ref, v_ref, x_ref, keep_ref, f3_ref.shape[0] // 3
    )


def inner_kernel(
    xf_ref,
    xo_ref,
    v_ref,
    teach_ref,
    b_ref,
    c_ref,
    enter3_ref,
    sf3_ref,
    rows_ref,
    ids_ref,
    bm_ref,
    cm_ref,
    base_ref,
    st_ref,
    enter_ref,
    sf_ref,
    bm2_ref,
    cm2_ref,
):
    length, total = base_ref.shape
    width = total // STEPS
    heads = enter3_ref.shape[0] // 3
    bm2_ref[...] = twice(bm_ref[...].astype(F32)).T.astype(BF16)
    cm2_ref[...] = twice(cm_ref[...].astype(F32)).T.astype(BF16)
    same = same_doc(ids_ref)
    down = iota((length, length), 0)
    along = iota((length, length), 1)
    s = jnp.where(same & (down >= along), dot_tn(c_ref[...], b_ref[...]), 0.0).astype(BF16)
    st_ref[...] = jnp.where(same & (down <= along), dot_tn(b_ref[...], c_ref[...]), 0.0).astype(BF16)
    for j in range(STEPS):
        rel = slice(j * width, (j + 1) * width)
        a = j % (STEPS // 2)
        x_ref = xf_ref if j < STEPS // 2 else xo_ref
        spread = expander(heads, total // heads, width, j)
        enter = dot_tn(enter3_ref[...], spread)
        enter_ref[:, rel] = enter
        sf_ref[:, rel] = dot_tn(sf3_ref[...], spread)
        base_ref[:, rel] = (
            enter * dot(s, x_ref[:, a * width : (a + 1) * width])
            + rows_ref[3:4, rel] * v_ref[:, rel].astype(F32)
            - teach_ref[:, rel].astype(F32)
        )


def mismatch_kernel(first, base_ref, enter_ref, rows_ref, cm_ref, cm2_ref, state_ref, *refs):
    more, (mm_ref, y_ref, message_ref) = refs[:-3], refs[-3:]
    length, total = base_ref.shape
    width = total // STEPS
    cm = cm_ref[...]
    sums = jnp.zeros((8, width), F32)
    for a in range(STEPS // 2):
        j = first + a
        rel = slice(j * width, (j + 1) * width)
        part = slice(a * width, (a + 1) * width)
        enter = enter_ref[:, rel]
        state = split2(get_half(a, cm.shape[0], state_ref, width) * rows_ref[0:1, rel])
        mm = base_ref[:, rel] + enter * dot(cm2_ref[...], state)
        mm_ref[:, part] = mm
        y = (enter * mm).astype(BF16)
        y_ref[:, part] = y
        sums = sums + jnp.sum((mm * mm).reshape(length // 8, 8, width), axis=0)
        put_half(a, message_ref, dot(cm, y) * rows_ref[0:1, rel], rows_ref[2:3, rel])
    line = sums[:, :128]
    for q in range(1, width // 128):
        line = line + sums[:, q * 128 : (q + 1) * 128]
    for ref in more:
        line = line + ref[ref.shape[0] - 1]
    message_ref[message_ref.shape[0] - 1] = line


def pair_kernel(
    mmf_ref,
    mmo_ref,
    yf_ref,
    yo_ref,
    xf_ref,
    xo_ref,
    st_ref,
    sf_ref,
    rows_ref,
    b_ref,
    c_ref,
    ids_ref,
    other_ref,
    mine_ref,
    gf_ref,
    go_ref,
    gb_ref,
    gc_hbm,
    pair,
    gc,
    sem,
):
    length, half = mmf_ref.shape
    width = 2 * half // STEPS
    n = b_ref.shape[0]
    acc = jnp.zeros((2 * n, length), F32)
    for j in range(STEPS):
        a = j % (STEPS // 2)
        rel = slice(j * width, (j + 1) * width)
        part = slice(a * width, (a + 1) * width)
        far = j < STEPS // 2
        mm_ref, y_ref, state_ref, g_ref = (
            (mmf_ref, yf_ref, other_ref, gf_ref) if far else (mmo_ref, yo_ref, mine_ref, go_ref)
        )
        y = y_ref[:, part]
        g_ref[:, part] = rows_ref[3:4, rel] * mm_ref[:, part] + sf_ref[:, rel] * dot(st_ref[...], y)
        acc = acc + dot_nt(split2(get_half(a, n, state_ref, width) * rows_ref[0:1, rel]), y)
    pair[...] = dot_nt(yf_ref[...], xf_ref[...])
    pair[...] += dot_nt(yo_ref[...], xo_ref[...])
    keep = same_doc(ids_ref) & (iota((length, length), 0) >= iota((length, length), 1))
    masked = jnp.where(keep, pair[...], 0.0)
    hi = masked.astype(BF16)
    lo = (masked - hi.astype(F32)).astype(BF16)
    through = (acc[:n] + acc[n:]) * ids_ref[1:2, :]
    gc[...] = dot_nt(b_ref[...], hi) + dot_nt(b_ref[...], lo) + through
    copy = pltpu.make_async_copy(gc, gc_hbm, sem)
    copy.start()
    gb_ref[...] = dot(c_ref[...], hi) + dot(c_ref[...], lo)
    copy.wait()


def finish_half(first, g_ref, x_ref, sf_ref, rows_ref, bm2_ref, state_ref, gv_hbm, gv, sems):
    half = g_ref.shape[1]
    width = 2 * half // STEPS
    n = bm2_ref.shape[1] // 2
    copies = []
    acc = jnp.zeros(bm2_ref.shape, F32)
    for a in range(STEPS // 2):
        j = first + a
        rel = slice(j * width, (j + 1) * width)
        part = slice(a * width, (a + 1) * width)
        adjoint = split2(get_half(a, n, state_ref, width) * rows_ref[1:2, rel])
        gv[:, part] = g_ref[:, part] + sf_ref[:, rel] * dot(bm2_ref[...], adjoint)
        copies.append(pltpu.make_async_copy(gv.at[:, part], gv_hbm.at[:, span_of(j, width)], sems.at[a]))
        copies[a].start()
        acc = acc + dot_nt(x_ref[:, part], adjoint)
    return acc, copies


def finish_own_kernel(g_ref, x_ref, sf_ref, rows_ref, bm2_ref, mine_ref, gv_hbm, acc_ref, gv, sems):
    acc, copies = finish_half(STEPS // 2, g_ref, x_ref, sf_ref, rows_ref, bm2_ref, mine_ref, gv_hbm, gv, sems)
    acc_ref[...] = acc
    for copy in copies:
        copy.wait()


def finish_kernel(
    scale,
    _gv_in,
    g_ref,
    x_ref,
    sf_ref,
    rows_ref,
    bm2_ref,
    ids_ref,
    gb_part_ref,
    acc_ref,
    mine_ref,
    other_ref,
    gv_hbm,
    gb_hbm,
    loss_hbm,
    gv,
    gb,
    loss,
    sems,
):
    n = bm2_ref.shape[1] // 2
    last = mine_ref.shape[0] - 1
    loss[...] = jnp.broadcast_to(jnp.sum(mine_ref[last] + other_ref[last]) * scale, (1, 128))
    half = STEPS // 2
    out_loss = pltpu.make_async_copy(loss, loss_hbm, sems.at[half])
    out_loss.start()
    acc, copies = finish_half(0, g_ref, x_ref, sf_ref, rows_ref, bm2_ref, other_ref, gv_hbm, gv, sems)
    acc = acc + acc_ref[...]
    gb[...] = gb_part_ref[...] + (acc[:, :n] + acc[:, n:]).T * ids_ref[2:3, :]
    out_gb = pltpu.make_async_copy(gb, gb_hbm, sems.at[half + 1])
    out_gb.start()
    for copy in (*copies, out_loss, out_gb):
        copy.wait()


def call(kernel, ins, outs, flops=0, in_specs=None, out_specs=None, scratch=(), aliases=None):
    size = sum(a.size * a.dtype.itemsize for a in ins) + sum(o.size * o.dtype.itemsize for o in outs)
    return pl.pallas_call(
        kernel,
        out_shape=outs,
        in_specs=in_specs or [VMEM] * len(ins),
        out_specs=out_specs or [VMEM] * len(outs),
        scratch_shapes=scratch,
        input_output_aliases=aliases or {},
        compiler_params=pltpu.CompilerParams(vmem_limit_bytes=LIMIT),
        cost_estimate=pl.CostEstimate(flops=flops, bytes_accessed=size, transcendentals=0),
    )(*ins)


def out(*shape, dtype=F32):
    return jax.ShapeDtypeStruct(shape, dtype)


def swap(x, devices):
    return lax.ppermute(x, "seq", [(i, i ^ 1) for i in range(devices)])


def shift(x, by, devices):
    return lax.ppermute(
        x, "seq", [(i, i + by) for i in range(devices) if 0 <= i + by < devices]
    )


def turn(x, by, devices):
    return lax.ppermute(x, "seq", [(i, (i + by) % devices) for i in range(devices)])


def in_order(way, keep_ref, got_ref, body):
    near = odd_core() == (0 if way == 1 else 1)
    pl.when(near)(lambda: body(keep_ref, got_ref, True))
    pl.when(jnp.logical_not(near))(lambda: body(got_ref, keep_ref, False))


def columns(groups, count):
    return [(q, range(q, count, groups)) for q in range(groups)]


def compose_kernel(way, groups, keep_ref, send_ref, got_ref, packed_ref, both_ref, line_ref):
    count = both_ref.shape[0] - 1

    def body(first_ref, second_ref, _near):
        packed_ref[count] = first_ref[count] * second_ref[count]
        for q, places in columns(groups, count):
            decay = second_ref[count, q : q + 1, :]
            for t in places:
                both = second_ref[t] + decay * first_ref[t]
                packed_ref[t] = both
                both_ref[t] = both

    in_order(way, keep_ref, got_ref, body)
    line = send_ref[count + 1] + got_ref[count + 1]
    packed_ref[count + 1] = line
    both_ref[count] = line
    line_ref[...] = line


def arrive_kernel(way, groups, near_chips, keep_ref, got_ref, line_ref, one_ref, two_ref, *refs):
    more_refs, mine_ref, theirs_ref = refs[:-2], refs[-2], refs[-1]
    count = mine_ref.shape[0] - 1

    def body(first_ref, _second_ref, near):
        outer_ref, inner_ref = (mine_ref, theirs_ref) if near else (theirs_ref, mine_ref)
        for q, places in columns(groups, count):
            far_decay = one_ref[count, q : q + 1, :]
            decay = first_ref[count, q : q + 1, :]
            for t in places:
                state = one_ref[t] + far_decay * two_ref[t]
                outer_ref[t] = state
                inner_ref[t] = first_ref[t] + decay * state

    in_order(way, keep_ref, got_ref, body)
    line = jnp.zeros((8, 128), F32)
    if near_chips:
        line = line_ref[...] + one_ref[count + 1] + two_ref[count]
        line = jnp.where((odd_core() == 0).astype(F32) > 0.5, line, 0.0)
    for ref in more_refs:
        line = line + ref[...]
    mine_ref[count] = line
    theirs_ref[count] = line


def far_squares(line, devices):
    chips = devices // 2
    if chips != 8:
        return [lax.psum(line, "seq") * 0.25], False
    lines = []
    for far in range(3, chips, 2):
        pairs = [(i, (i - 2 * (far + i % 2)) % devices) for i in range(devices) if far + i % 2 < chips]
        lines.append(lax.ppermute(line, "seq", pairs))
    return lines, True


def carry(keep, send, groups, devices, way, beside):
    count = keep.shape[0] - 2
    got = swap(send, devices)
    packed, both, line = call(
        functools.partial(compose_kernel, way, groups),
        [keep, send, got],
        [out(*keep.shape), out(count + 1, 8, 128), out(8, 128)],
    )
    reach = max(1, devices // 8)
    move = shift if way == 1 else turn
    one = move(packed, 2 * way, devices)
    two = move(packed if reach > 2 else both, 4 * way, devices)
    lines, near_chips = [], False
    if way == -1:
        lines, near_chips = far_squares(line, devices)
    if reach > 2:

        def join(near, far):
            decay = near[count, :groups]
            state = near[:count].reshape(-1, groups, 8, 128) + decay[:, None, :] * far[:count].reshape(-1, groups, 8, 128)
            return jnp.concatenate([state.reshape(count, 8, 128), (near[count:] * far[count:])], axis=0)

        one = join(one, two)
        span = 2
        while span < reach:
            one = join(one, shift(one, 2 * span * way, devices))
            span *= 2
        two = jnp.zeros_like(both)
    mine, theirs = call(
        functools.partial(arrive_kernel, way, groups, near_chips),
        [keep, got, line, one, two, *lines],
        [out(count + 1, 8, 128), out(count + 1, 8, 128)],
    )
    theirs, beside = lax.optimization_barrier((theirs, beside))
    return mine, swap(theirs, devices), beside


def local(values, b_proj, c_proj, step_sizes, decay_rates, skip_gain, teacher, doc_lengths):
    length, total = values.shape
    heads = step_sizes.shape[1]
    state = b_proj.shape[1]
    devices = lax.axis_size("seq")
    b = b_proj.T
    c = c_proj.T
    groups = total // 2 // 128
    half = out(state // 8 * groups + 2, 8, 128)
    thirds = out(3 * heads, length, dtype=BF16)
    narrow = out(state, length, dtype=BF16)
    square = 2 * length * length * total
    dma = pltpu.SemaphoreType.DMA
    wide = out(length, total, dtype=BF16)
    part = out(length, total // 2)
    doubled = out(length, 2 * state, dtype=BF16)
    part16 = out(length, total // 2, dtype=BF16)
    x_far, send, enter3, sf3, f3, s3, rows, bm, cm, ids, v, teach, b, c = call(
        prepare_kernel,
        [
            pltpu.with_memory_space_constraint(a, pltpu.MemorySpace.HBM)
            for a in (
                doc_lengths,
                values,
                teacher,
                b,
                c,
                step_sizes.T,
                decay_rates.reshape(1, heads),
                skip_gain.reshape(1, heads),
            )
        ],
        [
            part16,
            half,
            thirds,
            thirds,
            thirds,
            thirds,
            out(PAD, total),
            narrow,
            narrow,
            out(PAD, length),
            wide,
            wide,
            narrow,
            narrow,
        ],
        in_specs=[HBM] * 8,
        scratch=[
            pltpu.SMEM(doc_lengths.shape, jnp.int32),
            pltpu.VMEM((heads, length), F32),
            pltpu.VMEM((1, heads), F32),
            pltpu.VMEM((1, heads), F32),
            dma((6,)),
            dma((STEPS,)),
            dma((STEPS,)),
        ],
    )
    x_own, keep = call(prepare_own_kernel, [f3, s3, bm, rows, v], [part16, half])
    inner = call(
        inner_kernel,
        [x_far, x_own, v, teach, b, c, enter3, sf3, rows, ids, bm, cm],
        [
            out(length, total),
            out(length, length, dtype=BF16),
            out(length, total),
            out(length, total),
            doubled,
            doubled,
        ],
        square,
    )
    mine, other, (base, score_t, enter, sf, bm2, cm2) = carry(keep, send, groups, devices, 1, inner)
    mm_own, y_own, keep = call(
        functools.partial(mismatch_kernel, STEPS // 2), [base, enter, rows, cm, cm2, mine], [part, part16, half]
    )
    mm_far, y_far, send = call(
        functools.partial(mismatch_kernel, 0), [base, enter, rows, cm, cm2, other, keep], [part, part16, half]
    )
    pairs = call(
        pair_kernel,
        [mm_far, mm_own, y_far, y_own, x_far, x_own, score_t, sf, rows, b, c, ids, other, mine],
        [part, part, out(state, length), out(state, length)],
        2 * square,
        out_specs=[VMEM, VMEM, VMEM, HBM],
        scratch=[pltpu.VMEM((length, length), F32), pltpu.VMEM((state, length), F32), dma],
    )
    mine, other, (g_far, g_own, gb_part, grad_c) = carry(keep, send, groups, devices, -1, pairs)
    grad_values, acc = call(
        finish_own_kernel,
        [g_own, x_own, sf, rows, bm2, mine],
        [out(length, total), out(length, 2 * state)],
        out_specs=[HBM, VMEM],
        scratch=[pltpu.VMEM((length, total // 2), F32), dma((STEPS // 2,))],
    )
    scale = 1.0 / (devices * length * total)
    grad_values, grad_b, loss = call(
        functools.partial(finish_kernel, scale),
        [grad_values, g_far, x_far, sf, rows, bm2, ids, gb_part, acc, mine, other],
        [out(length, total), out(state, length), out(1, 128)],
        in_specs=[HBM] + [VMEM] * 10,
        out_specs=[HBM, HBM, HBM],
        scratch=[
            pltpu.VMEM((length, total // 2), F32),
            pltpu.VMEM((state, length), F32),
            pltpu.VMEM((1, 128), F32),
            dma((STEPS // 2 + 2,)),
        ],
        aliases={0: 0},
    )
    return loss[0, :1], grad_values, grad_b.T, grad_c.T


def solution(mesh):
    rows = P(("groups", "seq"), None)
    in_specs = (rows, rows, rows, rows, P(), P(), rows, P("groups"))
    out_specs = (P("groups"), rows, rows, rows)
    return jax.shard_map(local, mesh=mesh, in_specs=in_specs, out_specs=out_specs, check_vma=False)
```

```python
import functools
import jax
import jax.numpy as jnp
from jax import lax
from jax.experimental import pallas as pl
from jax.experimental.pallas import tpu as pltpu
from jax.sharding import PartitionSpec as P

F32 = jnp.float32
BF16 = jnp.bfloat16
PAD = 8
STEPS = 2
LIMIT = 24 << 20
HBM = pl.BlockSpec(memory_space=pltpu.MemorySpace.HBM)
VMEM = pl.BlockSpec(memory_space=pltpu.MemorySpace.VMEM)


def dot(a, b):
    return jnp.dot(a, b, preferred_element_type=F32)


def dot_nt(a, b):
    return lax.dot_general(a, b, (((1,), (1,)), ((), ())), preferred_element_type=F32)


def dot_tn(a, b):
    return lax.dot_general(a, b, (((0,), (0,)), ((), ())), preferred_element_type=F32)


def iota(shape, axis):
    return lax.broadcasted_iota(jnp.int32, shape, axis)


def split3(x):
    hi = x.astype(BF16)
    rest = x - hi.astype(F32)
    mid = rest.astype(BF16)
    lo = (rest - mid.astype(F32)).astype(BF16)
    return jnp.concatenate([hi, mid, lo], axis=0)


def split2(x):
    hi = x.astype(BF16)
    lo = (x - hi.astype(F32)).astype(BF16)
    return jnp.concatenate([hi, lo], axis=0)


def twice(x):
    return jnp.concatenate([x, x], axis=0)


def chunk_of(j):
    half = STEPS // 2
    return jnp.where(odd_core() == 0, (j + half) % STEPS, j)


def span_of(j, width):
    return pl.ds(pl.multiple_of(chunk_of(j) * width, width), width)


def expander(heads, head_dim, width, j):
    rows = lax.rem(iota((3 * heads, width), 0), heads)
    cols = iota((3 * heads, width), 1) // head_dim + chunk_of(j) * (width // head_dim)
    return (rows == cols).astype(F32).astype(BF16)


def column(row):
    n = row.shape[1]
    return jnp.sum(jnp.where(iota((n, n), 0) == iota((n, n), 1), row, 0.0), axis=1, keepdims=True)


def tall(row):
    return jnp.broadcast_to(row, (128, row.shape[1])).T


def same_doc(ids_ref):
    ids = ids_ref[0:1, :]
    return tall(ids)[:, 0:1] == ids


def odd_core():
    return lax.rem(lax.axis_index("seq"), 2)


def put_half(a, ref, state, decay):
    rows, width = state.shape
    groups = ref.shape[0] // (rows // 8)
    for q in range(width // 128):
        g = a * (width // 128) + q
        cols = slice(q * 128, (q + 1) * 128)
        for r in range(rows // 8):
            ref[r * groups + g] = state[r * 8 : (r + 1) * 8, cols]
        ref[groups * (rows // 8), g : g + 1, :] = decay[:, cols]


def get_half(a, rows, ref, width):
    groups = ref.shape[0] // (rows // 8)
    inside = range(a * (width // 128), (a + 1) * (width // 128))
    return jnp.concatenate(
        [jnp.concatenate([ref[r * groups + g] for g in inside], axis=1) for r in range(rows // 8)], axis=0
    )


def state_half(first, f3, s3, bm, rows_ref, v_ref, x_ref, message_ref, heads):
    total = v_ref.shape[1]
    width = total // STEPS
    for a in range(STEPS // 2):
        j = first + a
        rel = slice(j * width, (j + 1) * width)
        spread = expander(heads, total // heads, width, j)
        scaled = (dot_tn(s3, spread) * v_ref[:, rel].astype(F32)).astype(BF16).astype(F32)
        x = dot_tn(f3, spread) * scaled
        hi = x.astype(BF16)
        x_ref[:, a * width : (a + 1) * width] = hi
        state = dot(bm, hi) * rows_ref[1:2, rel]
        put_half(a, message_ref, state, rows_ref[2:3, rel])
    message_ref[message_ref.shape[0] - 1] = jnp.zeros((8, 128), F32)


def prepare_kernel(
    lengths_hbm,
    v_hbm,
    teach_hbm,
    b_hbm,
    c_hbm,
    step_hbm,
    rate_hbm,
    gain_hbm,
    x_ref,
    send_ref,
    enter3_ref,
    sf3_ref,
    f3_ref,
    s3_ref,
    rows_ref,
    bm_ref,
    cm_ref,
    ids_ref,
    v,
    teach,
    b,
    c,
    lengths,
    step,
    rate,
    gain,
    sems,
    v_sems,
    t_sems,
):
    heads, length = step.shape
    total = v.shape[1]
    width = total // STEPS
    small = [(step_hbm, step), (rate_hbm, rate), (gain_hbm, gain), (lengths_hbm, lengths), (b_hbm, b), (c_hbm, c)]
    small = [pltpu.make_async_copy(src, dst, sems.at[i]) for i, (src, dst) in enumerate(small)]
    large = []
    for src, dst, sem in ((v_hbm, v, v_sems), (teach_hbm, teach, t_sems)):
        for j in range(STEPS):
            rel = slice(j * width, (j + 1) * width)
            large.append(pltpu.make_async_copy(src.at[:, span_of(j, width)], dst.at[:, rel], sem.at[j]))
    for copy in small + large:
        copy.start()
    upper = (iota((length, length), 0) <= iota((length, length), 1)).astype(F32).astype(BF16)
    for copy in small:
        copy.wait()
    sums = dot(split3(-(step[...] * column(rate[...]))), upper)
    level = sums[:heads] + sums[heads : 2 * heads] + sums[2 * heads :]
    middle = level[:, length // 2 - 1 : length // 2]
    last = level[:, length - 1 : length]
    place = iota((1, length), 1)
    ids = jnp.zeros((1, length), jnp.int32)
    before = jnp.int32(0)
    final = jnp.int32(0)
    start = -lax.axis_index("seq") * length
    for d in range(lengths.shape[0]):
        ids = ids + (place >= start).astype(jnp.int32)
        before = before + (start <= -1).astype(jnp.int32)
        final = final + (start <= length - 1).astype(jnp.int32)
        start = start + lengths[d]
    first_doc = (ids == before).astype(F32)
    last_doc = (ids == final).astype(F32)
    ids_ref[0:1, :] = ids.astype(F32)
    ids_ref[1:2, :] = first_doc
    ids_ref[2:3, :] = last_doc
    leave = jnp.exp(middle - level)
    enter3_ref[...] = split3(jnp.exp(level - middle))
    f3 = split3(leave)
    s3 = split3(step[...])
    f3_ref[...] = f3
    s3_ref[...] = s3
    sf3_ref[...] = split3(step[...] * leave)
    through = jnp.where(before == final, jnp.exp(last), 0.0)
    pick = iota((heads, 128), 1)
    table = jnp.where(pick == 0, jnp.exp(middle), 0.0)
    table = jnp.where(pick == 1, jnp.exp(last - middle), table)
    table = jnp.where(pick == 2, through, table)
    table = jnp.where(pick == 3, column(gain[...]), table)
    r3 = split3(table)
    for j in range(STEPS):
        spread = expander(heads, total // heads, width, j)
        rows_ref[:, j * width : (j + 1) * width] = dot_tn(r3, spread)[:PAD]
    bm = (b[...].astype(F32) * last_doc).astype(BF16)
    bm_ref[...] = bm
    cm_ref[...] = (c[...].astype(F32) * first_doc).astype(BF16)
    for copy in large[: STEPS // 2]:
        copy.wait()
    state_half(0, f3, s3, bm, rows_ref, v, x_ref, send_ref, heads)
    for copy in large[STEPS // 2 :]:
        copy.wait()


def prepare_own_kernel(f3_ref, s3_ref, bm_ref, rows_ref, v_ref, x_ref, keep_ref):
    state_half(
        STEPS // 2, f3_ref[...], s3_ref[...], bm_ref[...], rows_ref, v_ref, x_ref, keep_ref, f3_ref.shape[0] // 3
    )


def inner_kernel(
    xf_ref,
    xo_ref,
    v_ref,
    teach_ref,
    b_ref,
    c_ref,
    enter3_ref,
    sf3_ref,
    rows_ref,
    ids_ref,
    bm_ref,
    cm_ref,
    base_ref,
    st_ref,
    enter_ref,
    sf_ref,
    bm2_ref,
    cm2_ref,
):
    length, total = base_ref.shape
    width = total // STEPS
    heads = enter3_ref.shape[0] // 3
    bm2_ref[...] = twice(bm_ref[...].astype(F32)).T.astype(BF16)
    cm2_ref[...] = twice(cm_ref[...].astype(F32)).T.astype(BF16)
    same = same_doc(ids_ref)
    down = iota((length, length), 0)
    along = iota((length, length), 1)
    s = jnp.where(same & (down >= along), dot_tn(c_ref[...], b_ref[...]), 0.0).astype(BF16)
    st_ref[...] = jnp.where(same & (down <= along), dot_tn(b_ref[...], c_ref[...]), 0.0).astype(BF16)
    for j in range(STEPS):
        rel = slice(j * width, (j + 1) * width)
        a = j % (STEPS // 2)
        x_ref = xf_ref if j < STEPS // 2 else xo_ref
        spread = expander(heads, total // heads, width, j)
        enter = dot_tn(enter3_ref[...], spread)
        enter_ref[:, rel] = enter
        sf_ref[:, rel] = dot_tn(sf3_ref[...], spread)
        base_ref[:, rel] = (
            enter * dot(s, x_ref[:, a * width : (a + 1) * width])
            + rows_ref[3:4, rel] * v_ref[:, rel].astype(F32)
            - teach_ref[:, rel].astype(F32)
        )


def mismatch_kernel(first, base_ref, enter_ref, rows_ref, cm_ref, cm2_ref, state_ref, *refs):
    more, (mm_ref, y_ref, message_ref) = refs[:-3], refs[-3:]
    length, total = base_ref.shape
    width = total // STEPS
    cm = cm_ref[...]
    sums = jnp.zeros((8, width), F32)
    for a in range(STEPS // 2):
        j = first + a
        rel = slice(j * width, (j + 1) * width)
        part = slice(a * width, (a + 1) * width)
        enter = enter_ref[:, rel]
        state = split2(get_half(a, cm.shape[0], state_ref, width) * rows_ref[0:1, rel])
        mm = base_ref[:, rel] + enter * dot(cm2_ref[...], state)
        mm_ref[:, part] = mm
        y = (enter * mm).astype(BF16)
        y_ref[:, part] = y
        sums = sums + jnp.sum((mm * mm).reshape(length // 8, 8, width), axis=0)
        put_half(a, message_ref, dot(cm, y) * rows_ref[0:1, rel], rows_ref[2:3, rel])
    line = sums[:, :128]
    for q in range(1, width // 128):
        line = line + sums[:, q * 128 : (q + 1) * 128]
    for ref in more:
        line = line + ref[ref.shape[0] - 1]
    message_ref[message_ref.shape[0] - 1] = line


def pair_kernel(
    mmf_ref,
    mmo_ref,
    yf_ref,
    yo_ref,
    xf_ref,
    xo_ref,
    st_ref,
    sf_ref,
    rows_ref,
    b_ref,
    c_ref,
    ids_ref,
    other_ref,
    mine_ref,
    gf_ref,
    go_ref,
    gb_ref,
    gc_hbm,
    pair,
    gc,
    sem,
):
    length, half = mmf_ref.shape
    width = 2 * half // STEPS
    n = b_ref.shape[0]
    acc = jnp.zeros((2 * n, length), F32)
    for j in range(STEPS):
        a = j % (STEPS // 2)
        rel = slice(j * width, (j + 1) * width)
        part = slice(a * width, (a + 1) * width)
        far = j < STEPS // 2
        mm_ref, y_ref, state_ref, g_ref = (
            (mmf_ref, yf_ref, other_ref, gf_ref) if far else (mmo_ref, yo_ref, mine_ref, go_ref)
        )
        y = y_ref[:, part]
        g_ref[:, part] = rows_ref[3:4, rel] * mm_ref[:, part] + sf_ref[:, rel] * dot(st_ref[...], y)
        acc = acc + dot_nt(split2(get_half(a, n, state_ref, width) * rows_ref[0:1, rel]), y)
    pair[...] = dot_nt(yf_ref[...], xf_ref[...])
    pair[...] += dot_nt(yo_ref[...], xo_ref[...])
    keep = same_doc(ids_ref) & (iota((length, length), 0) >= iota((length, length), 1))
    masked = jnp.where(keep, pair[...], 0.0)
    hi = masked.astype(BF16)
    lo = (masked - hi.astype(F32)).astype(BF16)
    through = (acc[:n] + acc[n:]) * ids_ref[1:2, :]
    gc[...] = dot_nt(b_ref[...], hi) + dot_nt(b_ref[...], lo) + through
    copy = pltpu.make_async_copy(gc, gc_hbm, sem)
    copy.start()
    gb_ref[...] = dot(c_ref[...], hi) + dot(c_ref[...], lo)
    copy.wait()


def finish_half(first, g_ref, x_ref, sf_ref, rows_ref, bm2_ref, state_ref, gv_hbm, gv, sems):
    half = g_ref.shape[1]
    width = 2 * half // STEPS
    n = bm2_ref.shape[1] // 2
    copies = []
    acc = jnp.zeros(bm2_ref.shape, F32)
    for a in range(STEPS // 2):
        j = first + a
        rel = slice(j * width, (j + 1) * width)
        part = slice(a * width, (a + 1) * width)
        adjoint = split2(get_half(a, n, state_ref, width) * rows_ref[1:2, rel])
        gv[:, part] = g_ref[:, part] + sf_ref[:, rel] * dot(bm2_ref[...], adjoint)
        copies.append(pltpu.make_async_copy(gv.at[:, part], gv_hbm.at[:, span_of(j, width)], sems.at[a]))
        copies[a].start()
        acc = acc + dot_nt(x_ref[:, part], adjoint)
    return acc, copies


def finish_own_kernel(g_ref, x_ref, sf_ref, rows_ref, bm2_ref, mine_ref, gv_hbm, acc_ref, gv, sems):
    acc, copies = finish_half(STEPS // 2, g_ref, x_ref, sf_ref, rows_ref, bm2_ref, mine_ref, gv_hbm, gv, sems)
    acc_ref[...] = acc
    for copy in copies:
        copy.wait()


def finish_kernel(
    scale,
    _gv_in,
    g_ref,
    x_ref,
    sf_ref,
    rows_ref,
    bm2_ref,
    ids_ref,
    gb_part_ref,
    acc_ref,
    mine_ref,
    other_ref,
    gv_hbm,
    gb_hbm,
    loss_hbm,
    gv,
    gb,
    loss,
    sems,
):
    n = bm2_ref.shape[1] // 2
    last = mine_ref.shape[0] - 1
    loss[...] = jnp.broadcast_to(jnp.sum(mine_ref[last] + other_ref[last]) * scale, (1, 128))
    half = STEPS // 2
    out_loss = pltpu.make_async_copy(loss, loss_hbm, sems.at[half])
    out_loss.start()
    acc, copies = finish_half(0, g_ref, x_ref, sf_ref, rows_ref, bm2_ref, other_ref, gv_hbm, gv, sems)
    acc = acc + acc_ref[...]
    gb[...] = gb_part_ref[...] + (acc[:, :n] + acc[:, n:]).T * ids_ref[2:3, :]
    out_gb = pltpu.make_async_copy(gb, gb_hbm, sems.at[half + 1])
    out_gb.start()
    for copy in (*copies, out_loss, out_gb):
        copy.wait()


def call(kernel, ins, outs, flops=0, in_specs=None, out_specs=None, scratch=(), aliases=None):
    size = sum(a.size * a.dtype.itemsize for a in ins) + sum(o.size * o.dtype.itemsize for o in outs)
    return pl.pallas_call(
        kernel,
        out_shape=outs,
        in_specs=in_specs or [VMEM] * len(ins),
        out_specs=out_specs or [VMEM] * len(outs),
        scratch_shapes=scratch,
        input_output_aliases=aliases or {},
        compiler_params=pltpu.CompilerParams(vmem_limit_bytes=LIMIT),
        cost_estimate=pl.CostEstimate(flops=flops, bytes_accessed=size, transcendentals=0),
    )(*ins)


def out(*shape, dtype=F32):
    return jax.ShapeDtypeStruct(shape, dtype)


def swap(x, devices):
    return lax.ppermute(x, "seq", [(i, i ^ 1) for i in range(devices)])


def shift(x, by, devices):
    return lax.ppermute(
        x, "seq", [(i, i + by) for i in range(devices) if 0 <= i + by < devices]
    )


def turn(x, by, devices):
    return lax.ppermute(x, "seq", [(i, (i + by) % devices) for i in range(devices)])


def in_order(way, keep_ref, got_ref, body):
    near = odd_core() == (0 if way == 1 else 1)
    pl.when(near)(lambda: body(keep_ref, got_ref, True))
    pl.when(jnp.logical_not(near))(lambda: body(got_ref, keep_ref, False))


def columns(groups, count):
    return [(q, range(q, count, groups)) for q in range(groups)]


def compose_kernel(way, groups, keep_ref, send_ref, got_ref, packed_ref, both_ref, line_ref):
    count = both_ref.shape[0] - 1

    def body(first_ref, second_ref, _near):
        packed_ref[count] = first_ref[count] * second_ref[count]
        for q, places in columns(groups, count):
            decay = second_ref[count, q : q + 1, :]
            for t in places:
                both = second_ref[t] + decay * first_ref[t]
                packed_ref[t] = both
                both_ref[t] = both

    in_order(way, keep_ref, got_ref, body)
    line = send_ref[count + 1] + got_ref[count + 1]
    packed_ref[count + 1] = line
    both_ref[count] = line
    line_ref[...] = line


def arrive_kernel(way, groups, near_chips, keep_ref, got_ref, line_ref, one_ref, two_ref, *refs):
    more_refs, mine_ref, theirs_ref = refs[:-2], refs[-2], refs[-1]
    count = mine_ref.shape[0] - 1

    def body(first_ref, _second_ref, near):
        outer_ref, inner_ref = (mine_ref, theirs_ref) if near else (theirs_ref, mine_ref)
        for q, places in columns(groups, count):
            far_decay = one_ref[count, q : q + 1, :]
            decay = first_ref[count, q : q + 1, :]
            for t in places:
                state = one_ref[t] + far_decay * two_ref[t]
                outer_ref[t] = state
                inner_ref[t] = first_ref[t] + decay * state

    in_order(way, keep_ref, got_ref, body)
    line = jnp.zeros((8, 128), F32)
    if near_chips:
        line = line_ref[...] + one_ref[count + 1] + two_ref[count]
        line = jnp.where((odd_core() == 0).astype(F32) > 0.5, line, 0.0)
    for ref in more_refs:
        line = line + ref[...]
    mine_ref[count] = line
    theirs_ref[count] = line


def far_squares(line, devices):
    chips = devices // 2
    if chips != 8:
        return [lax.psum(line, "seq") * 0.25], False
    lines = []
    for far in range(3, chips, 2):
        pairs = [(i, (i - 2 * (far + i % 2)) % devices) for i in range(devices) if far + i % 2 < chips]
        lines.append(lax.ppermute(line, "seq", pairs))
    return lines, True


def carry(keep, send, groups, devices, way, beside):
    count = keep.shape[0] - 2
    got = swap(send, devices)
    packed, both, line = call(
        functools.partial(compose_kernel, way, groups),
        [keep, send, got],
        [out(*keep.shape), out(count + 1, 8, 128), out(8, 128)],
    )
    reach = max(1, devices // 8)
    move = shift if way == 1 else turn
    one = move(packed, 2 * way, devices)
    two = move(packed if reach > 2 else both, 4 * way, devices)
    lines, near_chips = [], False
    if way == -1:
        lines, near_chips = far_squares(line, devices)
    if reach > 2:

        def join(near, far):
            decay = near[count, :groups]
            state = near[:count].reshape(-1, groups, 8, 128) + decay[:, None, :] * far[:count].reshape(-1, groups, 8, 128)
            return jnp.concatenate([state.reshape(count, 8, 128), (near[count:] * far[count:])], axis=0)

        one = join(one, two)
        span = 2
        while span < reach:
            one = join(one, shift(one, 2 * span * way, devices))
            span *= 2
        two = jnp.zeros_like(both)
    mine, theirs = call(
        functools.partial(arrive_kernel, way, groups, near_chips),
        [keep, got, line, one, two, *lines],
        [out(count + 1, 8, 128), out(count + 1, 8, 128)],
    )
    theirs, beside = lax.optimization_barrier((theirs, beside))
    return mine, swap(theirs, devices), beside


def local(values, b_proj, c_proj, step_sizes, decay_rates, skip_gain, teacher, doc_lengths):
    length, total = values.shape
    heads = step_sizes.shape[1]
    state = b_proj.shape[1]
    devices = lax.axis_size("seq")
    b = b_proj.T
    c = c_proj.T
    groups = total // 2 // 128
    half = out(state // 8 * groups + 2, 8, 128)
    thirds = out(3 * heads, length, dtype=BF16)
    narrow = out(state, length, dtype=BF16)
    square = 2 * length * length * total
    dma = pltpu.SemaphoreType.DMA
    wide = out(length, total, dtype=BF16)
    part = out(length, total // 2)
    doubled = out(length, 2 * state, dtype=BF16)
    part16 = out(length, total // 2, dtype=BF16)
    x_far, send, enter3, sf3, f3, s3, rows, bm, cm, ids, v, teach, b, c = call(
        prepare_kernel,
        [
            pltpu.with_memory_space_constraint(a, pltpu.MemorySpace.HBM)
            for a in (
                doc_lengths,
                values,
                teacher,
                b,
                c,
                step_sizes.T,
                decay_rates.reshape(1, heads),
                skip_gain.reshape(1, heads),
            )
        ],
        [
            part16,
            half,
            thirds,
            thirds,
            thirds,
            thirds,
            out(PAD, total),
            narrow,
            narrow,
            out(PAD, length),
            wide,
            wide,
            narrow,
            narrow,
        ],
        in_specs=[HBM] * 8,
        scratch=[
            pltpu.SMEM(doc_lengths.shape, jnp.int32),
            pltpu.VMEM((heads, length), F32),
            pltpu.VMEM((1, heads), F32),
            pltpu.VMEM((1, heads), F32),
            dma((6,)),
            dma((STEPS,)),
            dma((STEPS,)),
        ],
    )
    x_own, keep = call(prepare_own_kernel, [f3, s3, bm, rows, v], [part16, half])
    inner = call(
        inner_kernel,
        [x_far, x_own, v, teach, b, c, enter3, sf3, rows, ids, bm, cm],
        [
            out(length, total),
            out(length, length, dtype=BF16),
            out(length, total),
            out(length, total),
            doubled,
            doubled,
        ],
        square,
    )
    mine, other, (base, score_t, enter, sf, bm2, cm2) = carry(keep, send, groups, devices, 1, inner)
    mm_own, y_own, keep = call(
        functools.partial(mismatch_kernel, STEPS // 2), [base, enter, rows, cm, cm2, mine], [part, part16, half]
    )
    mm_far, y_far, send = call(
        functools.partial(mismatch_kernel, 0), [base, enter, rows, cm, cm2, other, keep], [part, part16, half]
    )
    pairs = call(
        pair_kernel,
        [mm_far, mm_own, y_far, y_own, x_far, x_own, score_t, sf, rows, b, c, ids, other, mine],
        [part, part, out(state, length), out(state, length)],
        2 * square,
        out_specs=[VMEM, VMEM, VMEM, HBM],
        scratch=[pltpu.VMEM((length, length), F32), pltpu.VMEM((state, length), F32), dma],
    )
    mine, other, (g_far, g_own, gb_part, grad_c) = carry(keep, send, groups, devices, -1, pairs)
    grad_values, acc = call(
        finish_own_kernel,
        [g_own, x_own, sf, rows, bm2, mine],
        [out(length, total), out(length, 2 * state)],
        out_specs=[HBM, VMEM],
        scratch=[pltpu.VMEM((length, total // 2), F32), dma((STEPS // 2,))],
    )
    scale = 1.0 / (devices * length * total)
    grad_values, grad_b, loss = call(
        functools.partial(finish_kernel, scale),
        [grad_values, g_far, x_far, sf, rows, bm2, ids, gb_part, acc, mine, other],
        [out(length, total), out(state, length), out(1, 128)],
        in_specs=[HBM] + [VMEM] * 10,
        out_specs=[HBM, HBM, HBM],
        scratch=[
            pltpu.VMEM((length, total // 2), F32),
            pltpu.VMEM((state, length), F32),
            pltpu.VMEM((1, 128), F32),
            dma((STEPS // 2 + 2,)),
        ],
        aliases={0: 0},
    )
    return loss[0, :1], grad_values, grad_b.T, grad_c.T


def solution(mesh):
    rows = P(("groups", "seq"), None)
    in_specs = (rows, rows, rows, rows, P(), P(), rows, P("groups"))
    out_specs = (P("groups"), rows, rows, rows)
    return jax.shard_map(local, mesh=mesh, in_specs=in_specs, out_specs=out_specs, check_vma=False)
```

```python
import functools
import jax
import jax.numpy as jnp
from jax import lax
from jax.experimental import pallas as pl
from jax.experimental.pallas import tpu as pltpu
from jax.sharding import PartitionSpec as P

F32 = jnp.float32
BF16 = jnp.bfloat16
PAD = 8
STEPS = 2
PIECES = 2
LIMIT = 24 << 20
HBM = pl.BlockSpec(memory_space=pltpu.MemorySpace.HBM)
VMEM = pl.BlockSpec(memory_space=pltpu.MemorySpace.VMEM)


def dot(a, b):
    return jnp.dot(a, b, preferred_element_type=F32)


def dot_nt(a, b):
    return lax.dot_general(a, b, (((1,), (1,)), ((), ())), preferred_element_type=F32)


def dot_tn(a, b):
    return lax.dot_general(a, b, (((0,), (0,)), ((), ())), preferred_element_type=F32)


def iota(shape, axis):
    return lax.broadcasted_iota(jnp.int32, shape, axis)


def split3(x):
    hi = x.astype(BF16)
    rest = x - hi.astype(F32)
    mid = rest.astype(BF16)
    lo = (rest - mid.astype(F32)).astype(BF16)
    return jnp.concatenate([hi, mid, lo], axis=0)


def split2(x):
    hi = x.astype(BF16)
    lo = (x - hi.astype(F32)).astype(BF16)
    return jnp.concatenate([hi, lo], axis=0)


def twice(x):
    return jnp.concatenate([x, x], axis=0)


def chunk_of(j):
    half = STEPS // 2
    return jnp.where(odd_core() == 0, (j + half) % STEPS, j)


def span_of(j, width):
    return pl.ds(pl.multiple_of(chunk_of(j) * width, width), width)


def expander(heads, head_dim, width, j):
    rows = lax.rem(iota((3 * heads, width), 0), heads)
    cols = iota((3 * heads, width), 1) // head_dim + chunk_of(j) * (width // head_dim)
    return (rows == cols).astype(F32).astype(BF16)


def column(row):
    n = row.shape[1]
    return jnp.sum(jnp.where(iota((n, n), 0) == iota((n, n), 1), row, 0.0), axis=1, keepdims=True)


def tall(row):
    return jnp.broadcast_to(row, (128, row.shape[1])).T


def same_doc(ids_ref):
    ids = ids_ref[0:1, :]
    return tall(ids)[:, 0:1] == ids


def odd_core():
    return lax.rem(lax.axis_index("seq"), 2)


def put_half(a, ref, state, decay):
    rows, width = state.shape
    groups = ref.shape[0] // (rows // 8)
    for q in range(width // 128):
        g = a * (width // 128) + q
        cols = slice(q * 128, (q + 1) * 128)
        for r in range(rows // 8):
            ref[r * groups + g] = state[r * 8 : (r + 1) * 8, cols]
        ref[groups * (rows // 8), g : g + 1, :] = decay[:, cols]


def get_half(a, rows, ref, width):
    groups = ref.shape[0] // (rows // 8)
    inside = range(a * (width // 128), (a + 1) * (width // 128))
    return jnp.concatenate(
        [jnp.concatenate([ref[r * groups + g] for g in inside], axis=1) for r in range(rows // 8)], axis=0
    )


def state_half(first, f3, s3, bm, rows_ref, v_ref, x_ref, message_ref, heads):
    total = v_ref.shape[1]
    width = total // STEPS
    for a in range(STEPS // 2):
        j = first + a
        rel = slice(j * width, (j + 1) * width)
        spread = expander(heads, total // heads, width, j)
        scaled = (dot_tn(s3, spread) * v_ref[:, rel].astype(F32)).astype(BF16).astype(F32)
        x = dot_tn(f3, spread) * scaled
        hi = x.astype(BF16)
        x_ref[:, a * width : (a + 1) * width] = hi
        state = dot(bm, hi) * rows_ref[1:2, rel]
        put_half(a, message_ref, state, rows_ref[2:3, rel])
    message_ref[message_ref.shape[0] - 1] = jnp.zeros((8, 128), F32)


def prepare_kernel(
    lengths_hbm,
    v_hbm,
    teach_hbm,
    b_hbm,
    c_hbm,
    step_hbm,
    rate_hbm,
    gain_hbm,
    x_ref,
    send_ref,
    enter3_ref,
    sf3_ref,
    f3_ref,
    s3_ref,
    rows_ref,
    bm_ref,
    cm_ref,
    ids_ref,
    v,
    teach,
    b,
    c,
    lengths,
    step,
    rate,
    gain,
    sems,
    v_sems,
    t_sems,
):
    heads, length = step.shape
    total = v.shape[1]
    width = total // STEPS
    small = [(step_hbm, step), (rate_hbm, rate), (gain_hbm, gain), (lengths_hbm, lengths), (b_hbm, b), (c_hbm, c)]
    small = [pltpu.make_async_copy(src, dst, sems.at[i]) for i, (src, dst) in enumerate(small)]
    large = []
    for src, dst, sem in ((v_hbm, v, v_sems), (teach_hbm, teach, t_sems)):
        for j in range(STEPS):
            rel = slice(j * width, (j + 1) * width)
            large.append(pltpu.make_async_copy(src.at[:, span_of(j, width)], dst.at[:, rel], sem.at[j]))
    for copy in small + large:
        copy.start()
    upper = (iota((length, length), 0) <= iota((length, length), 1)).astype(F32).astype(BF16)
    for copy in small:
        copy.wait()
    sums = dot(split3(-(step[...] * column(rate[...]))), upper)
    level = sums[:heads] + sums[heads : 2 * heads] + sums[2 * heads :]
    middle = level[:, length // 2 - 1 : length // 2]
    last = level[:, length - 1 : length]
    place = iota((1, length), 1)
    ids = jnp.zeros((1, length), jnp.int32)
    before = jnp.int32(0)
    final = jnp.int32(0)
    start = -lax.axis_index("seq") * length
    for d in range(lengths.shape[0]):
        ids = ids + (place >= start).astype(jnp.int32)
        before = before + (start <= -1).astype(jnp.int32)
        final = final + (start <= length - 1).astype(jnp.int32)
        start = start + lengths[d]
    first_doc = (ids == before).astype(F32)
    last_doc = (ids == final).astype(F32)
    ids_ref[0:1, :] = ids.astype(F32)
    ids_ref[1:2, :] = first_doc
    ids_ref[2:3, :] = last_doc
    leave = jnp.exp(middle - level)
    enter3_ref[...] = split3(jnp.exp(level - middle))
    f3 = split3(leave)
    s3 = split3(step[...])
    f3_ref[...] = f3
    s3_ref[...] = s3
    sf3_ref[...] = split3(step[...] * leave)
    through = jnp.where(before == final, jnp.exp(last), 0.0)
    pick = iota((heads, 128), 1)
    table = jnp.where(pick == 0, jnp.exp(middle), 0.0)
    table = jnp.where(pick == 1, jnp.exp(last - middle), table)
    table = jnp.where(pick == 2, through, table)
    table = jnp.where(pick == 3, column(gain[...]), table)
    r3 = split3(table)
    for j in range(STEPS):
        spread = expander(heads, total // heads, width, j)
        rows_ref[:, j * width : (j + 1) * width] = dot_tn(r3, spread)[:PAD]
    bm = (b[...].astype(F32) * last_doc).astype(BF16)
    bm_ref[...] = bm
    cm_ref[...] = (c[...].astype(F32) * first_doc).astype(BF16)
    for copy in large[: STEPS // 2]:
        copy.wait()
    state_half(0, f3, s3, bm, rows_ref, v, x_ref, send_ref, heads)
    for copy in large[STEPS // 2 :]:
        copy.wait()


def prepare_own_kernel(f3_ref, s3_ref, bm_ref, rows_ref, v_ref, x_ref, keep_ref):
    state_half(
        STEPS // 2, f3_ref[...], s3_ref[...], bm_ref[...], rows_ref, v_ref, x_ref, keep_ref, f3_ref.shape[0] // 3
    )


def inner_kernel(
    xf_ref,
    xo_ref,
    v_ref,
    teach_ref,
    b_ref,
    c_ref,
    enter3_ref,
    sf3_ref,
    rows_ref,
    ids_ref,
    bm_ref,
    cm_ref,
    base_ref,
    st_ref,
    enter_ref,
    sf_ref,
    bm2_ref,
    cm2_ref,
):
    length, total = base_ref.shape
    width = total // STEPS
    heads = enter3_ref.shape[0] // 3
    bm2_ref[...] = twice(bm_ref[...].astype(F32)).T.astype(BF16)
    cm2_ref[...] = twice(cm_ref[...].astype(F32)).T.astype(BF16)
    same = same_doc(ids_ref)
    down = iota((length, length), 0)
    along = iota((length, length), 1)
    s = jnp.where(same & (down >= along), dot_tn(c_ref[...], b_ref[...]), 0.0).astype(BF16)
    st_ref[...] = jnp.where(same & (down <= along), dot_tn(b_ref[...], c_ref[...]), 0.0).astype(BF16)
    for j in range(STEPS):
        rel = slice(j * width, (j + 1) * width)
        a = j % (STEPS // 2)
        x_ref = xf_ref if j < STEPS // 2 else xo_ref
        spread = expander(heads, total // heads, width, j)
        enter = dot_tn(enter3_ref[...], spread)
        enter_ref[:, rel] = enter
        sf_ref[:, rel] = dot_tn(sf3_ref[...], spread)
        base_ref[:, rel] = (
            enter * dot(s, x_ref[:, a * width : (a + 1) * width])
            + rows_ref[3:4, rel] * v_ref[:, rel].astype(F32)
            - teach_ref[:, rel].astype(F32)
        )


def mismatch_kernel(first, base_ref, enter_ref, rows_ref, cm_ref, cm2_ref, state_ref, *refs):
    more, (mm_ref, y_ref, message_ref) = refs[:-3], refs[-3:]
    length, total = base_ref.shape
    width = total // STEPS
    cm = cm_ref[...]
    sums = jnp.zeros((8, width), F32)
    for a in range(STEPS // 2):
        j = first + a
        rel = slice(j * width, (j + 1) * width)
        part = slice(a * width, (a + 1) * width)
        enter = enter_ref[:, rel]
        state = split2(get_half(a, cm.shape[0], state_ref, width) * rows_ref[0:1, rel])
        mm = base_ref[:, rel] + enter * dot(cm2_ref[...], state)
        mm_ref[:, part] = mm
        y = (enter * mm).astype(BF16)
        y_ref[:, part] = y
        sums = sums + jnp.sum((mm * mm).reshape(length // 8, 8, width), axis=0)
        put_half(a, message_ref, dot(cm, y) * rows_ref[0:1, rel], rows_ref[2:3, rel])
    line = sums[:, :128]
    for q in range(1, width // 128):
        line = line + sums[:, q * 128 : (q + 1) * 128]
    for ref in more:
        line = line + ref[ref.shape[0] - 1]
    message_ref[message_ref.shape[0] - 1] = line


def pair_kernel(
    mmf_ref,
    mmo_ref,
    yf_ref,
    yo_ref,
    xf_ref,
    xo_ref,
    st_ref,
    sf_ref,
    rows_ref,
    b_ref,
    c_ref,
    ids_ref,
    other_ref,
    mine_ref,
    gf_ref,
    go_ref,
    gb_ref,
    gc_hbm,
    pair,
    gc,
    sem,
):
    length, half = mmf_ref.shape
    width = 2 * half // STEPS
    n = b_ref.shape[0]
    acc = jnp.zeros((2 * n, length), F32)
    for j in range(STEPS):
        a = j % (STEPS // 2)
        rel = slice(j * width, (j + 1) * width)
        part = slice(a * width, (a + 1) * width)
        far = j < STEPS // 2
        mm_ref, y_ref, state_ref, g_ref = (
            (mmf_ref, yf_ref, other_ref, gf_ref) if far else (mmo_ref, yo_ref, mine_ref, go_ref)
        )
        y = y_ref[:, part]
        g_ref[:, part] = rows_ref[3:4, rel] * mm_ref[:, part] + sf_ref[:, rel] * dot(st_ref[...], y)
        acc = acc + dot_nt(split2(get_half(a, n, state_ref, width) * rows_ref[0:1, rel]), y)
    pair[...] = dot_nt(yf_ref[...], xf_ref[...])
    pair[...] += dot_nt(yo_ref[...], xo_ref[...])
    keep = same_doc(ids_ref) & (iota((length, length), 0) >= iota((length, length), 1))
    masked = jnp.where(keep, pair[...], 0.0)
    hi = masked.astype(BF16)
    lo = (masked - hi.astype(F32)).astype(BF16)
    through = (acc[:n] + acc[n:]) * ids_ref[1:2, :]
    gc[...] = dot_nt(b_ref[...], hi) + dot_nt(b_ref[...], lo) + through
    copy = pltpu.make_async_copy(gc, gc_hbm, sem)
    copy.start()
    gb_ref[...] = dot(c_ref[...], hi) + dot(c_ref[...], lo)
    copy.wait()


def finish_half(first, g_ref, x_ref, sf_ref, rows_ref, bm2_ref, state_ref, gv_hbm, gv, sems):
    half = g_ref.shape[1]
    width = 2 * half // STEPS
    piece = width // PIECES
    n = bm2_ref.shape[1] // 2
    copies = []
    acc = jnp.zeros(bm2_ref.shape, F32)
    for a in range(STEPS // 2):
        j = first + a
        rel = slice(j * width, (j + 1) * width)
        adjoint = split2(get_half(a, n, state_ref, width) * rows_ref[1:2, rel])
        for k in range(PIECES):
            part = slice(a * width + k * piece, a * width + (k + 1) * piece)
            near = slice(j * width + k * piece, j * width + (k + 1) * piece)
            gv[:, part] = g_ref[:, part] + sf_ref[:, near] * dot(
                bm2_ref[...], adjoint[:, k * piece : (k + 1) * piece]
            )
            place = pl.ds(pl.multiple_of(chunk_of(j) * width + k * piece, piece), piece)
            copies.append(pltpu.make_async_copy(gv.at[:, part], gv_hbm.at[:, place], sems.at[a * PIECES + k]))
            copies[-1].start()
        acc = acc + dot_nt(x_ref[:, a * width : (a + 1) * width], adjoint)
    return acc, copies


def finish_own_kernel(g_ref, x_ref, sf_ref, rows_ref, bm2_ref, mine_ref, gv_hbm, acc_ref, gv, sems):
    acc, copies = finish_half(STEPS // 2, g_ref, x_ref, sf_ref, rows_ref, bm2_ref, mine_ref, gv_hbm, gv, sems)
    acc_ref[...] = acc
    for copy in copies:
        copy.wait()


def finish_kernel(
    scale,
    _gv_in,
    g_ref,
    x_ref,
    sf_ref,
    rows_ref,
    bm2_ref,
    ids_ref,
    gb_part_ref,
    acc_ref,
    mine_ref,
    other_ref,
    gv_hbm,
    gb_hbm,
    loss_hbm,
    gv,
    gb,
    loss,
    sems,
):
    n = bm2_ref.shape[1] // 2
    last = mine_ref.shape[0] - 1
    loss[...] = jnp.broadcast_to(jnp.sum(mine_ref[last] + other_ref[last]) * scale, (1, 128))
    half = STEPS // 2 * PIECES
    out_loss = pltpu.make_async_copy(loss, loss_hbm, sems.at[half])
    out_loss.start()
    acc, copies = finish_half(0, g_ref, x_ref, sf_ref, rows_ref, bm2_ref, other_ref, gv_hbm, gv, sems)
    acc = acc + acc_ref[...]
    gb[...] = gb_part_ref[...] + (acc[:, :n] + acc[:, n:]).T * ids_ref[2:3, :]
    out_gb = pltpu.make_async_copy(gb, gb_hbm, sems.at[half + 1])
    out_gb.start()
    for copy in (*copies, out_loss, out_gb):
        copy.wait()


def call(kernel, ins, outs, flops=0, in_specs=None, out_specs=None, scratch=(), aliases=None):
    size = sum(a.size * a.dtype.itemsize for a in ins) + sum(o.size * o.dtype.itemsize for o in outs)
    return pl.pallas_call(
        kernel,
        out_shape=outs,
        in_specs=in_specs or [VMEM] * len(ins),
        out_specs=out_specs or [VMEM] * len(outs),
        scratch_shapes=scratch,
        input_output_aliases=aliases or {},
        compiler_params=pltpu.CompilerParams(vmem_limit_bytes=LIMIT),
        cost_estimate=pl.CostEstimate(flops=flops, bytes_accessed=size, transcendentals=0),
    )(*ins)


def out(*shape, dtype=F32):
    return jax.ShapeDtypeStruct(shape, dtype)


def swap(x, devices):
    return lax.ppermute(x, "seq", [(i, i ^ 1) for i in range(devices)])


def shift(x, by, devices):
    return lax.ppermute(
        x, "seq", [(i, i + by) for i in range(devices) if 0 <= i + by < devices]
    )


def turn(x, by, devices):
    return lax.ppermute(x, "seq", [(i, (i + by) % devices) for i in range(devices)])


def in_order(way, keep_ref, got_ref, body):
    near = odd_core() == (0 if way == 1 else 1)
    pl.when(near)(lambda: body(keep_ref, got_ref, True))
    pl.when(jnp.logical_not(near))(lambda: body(got_ref, keep_ref, False))


def columns(groups, count):
    return [(q, range(q, count, groups)) for q in range(groups)]


def compose_kernel(way, groups, keep_ref, send_ref, got_ref, packed_ref, both_ref, line_ref):
    count = both_ref.shape[0] - 1

    def body(first_ref, second_ref, _near):
        packed_ref[count] = first_ref[count] * second_ref[count]
        for q, places in columns(groups, count):
            decay = second_ref[count, q : q + 1, :]
            for t in places:
                both = second_ref[t] + decay * first_ref[t]
                packed_ref[t] = both
                both_ref[t] = both

    in_order(way, keep_ref, got_ref, body)
    line = send_ref[count + 1] + got_ref[count + 1]
    packed_ref[count + 1] = line
    both_ref[count] = line
    line_ref[...] = line


def arrive_kernel(way, groups, near_chips, keep_ref, got_ref, line_ref, one_ref, two_ref, *refs):
    more_refs, mine_ref, theirs_ref = refs[:-2], refs[-2], refs[-1]
    count = mine_ref.shape[0] - 1

    def body(first_ref, _second_ref, near):
        outer_ref, inner_ref = (mine_ref, theirs_ref) if near else (theirs_ref, mine_ref)
        for q, places in columns(groups, count):
            far_decay = one_ref[count, q : q + 1, :]
            decay = first_ref[count, q : q + 1, :]
            for t in places:
                state = one_ref[t] + far_decay * two_ref[t]
                outer_ref[t] = state
                inner_ref[t] = first_ref[t] + decay * state

    in_order(way, keep_ref, got_ref, body)
    line = jnp.zeros((8, 128), F32)
    if near_chips:
        line = line_ref[...] + one_ref[count + 1] + two_ref[count]
        line = jnp.where((odd_core() == 0).astype(F32) > 0.5, line, 0.0)
    for ref in more_refs:
        line = line + ref[...]
    mine_ref[count] = line
    theirs_ref[count] = line


def far_squares(line, devices):
    chips = devices // 2
    if chips != 8:
        return [lax.psum(line, "seq") * 0.25], False
    lines = []
    for far in range(3, chips, 2):
        pairs = [(i, (i - 2 * (far + i % 2)) % devices) for i in range(devices) if far + i % 2 < chips]
        lines.append(lax.ppermute(line, "seq", pairs))
    return lines, True


def carry(keep, send, groups, devices, way, beside):
    count = keep.shape[0] - 2
    got = swap(send, devices)
    packed, both, line = call(
        functools.partial(compose_kernel, way, groups),
        [keep, send, got],
        [out(*keep.shape), out(count + 1, 8, 128), out(8, 128)],
    )
    reach = max(1, devices // 8)
    move = shift if way == 1 else turn
    one = move(packed, 2 * way, devices)
    two = move(packed if reach > 2 else both, 4 * way, devices)
    lines, near_chips = [], False
    if way == -1:
        lines, near_chips = far_squares(line, devices)
    if reach > 2:

        def join(near, far):
            decay = near[count, :groups]
            state = near[:count].reshape(-1, groups, 8, 128) + decay[:, None, :] * far[:count].reshape(-1, groups, 8, 128)
            return jnp.concatenate([state.reshape(count, 8, 128), (near[count:] * far[count:])], axis=0)

        one = join(one, two)
        span = 2
        while span < reach:
            one = join(one, shift(one, 2 * span * way, devices))
            span *= 2
        two = jnp.zeros_like(both)
    mine, theirs = call(
        functools.partial(arrive_kernel, way, groups, near_chips),
        [keep, got, line, one, two, *lines],
        [out(count + 1, 8, 128), out(count + 1, 8, 128)],
    )
    theirs, beside = lax.optimization_barrier((theirs, beside))
    return mine, swap(theirs, devices), beside


def local(values, b_proj, c_proj, step_sizes, decay_rates, skip_gain, teacher, doc_lengths):
    length, total = values.shape
    heads = step_sizes.shape[1]
    state = b_proj.shape[1]
    devices = lax.axis_size("seq")
    b = b_proj.T
    c = c_proj.T
    groups = total // 2 // 128
    half = out(state // 8 * groups + 2, 8, 128)
    thirds = out(3 * heads, length, dtype=BF16)
    narrow = out(state, length, dtype=BF16)
    square = 2 * length * length * total
    dma = pltpu.SemaphoreType.DMA
    wide = out(length, total, dtype=BF16)
    part = out(length, total // 2)
    doubled = out(length, 2 * state, dtype=BF16)
    part16 = out(length, total // 2, dtype=BF16)
    x_far, send, enter3, sf3, f3, s3, rows, bm, cm, ids, v, teach, b, c = call(
        prepare_kernel,
        [
            pltpu.with_memory_space_constraint(a, pltpu.MemorySpace.HBM)
            for a in (
                doc_lengths,
                values,
                teacher,
                b,
                c,
                step_sizes.T,
                decay_rates.reshape(1, heads),
                skip_gain.reshape(1, heads),
            )
        ],
        [
            part16,
            half,
            thirds,
            thirds,
            thirds,
            thirds,
            out(PAD, total),
            narrow,
            narrow,
            out(PAD, length),
            wide,
            wide,
            narrow,
            narrow,
        ],
        in_specs=[HBM] * 8,
        scratch=[
            pltpu.SMEM(doc_lengths.shape, jnp.int32),
            pltpu.VMEM((heads, length), F32),
            pltpu.VMEM((1, heads), F32),
            pltpu.VMEM((1, heads), F32),
            dma((6,)),
            dma((STEPS,)),
            dma((STEPS,)),
        ],
    )
    x_own, keep = call(prepare_own_kernel, [f3, s3, bm, rows, v], [part16, half])
    inner = call(
        inner_kernel,
        [x_far, x_own, v, teach, b, c, enter3, sf3, rows, ids, bm, cm],
        [
            out(length, total),
            out(length, length, dtype=BF16),
            out(length, total),
            out(length, total),
            doubled,
            doubled,
        ],
        square,
    )
    mine, other, (base, score_t, enter, sf, bm2, cm2) = carry(keep, send, groups, devices, 1, inner)
    mm_own, y_own, keep = call(
        functools.partial(mismatch_kernel, STEPS // 2), [base, enter, rows, cm, cm2, mine], [part, part16, half]
    )
    mm_far, y_far, send = call(
        functools.partial(mismatch_kernel, 0), [base, enter, rows, cm, cm2, other, keep], [part, part16, half]
    )
    pairs = call(
        pair_kernel,
        [mm_far, mm_own, y_far, y_own, x_far, x_own, score_t, sf, rows, b, c, ids, other, mine],
        [part, part, out(state, length), out(state, length)],
        2 * square,
        out_specs=[VMEM, VMEM, VMEM, HBM],
        scratch=[pltpu.VMEM((length, length), F32), pltpu.VMEM((state, length), F32), dma],
    )
    mine, other, (g_far, g_own, gb_part, grad_c) = carry(keep, send, groups, devices, -1, pairs)
    grad_values, acc = call(
        finish_own_kernel,
        [g_own, x_own, sf, rows, bm2, mine],
        [out(length, total), out(length, 2 * state)],
        out_specs=[HBM, VMEM],
        scratch=[pltpu.VMEM((length, total // 2), F32), dma((STEPS // 2 * PIECES,))],
    )
    scale = 1.0 / (devices * length * total)
    grad_values, grad_b, loss = call(
        functools.partial(finish_kernel, scale),
        [grad_values, g_far, x_far, sf, rows, bm2, ids, gb_part, acc, mine, other],
        [out(length, total), out(state, length), out(1, 128)],
        in_specs=[HBM] + [VMEM] * 10,
        out_specs=[HBM, HBM, HBM],
        scratch=[
            pltpu.VMEM((length, total // 2), F32),
            pltpu.VMEM((state, length), F32),
            pltpu.VMEM((1, 128), F32),
            dma((STEPS // 2 * PIECES + 2,)),
        ],
        aliases={0: 0},
    )
    return loss[0, :1], grad_values, grad_b.T, grad_c.T


def solution(mesh):
    rows = P(("groups", "seq"), None)
    in_specs = (rows, rows, rows, rows, P(), P(), rows, P("groups"))
    out_specs = (P("groups"), rows, rows, rows)
    return jax.shard_map(local, mesh=mesh, in_specs=in_specs, out_specs=out_specs, check_vma=False)
```

```python
import functools
import jax
import jax.numpy as jnp
from jax import lax
from jax.experimental import pallas as pl
from jax.experimental.pallas import tpu as pltpu
from jax.sharding import PartitionSpec as P

F32 = jnp.float32
BF16 = jnp.bfloat16
PAD = 8
STEPS = 2
PIECES = 4
LIMIT = 24 << 20
HBM = pl.BlockSpec(memory_space=pltpu.MemorySpace.HBM)
VMEM = pl.BlockSpec(memory_space=pltpu.MemorySpace.VMEM)


def dot(a, b):
    return jnp.dot(a, b, preferred_element_type=F32)


def dot_nt(a, b):
    return lax.dot_general(a, b, (((1,), (1,)), ((), ())), preferred_element_type=F32)


def dot_tn(a, b):
    return lax.dot_general(a, b, (((0,), (0,)), ((), ())), preferred_element_type=F32)


def iota(shape, axis):
    return lax.broadcasted_iota(jnp.int32, shape, axis)


def split3(x):
    hi = x.astype(BF16)
    rest = x - hi.astype(F32)
    mid = rest.astype(BF16)
    lo = (rest - mid.astype(F32)).astype(BF16)
    return jnp.concatenate([hi, mid, lo], axis=0)


def split2(x):
    hi = x.astype(BF16)
    lo = (x - hi.astype(F32)).astype(BF16)
    return jnp.concatenate([hi, lo], axis=0)


def twice(x):
    return jnp.concatenate([x, x], axis=0)


def chunk_of(j):
    half = STEPS // 2
    return jnp.where(odd_core() == 0, (j + half) % STEPS, j)


def span_of(j, width):
    return pl.ds(pl.multiple_of(chunk_of(j) * width, width), width)


def expander(heads, head_dim, width, j):
    rows = lax.rem(iota((3 * heads, width), 0), heads)
    cols = iota((3 * heads, width), 1) // head_dim + chunk_of(j) * (width // head_dim)
    return (rows == cols).astype(F32).astype(BF16)


def column(row):
    n = row.shape[1]
    return jnp.sum(jnp.where(iota((n, n), 0) == iota((n, n), 1), row, 0.0), axis=1, keepdims=True)


def tall(row):
    return jnp.broadcast_to(row, (128, row.shape[1])).T


def same_doc(ids_ref):
    ids = ids_ref[0:1, :]
    return tall(ids)[:, 0:1] == ids


def odd_core():
    return lax.rem(lax.axis_index("seq"), 2)


def put_half(a, ref, state, decay):
    rows, width = state.shape
    groups = ref.shape[0] // (rows // 8)
    for q in range(width // 128):
        g = a * (width // 128) + q
        cols = slice(q * 128, (q + 1) * 128)
        for r in range(rows // 8):
            ref[r * groups + g] = state[r * 8 : (r + 1) * 8, cols]
        ref[groups * (rows // 8), g : g + 1, :] = decay[:, cols]


def get_half(a, rows, ref, width):
    groups = ref.shape[0] // (rows // 8)
    inside = range(a * (width // 128), (a + 1) * (width // 128))
    return jnp.concatenate(
        [jnp.concatenate([ref[r * groups + g] for g in inside], axis=1) for r in range(rows // 8)], axis=0
    )


def state_half(first, f3, s3, bm, rows_ref, v_ref, x_ref, message_ref, heads):
    total = v_ref.shape[1]
    width = total // STEPS
    for a in range(STEPS // 2):
        j = first + a
        rel = slice(j * width, (j + 1) * width)
        spread = expander(heads, total // heads, width, j)
        scaled = (dot_tn(s3, spread) * v_ref[:, rel].astype(F32)).astype(BF16).astype(F32)
        x = dot_tn(f3, spread) * scaled
        hi = x.astype(BF16)
        x_ref[:, a * width : (a + 1) * width] = hi
        state = dot(bm, hi) * rows_ref[1:2, rel]
        put_half(a, message_ref, state, rows_ref[2:3, rel])
    message_ref[message_ref.shape[0] - 1] = jnp.zeros((8, 128), F32)


def prepare_kernel(
    lengths_hbm,
    v_hbm,
    teach_hbm,
    b_hbm,
    c_hbm,
    step_hbm,
    rate_hbm,
    gain_hbm,
    x_ref,
    send_ref,
    enter3_ref,
    sf3_ref,
    f3_ref,
    s3_ref,
    rows_ref,
    bm_ref,
    cm_ref,
    ids_ref,
    v,
    teach,
    b,
    c,
    lengths,
    step,
    rate,
    gain,
    sems,
    v_sems,
    t_sems,
):
    heads, length = step.shape
    total = v.shape[1]
    width = total // STEPS
    small = [(step_hbm, step), (rate_hbm, rate), (gain_hbm, gain), (lengths_hbm, lengths), (b_hbm, b), (c_hbm, c)]
    small = [pltpu.make_async_copy(src, dst, sems.at[i]) for i, (src, dst) in enumerate(small)]
    large = []
    for src, dst, sem in ((v_hbm, v, v_sems), (teach_hbm, teach, t_sems)):
        for j in range(STEPS):
            rel = slice(j * width, (j + 1) * width)
            large.append(pltpu.make_async_copy(src.at[:, span_of(j, width)], dst.at[:, rel], sem.at[j]))
    for copy in small + large:
        copy.start()
    upper = (iota((length, length), 0) <= iota((length, length), 1)).astype(F32).astype(BF16)
    for copy in small:
        copy.wait()
    sums = dot(split3(-(step[...] * column(rate[...]))), upper)
    level = sums[:heads] + sums[heads : 2 * heads] + sums[2 * heads :]
    middle = level[:, length // 2 - 1 : length // 2]
    last = level[:, length - 1 : length]
    place = iota((1, length), 1)
    ids = jnp.zeros((1, length), jnp.int32)
    before = jnp.int32(0)
    final = jnp.int32(0)
    start = -lax.axis_index("seq") * length
    for d in range(lengths.shape[0]):
        ids = ids + (place >= start).astype(jnp.int32)
        before = before + (start <= -1).astype(jnp.int32)
        final = final + (start <= length - 1).astype(jnp.int32)
        start = start + lengths[d]
    first_doc = (ids == before).astype(F32)
    last_doc = (ids == final).astype(F32)
    ids_ref[0:1, :] = ids.astype(F32)
    ids_ref[1:2, :] = first_doc
    ids_ref[2:3, :] = last_doc
    leave = jnp.exp(middle - level)
    enter3_ref[...] = split3(jnp.exp(level - middle))
    f3 = split3(leave)
    s3 = split3(step[...])
    f3_ref[...] = f3
    s3_ref[...] = s3
    sf3_ref[...] = split3(step[...] * leave)
    through = jnp.where(before == final, jnp.exp(last), 0.0)
    pick = iota((heads, 128), 1)
    table = jnp.where(pick == 0, jnp.exp(middle), 0.0)
    table = jnp.where(pick == 1, jnp.exp(last - middle), table)
    table = jnp.where(pick == 2, through, table)
    table = jnp.where(pick == 3, column(gain[...]), table)
    r3 = split3(table)
    for j in range(STEPS):
        spread = expander(heads, total // heads, width, j)
        rows_ref[:, j * width : (j + 1) * width] = dot_tn(r3, spread)[:PAD]
    bm = (b[...].astype(F32) * last_doc).astype(BF16)
    bm_ref[...] = bm
    cm_ref[...] = (c[...].astype(F32) * first_doc).astype(BF16)
    for copy in large[: STEPS // 2]:
        copy.wait()
    state_half(0, f3, s3, bm, rows_ref, v, x_ref, send_ref, heads)
    for copy in large[STEPS // 2 :]:
        copy.wait()


def prepare_own_kernel(f3_ref, s3_ref, bm_ref, rows_ref, v_ref, x_ref, keep_ref):
    state_half(
        STEPS // 2, f3_ref[...], s3_ref[...], bm_ref[...], rows_ref, v_ref, x_ref, keep_ref, f3_ref.shape[0] // 3
    )


def inner_kernel(
    xf_ref,
    xo_ref,
    v_ref,
    teach_ref,
    b_ref,
    c_ref,
    enter3_ref,
    sf3_ref,
    rows_ref,
    ids_ref,
    bm_ref,
    cm_ref,
    base_ref,
    st_ref,
    enter_ref,
    sf_ref,
    bm2_ref,
    cm2_ref,
):
    length, total = base_ref.shape
    width = total // STEPS
    heads = enter3_ref.shape[0] // 3
    bm2_ref[...] = twice(bm_ref[...].astype(F32)).T.astype(BF16)
    cm2_ref[...] = twice(cm_ref[...].astype(F32)).T.astype(BF16)
    same = same_doc(ids_ref)
    down = iota((length, length), 0)
    along = iota((length, length), 1)
    s = jnp.where(same & (down >= along), dot_tn(c_ref[...], b_ref[...]), 0.0).astype(BF16)
    st_ref[...] = jnp.where(same & (down <= along), dot_tn(b_ref[...], c_ref[...]), 0.0).astype(BF16)
    for j in range(STEPS):
        rel = slice(j * width, (j + 1) * width)
        a = j % (STEPS // 2)
        x_ref = xf_ref if j < STEPS // 2 else xo_ref
        spread = expander(heads, total // heads, width, j)
        enter = dot_tn(enter3_ref[...], spread)
        enter_ref[:, rel] = enter
        sf_ref[:, rel] = dot_tn(sf3_ref[...], spread)
        base_ref[:, rel] = (
            enter * dot(s, x_ref[:, a * width : (a + 1) * width])
            + rows_ref[3:4, rel] * v_ref[:, rel].astype(F32)
            - teach_ref[:, rel].astype(F32)
        )


def mismatch_kernel(first, base_ref, enter_ref, rows_ref, cm_ref, cm2_ref, state_ref, *refs):
    more, (mm_ref, y_ref, message_ref) = refs[:-3], refs[-3:]
    length, total = base_ref.shape
    width = total // STEPS
    cm = cm_ref[...]
    sums = jnp.zeros((8, width), F32)
    for a in range(STEPS // 2):
        j = first + a
        rel = slice(j * width, (j + 1) * width)
        part = slice(a * width, (a + 1) * width)
        enter = enter_ref[:, rel]
        state = split2(get_half(a, cm.shape[0], state_ref, width) * rows_ref[0:1, rel])
        mm = base_ref[:, rel] + enter * dot(cm2_ref[...], state)
        mm_ref[:, part] = mm
        y = (enter * mm).astype(BF16)
        y_ref[:, part] = y
        sums = sums + jnp.sum((mm * mm).reshape(length // 8, 8, width), axis=0)
        put_half(a, message_ref, dot(cm, y) * rows_ref[0:1, rel], rows_ref[2:3, rel])
    line = sums[:, :128]
    for q in range(1, width // 128):
        line = line + sums[:, q * 128 : (q + 1) * 128]
    for ref in more:
        line = line + ref[ref.shape[0] - 1]
    message_ref[message_ref.shape[0] - 1] = line


def pair_kernel(
    mmf_ref,
    mmo_ref,
    yf_ref,
    yo_ref,
    xf_ref,
    xo_ref,
    st_ref,
    sf_ref,
    rows_ref,
    b_ref,
    c_ref,
    ids_ref,
    other_ref,
    mine_ref,
    gf_ref,
    go_ref,
    gb_ref,
    gc_hbm,
    pair,
    gc,
    sem,
):
    length, half = mmf_ref.shape
    width = 2 * half // STEPS
    n = b_ref.shape[0]
    acc = jnp.zeros((2 * n, length), F32)
    for j in range(STEPS):
        a = j % (STEPS // 2)
        rel = slice(j * width, (j + 1) * width)
        part = slice(a * width, (a + 1) * width)
        far = j < STEPS // 2
        mm_ref, y_ref, state_ref, g_ref = (
            (mmf_ref, yf_ref, other_ref, gf_ref) if far else (mmo_ref, yo_ref, mine_ref, go_ref)
        )
        y = y_ref[:, part]
        g_ref[:, part] = rows_ref[3:4, rel] * mm_ref[:, part] + sf_ref[:, rel] * dot(st_ref[...], y)
        acc = acc + dot_nt(split2(get_half(a, n, state_ref, width) * rows_ref[0:1, rel]), y)
    pair[...] = dot_nt(yf_ref[...], xf_ref[...])
    pair[...] += dot_nt(yo_ref[...], xo_ref[...])
    keep = same_doc(ids_ref) & (iota((length, length), 0) >= iota((length, length), 1))
    masked = jnp.where(keep, pair[...], 0.0)
    hi = masked.astype(BF16)
    lo = (masked - hi.astype(F32)).astype(BF16)
    through = (acc[:n] + acc[n:]) * ids_ref[1:2, :]
    gc[...] = dot_nt(b_ref[...], hi) + dot_nt(b_ref[...], lo) + through
    copy = pltpu.make_async_copy(gc, gc_hbm, sem)
    copy.start()
    gb_ref[...] = dot(c_ref[...], hi) + dot(c_ref[...], lo)
    copy.wait()


def finish_half(first, g_ref, x_ref, sf_ref, rows_ref, bm2_ref, state_ref, gv_hbm, gv, sems):
    half = g_ref.shape[1]
    width = 2 * half // STEPS
    piece = width // PIECES
    n = bm2_ref.shape[1] // 2
    copies = []
    acc = jnp.zeros(bm2_ref.shape, F32)
    for a in range(STEPS // 2):
        j = first + a
        rel = slice(j * width, (j + 1) * width)
        adjoint = split2(get_half(a, n, state_ref, width) * rows_ref[1:2, rel])
        for k in range(PIECES):
            part = slice(a * width + k * piece, a * width + (k + 1) * piece)
            near = slice(j * width + k * piece, j * width + (k + 1) * piece)
            gv[:, part] = g_ref[:, part] + sf_ref[:, near] * dot(
                bm2_ref[...], adjoint[:, k * piece : (k + 1) * piece]
            )
            place = pl.ds(pl.multiple_of(chunk_of(j) * width + k * piece, piece), piece)
            copies.append(pltpu.make_async_copy(gv.at[:, part], gv_hbm.at[:, place], sems.at[a * PIECES + k]))
            copies[-1].start()
        acc = acc + dot_nt(x_ref[:, a * width : (a + 1) * width], adjoint)
    return acc, copies


def finish_own_kernel(g_ref, x_ref, sf_ref, rows_ref, bm2_ref, mine_ref, gv_hbm, acc_ref, gv, sems):
    acc, copies = finish_half(STEPS // 2, g_ref, x_ref, sf_ref, rows_ref, bm2_ref, mine_ref, gv_hbm, gv, sems)
    acc_ref[...] = acc
    for copy in copies:
        copy.wait()


def finish_kernel(
    scale,
    _gv_in,
    g_ref,
    x_ref,
    sf_ref,
    rows_ref,
    bm2_ref,
    ids_ref,
    gb_part_ref,
    acc_ref,
    mine_ref,
    other_ref,
    gv_hbm,
    gb_hbm,
    loss_hbm,
    gv,
    gb,
    loss,
    sems,
):
    n = bm2_ref.shape[1] // 2
    last = mine_ref.shape[0] - 1
    loss[...] = jnp.broadcast_to(jnp.sum(mine_ref[last] + other_ref[last]) * scale, (1, 128))
    half = STEPS // 2 * PIECES
    out_loss = pltpu.make_async_copy(loss, loss_hbm, sems.at[half])
    out_loss.start()
    acc, copies = finish_half(0, g_ref, x_ref, sf_ref, rows_ref, bm2_ref, other_ref, gv_hbm, gv, sems)
    acc = acc + acc_ref[...]
    gb[...] = gb_part_ref[...] + (acc[:, :n] + acc[:, n:]).T * ids_ref[2:3, :]
    out_gb = pltpu.make_async_copy(gb, gb_hbm, sems.at[half + 1])
    out_gb.start()
    for copy in (*copies, out_loss, out_gb):
        copy.wait()


def call(kernel, ins, outs, flops=0, in_specs=None, out_specs=None, scratch=(), aliases=None):
    size = sum(a.size * a.dtype.itemsize for a in ins) + sum(o.size * o.dtype.itemsize for o in outs)
    return pl.pallas_call(
        kernel,
        out_shape=outs,
        in_specs=in_specs or [VMEM] * len(ins),
        out_specs=out_specs or [VMEM] * len(outs),
        scratch_shapes=scratch,
        input_output_aliases=aliases or {},
        compiler_params=pltpu.CompilerParams(vmem_limit_bytes=LIMIT),
        cost_estimate=pl.CostEstimate(flops=flops, bytes_accessed=size, transcendentals=0),
    )(*ins)


def out(*shape, dtype=F32):
    return jax.ShapeDtypeStruct(shape, dtype)


def swap(x, devices):
    return lax.ppermute(x, "seq", [(i, i ^ 1) for i in range(devices)])


def shift(x, by, devices):
    return lax.ppermute(
        x, "seq", [(i, i + by) for i in range(devices) if 0 <= i + by < devices]
    )


def turn(x, by, devices):
    return lax.ppermute(x, "seq", [(i, (i + by) % devices) for i in range(devices)])


def in_order(way, keep_ref, got_ref, body):
    near = odd_core() == (0 if way == 1 else 1)
    pl.when(near)(lambda: body(keep_ref, got_ref, True))
    pl.when(jnp.logical_not(near))(lambda: body(got_ref, keep_ref, False))


def columns(groups, count):
    return [(q, range(q, count, groups)) for q in range(groups)]


def compose_kernel(way, groups, keep_ref, send_ref, got_ref, packed_ref, both_ref, line_ref):
    count = both_ref.shape[0] - 1

    def body(first_ref, second_ref, _near):
        packed_ref[count] = first_ref[count] * second_ref[count]
        for q, places in columns(groups, count):
            decay = second_ref[count, q : q + 1, :]
            for t in places:
                both = second_ref[t] + decay * first_ref[t]
                packed_ref[t] = both
                both_ref[t] = both

    in_order(way, keep_ref, got_ref, body)
    line = send_ref[count + 1] + got_ref[count + 1]
    packed_ref[count + 1] = line
    both_ref[count] = line
    line_ref[...] = line


def arrive_kernel(way, groups, near_chips, keep_ref, got_ref, line_ref, one_ref, two_ref, *refs):
    more_refs, mine_ref, theirs_ref = refs[:-2], refs[-2], refs[-1]
    count = mine_ref.shape[0] - 1

    def body(first_ref, _second_ref, near):
        outer_ref, inner_ref = (mine_ref, theirs_ref) if near else (theirs_ref, mine_ref)
        for q, places in columns(groups, count):
            far_decay = one_ref[count, q : q + 1, :]
            decay = first_ref[count, q : q + 1, :]
            for t in places:
                state = one_ref[t] + far_decay * two_ref[t]
                outer_ref[t] = state
                inner_ref[t] = first_ref[t] + decay * state

    in_order(way, keep_ref, got_ref, body)
    line = jnp.zeros((8, 128), F32)
    if near_chips:
        line = line_ref[...] + one_ref[count + 1] + two_ref[count]
        line = jnp.where((odd_core() == 0).astype(F32) > 0.5, line, 0.0)
    for ref in more_refs:
        line = line + ref[...]
    mine_ref[count] = line
    theirs_ref[count] = line


def far_squares(line, devices):
    chips = devices // 2
    if chips != 8:
        return [lax.psum(line, "seq") * 0.25], False
    lines = []
    for far in range(3, chips, 2):
        pairs = [(i, (i - 2 * (far + i % 2)) % devices) for i in range(devices) if far + i % 2 < chips]
        lines.append(lax.ppermute(line, "seq", pairs))
    return lines, True


def carry(keep, send, groups, devices, way, beside):
    count = keep.shape[0] - 2
    got = swap(send, devices)
    packed, both, line = call(
        functools.partial(compose_kernel, way, groups),
        [keep, send, got],
        [out(*keep.shape), out(count + 1, 8, 128), out(8, 128)],
    )
    reach = max(1, devices // 8)
    move = shift if way == 1 else turn
    one = move(packed, 2 * way, devices)
    two = move(packed if reach > 2 else both, 4 * way, devices)
    lines, near_chips = [], False
    if way == -1:
        lines, near_chips = far_squares(line, devices)
    if reach > 2:

        def join(near, far):
            decay = near[count, :groups]
            state = near[:count].reshape(-1, groups, 8, 128) + decay[:, None, :] * far[:count].reshape(-1, groups, 8, 128)
            return jnp.concatenate([state.reshape(count, 8, 128), (near[count:] * far[count:])], axis=0)

        one = join(one, two)
        span = 2
        while span < reach:
            one = join(one, shift(one, 2 * span * way, devices))
            span *= 2
        two = jnp.zeros_like(both)
    mine, theirs = call(
        functools.partial(arrive_kernel, way, groups, near_chips),
        [keep, got, line, one, two, *lines],
        [out(count + 1, 8, 128), out(count + 1, 8, 128)],
    )
    theirs, beside = lax.optimization_barrier((theirs, beside))
    return mine, swap(theirs, devices), beside


def local(values, b_proj, c_proj, step_sizes, decay_rates, skip_gain, teacher, doc_lengths):
    length, total = values.shape
    heads = step_sizes.shape[1]
    state = b_proj.shape[1]
    devices = lax.axis_size("seq")
    b = b_proj.T
    c = c_proj.T
    groups = total // 2 // 128
    half = out(state // 8 * groups + 2, 8, 128)
    thirds = out(3 * heads, length, dtype=BF16)
    narrow = out(state, length, dtype=BF16)
    square = 2 * length * length * total
    dma = pltpu.SemaphoreType.DMA
    wide = out(length, total, dtype=BF16)
    part = out(length, total // 2)
    doubled = out(length, 2 * state, dtype=BF16)
    part16 = out(length, total // 2, dtype=BF16)
    x_far, send, enter3, sf3, f3, s3, rows, bm, cm, ids, v, teach, b, c = call(
        prepare_kernel,
        [
            pltpu.with_memory_space_constraint(a, pltpu.MemorySpace.HBM)
            for a in (
                doc_lengths,
                values,
                teacher,
                b,
                c,
                step_sizes.T,
                decay_rates.reshape(1, heads),
                skip_gain.reshape(1, heads),
            )
        ],
        [
            part16,
            half,
            thirds,
            thirds,
            thirds,
            thirds,
            out(PAD, total),
            narrow,
            narrow,
            out(PAD, length),
            wide,
            wide,
            narrow,
            narrow,
        ],
        in_specs=[HBM] * 8,
        scratch=[
            pltpu.SMEM(doc_lengths.shape, jnp.int32),
            pltpu.VMEM((heads, length), F32),
            pltpu.VMEM((1, heads), F32),
            pltpu.VMEM((1, heads), F32),
            dma((6,)),
            dma((STEPS,)),
            dma((STEPS,)),
        ],
    )
    x_own, keep = call(prepare_own_kernel, [f3, s3, bm, rows, v], [part16, half])
    inner = call(
        inner_kernel,
        [x_far, x_own, v, teach, b, c, enter3, sf3, rows, ids, bm, cm],
        [
            out(length, total),
            out(length, length, dtype=BF16),
            out(length, total),
            out(length, total),
            doubled,
            doubled,
        ],
        square,
    )
    mine, other, (base, score_t, enter, sf, bm2, cm2) = carry(keep, send, groups, devices, 1, inner)
    mm_own, y_own, keep = call(
        functools.partial(mismatch_kernel, STEPS // 2), [base, enter, rows, cm, cm2, mine], [part, part16, half]
    )
    mm_far, y_far, send = call(
        functools.partial(mismatch_kernel, 0), [base, enter, rows, cm, cm2, other, keep], [part, part16, half]
    )
    pairs = call(
        pair_kernel,
        [mm_far, mm_own, y_far, y_own, x_far, x_own, score_t, sf, rows, b, c, ids, other, mine],
        [part, part, out(state, length), out(state, length)],
        2 * square,
        out_specs=[VMEM, VMEM, VMEM, HBM],
        scratch=[pltpu.VMEM((length, length), F32), pltpu.VMEM((state, length), F32), dma],
    )
    mine, other, (g_far, g_own, gb_part, grad_c) = carry(keep, send, groups, devices, -1, pairs)
    grad_values, acc = call(
        finish_own_kernel,
        [g_own, x_own, sf, rows, bm2, mine],
        [out(length, total), out(length, 2 * state)],
        out_specs=[HBM, VMEM],
        scratch=[pltpu.VMEM((length, total // 2), F32), dma((STEPS // 2 * PIECES,))],
    )
    scale = 1.0 / (devices * length * total)
    grad_values, grad_b, loss = call(
        functools.partial(finish_kernel, scale),
        [grad_values, g_far, x_far, sf, rows, bm2, ids, gb_part, acc, mine, other],
        [out(length, total), out(state, length), out(1, 128)],
        in_specs=[HBM] + [VMEM] * 10,
        out_specs=[HBM, HBM, HBM],
        scratch=[
            pltpu.VMEM((length, total // 2), F32),
            pltpu.VMEM((state, length), F32),
            pltpu.VMEM((1, 128), F32),
            dma((STEPS // 2 * PIECES + 2,)),
        ],
        aliases={0: 0},
    )
    return loss[0, :1], grad_values, grad_b.T, grad_c.T


def solution(mesh):
    rows = P(("groups", "seq"), None)
    in_specs = (rows, rows, rows, rows, P(), P(), rows, P("groups"))
    out_specs = (P("groups"), rows, rows, rows)
    return jax.shard_map(local, mesh=mesh, in_specs=in_specs, out_specs=out_specs, check_vma=False)
```
